32 devices in a mesh: dp: 16 (over z, y, core), seq: 2 (over x).
Axes of the slice: x: 2, y: 2, z: 4, core: 2. Of those that a mesh axis runs over, the one named last changes fastest.
Arguments:
- targets: bfloat16 [256, 96, 768], P(('dp', 'seq')), may hold values from -6 to 6
- memory: bfloat16 [256, 1024, 768], P(('dp', 'seq')), may hold values from -6 to 6
- mem_lengths: int32 [256], P(('dp', 'seq')), may hold values from 512 to 1024, as said below
- buckets: int32 [96, 96], replicated, may hold values from 0 to 31
- cotangent: bfloat16 [256, 96, 768], P(('dp', 'seq')), may hold values from -6 to 6
- gain_self: bfloat16 [768], P(('dp', 'seq')), may hold values from 0.5 to 1.5
- gain_cross: bfloat16 [768], P(('dp', 'seq')), may hold values from 0.5 to 1.5
- gain_feed: bfloat16 [768], P(('dp', 'seq')), may hold values from 0.5 to 1.5
- self_query: bfloat16 [768, 768], P(('dp', 'seq')), may hold values from -0.0546875 to 0.0546875
- self_key: bfloat16 [768, 768], P(('dp', 'seq')), may hold values from -0.21875 to 0.21875
- self_value: bfloat16 [768, 768], P(('dp', 'seq')), may hold values from -0.21875 to 0.21875
- self_output: bfloat16 [768, 768], P(('dp', 'seq')), may hold values from -0.625 to 0.625
- cross_query: bfloat16 [768, 768], P(('dp', 'seq')), may hold values from -0.0546875 to 0.0546875
- cross_key: bfloat16 [768, 768], P(('dp', 'seq')), may hold values from -0.21875 to 0.21875
- cross_value: bfloat16 [768, 768], P(('dp', 'seq')), may hold values from -0.21875 to 0.21875
- cross_output: bfloat16 [768, 768], P(('dp', 'seq')), may hold values from -0.875 to 0.875
- gate_weight: bfloat16 [768, 2048], P(('dp', 'seq')), may hold values from -0.21875 to 0.21875
- up_weight: bfloat16 [768, 2048], P(('dp', 'seq')), may hold values from -0.21875 to 0.21875
- down_weight: bfloat16 [2048, 768], P(('dp', 'seq')), may hold values from -0.125 to 0.125
- bias_table: bfloat16 [32, 12], replicated, may hold values from -4 to 4
Outputs:
- outputs: bfloat16 [256, 96, 768], P(('dp', 'seq'))
- target_grad: bfloat16 [256, 96, 768], P(('dp', 'seq'))
- memory_grad: bfloat16 [256, 1024, 768], P(('dp', 'seq'))
- grad_gain_self: float32 [768], P(('dp', 'seq'))
- grad_gain_cross: float32 [768], P(('dp', 'seq'))
- grad_gain_feed: float32 [768], P(('dp', 'seq'))
- grad_self_query: float32 [768, 768], P(('dp', 'seq'))
- grad_self_key: float32 [768, 768], P(('dp', 'seq'))
- grad_self_value: float32 [768, 768], P(('dp', 'seq'))
- grad_self_output: float32 [768, 768], P(('dp', 'seq'))
- grad_cross_query: float32 [768, 768], P(('dp', 'seq'))
- grad_cross_key: float32 [768, 768], P(('dp', 'seq'))
- grad_cross_value: float32 [768, 768], P(('dp', 'seq'))
- grad_cross_output: float32 [768, 768], P(('dp', 'seq'))
- grad_gate_weight: float32 [768, 2048], P(('dp', 'seq'))
- grad_up_weight: float32 [768, 2048], P(('dp', 'seq'))
- grad_down_weight: float32 [2048, 768], P(('dp', 'seq'))
- grad_bias_table: float32 [32, 12], replicated
The draws below stay inside these ranges and needn't reach their ends.
Inputs may be any that keep to these rules, and one draw needn't show every extreme that they name: `mem_lengths`: each sequence has 512 or 1024 valid memory slots, the first ones; exactly half of all sequences have each.
All inputs are finite; a program needn't handle non-finite values.
Results may differ from the reference program's by a relative error of at most 0.025.
The reference program's roundings to bfloat16 on the way count: a program that leaves them out, or rounds other values in their place, can miss the bound.
Values may be sent and summed in bfloat16 or wider, within the bound.
No kernel may reach another device: no remote copies, remote signals or barrier semaphores. Data moves between devices by JAX's collectives and lax.ppermute only.
A program may use at most 320 MiB of HBM per device.

```python
import jax
import jax.numpy as jnp
from jax import lax

D = 768
HEADS = 12
FF = 2048
BUCKETS = 32
TGT = 96
MEM = 1024
BATCH = 256


def draw_mem_lengths(key, part):
    order = jax.random.permutation(key, BATCH)
    return jnp.where(order < BATCH // 2, MEM // 2, MEM).astype(jnp.int32)


def set_ends(array, stream_key, smallest, largest):
    extent = array.shape
    index_at = [jax.random.randint(jax.random.fold_in(stream_key, axis), (), 0, extent[axis]) for axis in range(len(extent))]
    array = array.at[tuple(index_at)].set(smallest)
    longest = extent.index(max(extent))
    index_at[longest] = (index_at[longest] + 1) % extent[longest]
    return array.at[tuple(index_at)].set(largest)


def with_spikes(drawn, rng, source, target, blocks, factor):
    def block_of(dim):
        return (jnp.arange(drawn.shape[dim]) // (drawn.shape[dim] // blocks)).reshape((-1,) + (1,) * (drawn.ndim - 1 - dim))

    near = jax.random.permutation(rng, blocks)[block_of(target)]
    second = (block_of(target) + blocks // 2) % blocks
    return jnp.where((block_of(source) == near) | (block_of(source) == second), factor * drawn, drawn)


def levels(rng, extent, cuts, smallest, high):
    def one(axis_at, parts):
        steps = jax.random.uniform(jax.random.fold_in(jax.random.fold_in(rng, 6), axis_at), (parts,), jnp.float32, smallest / len(cuts), high / len(cuts))
        return jnp.repeat(jnp.exp(steps), extent[axis_at] // parts).reshape((-1,) + (1,) * (len(extent) - axis_at - 1))

    loudness = one(*cuts[0])
    for cut in cuts[1:]:
        loudness = loudness * one(*cut)
    return loudness


def scatter_about(rng, extent, scale, bound, cuts=(), kind=jnp.bfloat16):
    drawn = scale * jax.random.normal(rng, extent, jnp.float32)
    if cuts:
        drawn = drawn * levels(rng, extent, cuts, -0.22, 0.18)
    return jnp.clip(drawn, -bound, bound).astype(kind)


def heavy_noise(key, shape, spread, reach, shards, heavy, kind=jnp.bfloat16):
    array = spread * jax.random.normal(key, shape, jnp.float32)
    if shards:
        array = array * levels(key, shape, shards, -0.22, 0.18)
    return jnp.clip(with_spikes(array, jax.random.fold_in(key, 3), *heavy), -reach, reach).astype(kind)


def setup_inputs(seed: int = 0) -> dict:
    key_of = jax.random.split(jax.random.key(seed), 21)
    return {
        "targets": heavy_noise(key_of[0], (BATCH, TGT, D), 1.0, 6.0, ((0, 32),), (0, 2, 32, 2.75)),
        "memory": scatter_about(key_of[1], (BATCH, MEM, D), 1.0, 6.0, ((0, 32),)),
        "mem_lengths": draw_mem_lengths(jax.random.fold_in(key_of[20], 71), 0),
        "buckets": set_ends(jax.random.randint(key_of[3], (TGT, TGT), 0, BUCKETS), jax.random.fold_in(key_of[3], 1), 0, BUCKETS - 1).astype(jnp.int32),
        "cotangent": scatter_about(key_of[4], (BATCH, TGT, D), 1.0, 6.0, ((0, 32),)),
        "gain_self": jnp.clip(1.0 + 0.1 * jax.random.normal(key_of[5], (D,), jnp.float32), 0.5, 1.5).astype(jnp.bfloat16),
        "gain_cross": jnp.clip(1.0 + 0.1 * jax.random.normal(key_of[6], (D,), jnp.float32), 0.5, 1.5).astype(jnp.bfloat16),
        "gain_feed": jnp.clip(1.0 + 0.1 * jax.random.normal(key_of[7], (D,), jnp.float32), 0.5, 1.5).astype(jnp.bfloat16),
        "self_query": scatter_about(key_of[8], (D, D), (16 * D) ** -0.5, 0.0546875, ((0, 32),)),
        "self_key": scatter_about(key_of[9], (D, D), D ** -0.5, 0.21875, ((0, 32),)),
        "self_value": scatter_about(key_of[10], (D, D), D ** -0.5, 0.21875, ((0, 32),)),
        "self_output": scatter_about(key_of[11], (D, D), (D // 8) ** -0.5, 0.625, ((0, 32),)),
        "cross_query": scatter_about(key_of[12], (D, D), (16 * D) ** -0.5, 0.0546875, ((0, 32),)),
        "cross_key": scatter_about(key_of[13], (D, D), D ** -0.5, 0.21875, ((0, 32),)),
        "cross_value": scatter_about(key_of[14], (D, D), D ** -0.5, 0.21875, ((0, 32),)),
        "cross_output": scatter_about(key_of[15], (D, D), (D // 16) ** -0.5, 0.875, ((0, 32),)),
        "gate_weight": scatter_about(key_of[16], (D, FF), D ** -0.5, 0.21875, ((0, 32),)),
        "up_weight": scatter_about(key_of[17], (D, FF), D ** -0.5, 0.21875, ((0, 32),)),
        "down_weight": scatter_about(key_of[18], (FF, D), FF ** -0.5, 0.125, ((0, 32),)),
        "bias_table": scatter_about(key_of[19], (BUCKETS, HEADS), 1.0, 4.0),
    }


@jax.custom_vjp
def low(v):
    return lax.optimization_barrier(v.astype(jnp.bfloat16)).astype(jnp.float32)

@jax.custom_vjp
def low_back(v):
    return v

def low_keep(v):
    return (low(v), None)

def low_pass(kept, grad):
    return (grad,)

def back_keep(v):
    return (v, None)

def back_low(kept, grad):
    return (low(grad),)
low.defvjp(low_keep, low_pass)
low_back.defvjp(back_keep, back_low)
epsilon = 1e-06
masked_out = -1e+30
highest = lax.Precision.HIGHEST

def rounded(values):
    return low(low_back(values))

def rms_norm(values, gain_row):
    return values * lax.rsqrt(lax.optimization_barrier(jnp.mean(values * values, axis=-1, keepdims=True)) + epsilon) * gain_row

def project(values, weight):
    return jnp.einsum('btd,de->bte', values, weight, precision=highest)

def attend(queries, key_rows, value_rows, extra_bias, keep_mask):
    scores = jnp.einsum('bihe,bjhe->bhij', queries, key_rows, precision=highest) + extra_bias
    scores = jnp.where(keep_mask, low_back(scores), masked_out)
    attn_weights = low(jax.nn.softmax(scores, axis=-1))
    return jnp.einsum('bhij,bjhe->bihe', attn_weights, value_rows, precision=highest)

def layer_forward(buckets, lengths, targets, memory, weights):
    gain_self, gain_cross, gain_feed, self_query, self_key, self_value, self_output, cross_query, cross_key, cross_value, cross_output, gate_weight, up_weight, down_weight, bias_table = weights
    group_size, target_len, model_width = targets.shape
    memory_len = memory.shape[1]
    head_count = bias_table.shape[1]
    head_size = model_width // head_count

    def to_heads(values):
        return values.reshape(values.shape[0], values.shape[1], head_count, head_size)

    def from_heads(values):
        return values.reshape(values.shape[0], values.shape[1], model_width)
    normed_one = low(rms_norm(targets, gain_self))
    queries = rounded(project(normed_one, self_query))
    key_rows = rounded(project(normed_one, self_key))
    value_rows = rounded(project(normed_one, self_value))
    position_bias = jnp.transpose(bias_table[buckets], (2, 0, 1))
    row_index = lax.broadcasted_iota(jnp.int32, (target_len, target_len), 0)
    col_index = lax.broadcasted_iota(jnp.int32, (target_len, target_len), 1)
    causal = col_index <= row_index
    self_context = rounded(from_heads(attend(to_heads(queries), to_heads(key_rows), to_heads(value_rows), position_bias, causal)))
    after_self = targets + low_back(project(self_context, self_output))
    normed_two = low(rms_norm(after_self, gain_cross))
    side_queries = rounded(project(normed_two, cross_query))
    mem_keys = rounded(project(memory, cross_key))
    mem_values = rounded(project(memory, cross_value))
    positions = lax.broadcasted_iota(jnp.int32, (group_size, memory_len), 1)
    valid_keys = (positions < lengths[:, None])[:, None, None, :]
    cross_context = rounded(from_heads(attend(to_heads(side_queries), to_heads(mem_keys), to_heads(mem_values), 0.0, valid_keys)))
    after_cross = after_self + low_back(project(cross_context, cross_output))
    normed_three = low(rms_norm(after_cross, gain_feed))
    gate_out = low_back(project(normed_three, gate_weight))
    up_out = low_back(project(normed_three, up_weight))
    hidden = low(jax.nn.gelu(gate_out, approximate=True) * up_out)
    return after_cross + low_back(jnp.einsum('btf,fd->btd', hidden, down_weight, precision=highest))

def reference(targets, memory, mem_lengths, buckets, cotangent, gain_self, gain_cross, gain_feed, self_query, self_key, self_value, self_output, cross_query, cross_key, cross_value, cross_output, gate_weight, up_weight, down_weight, bias_table):
    weights = tuple((weight_arg.astype(jnp.float32) for weight_arg in (gain_self, gain_cross, gain_feed, self_query, self_key, self_value, self_output, cross_query, cross_key, cross_value, cross_output, gate_weight, up_weight, down_weight, bias_table)))
    batch_size = targets.shape[0]
    group_size = 4
    group_total = batch_size // group_size

    def regroup(values):
        return values.reshape((group_total, group_size) + values.shape[1:])

    def one_group(totals, pieces):
        target_part, memory_part, length_part, cotangent_part = pieces

        def forward(target_vals, memory_vals, weight_vals):
            return layer_forward(buckets, length_part, target_vals, memory_vals, weight_vals)
        output, pullback = jax.vjp(forward, target_part.astype(jnp.float32), memory_part.astype(jnp.float32), weights)
        grad_target, grad_memory, grad_weights = pullback(cotangent_part.astype(jnp.float32))
        totals = tuple((left_term + right_term for left_term, right_term in zip(totals, grad_weights)))
        return (totals, (output.astype(jnp.bfloat16), grad_target.astype(jnp.bfloat16), grad_memory.astype(jnp.bfloat16)))
    zero_grads = tuple((jnp.zeros_like(weight_arg) for weight_arg in weights))
    totals, stacked = lax.scan(one_group, zero_grads, (regroup(targets), regroup(memory), regroup(mem_lengths), regroup(cotangent)))
    out_rows, target_rows, memory_rows = stacked
    total_gain_self, total_gain_cross, total_gain_feed, total_self_query, total_self_key, total_self_value, total_self_output, total_cross_query, total_cross_key, total_cross_value, total_cross_output, total_gate, total_up, total_down, total_table = totals
    return (out_rows.reshape(targets.shape), target_rows.reshape(targets.shape), memory_rows.reshape(memory.shape), total_gain_self, total_gain_cross, total_gain_feed, total_self_query, total_self_key, total_self_value, total_self_output, total_cross_query, total_cross_key, total_cross_value, total_cross_output, total_gate, total_up, total_down, total_table)
```

```python
import math

import jax
import jax.numpy as jnp
from jax import lax
from jax.experimental import pallas as pl
from jax.experimental.pallas import tpu as pltpu
from jax.sharding import PartitionSpec as P

epsilon = 1e-06
masked_out = -1e30
bf16 = jnp.bfloat16
f32 = jnp.float32
axes = ("dp", "seq")
lane_tile = 256
group_rows = 24
pair_width = 128
NN = (((1,), (0,)), ((), ()))
NT = (((1,), (1,)), ((), ()))
TN = (((0,), (0,)), ((), ()))
gelu_scale = math.sqrt(2.0 / math.pi)
gelu_cubic = 0.044715


def dot(left_side, right_side, dims=NN):
    return lax.dot_general(left_side, right_side, dims, preferred_element_type=f32)


def params():
    return pltpu.CompilerParams(vmem_limit_bytes=60 * 1024 * 1024)


def column_tile(packed_ref, index):
    tile = packed_ref[:, index * group_rows : (index + 1) * group_rows, :]
    return tile.reshape(tile.shape[0] * group_rows, lane_tile)


def put_column_tile(packed_ref, index, values):
    groups = packed_ref.shape[0]
    packed_ref[:, index * group_rows : (index + 1) * group_rows, :] = values.reshape(
        groups, group_rows, lane_tile
    ).astype(bf16)


def lane_halves(rows):
    lanes = lax.broadcasted_iota(jnp.int32, (rows, pair_width), 1)
    return lanes < pair_width // 2


def project(rows, packed_ref, base, tiles):
    return [dot(rows, column_tile(packed_ref, base + t)) for t in range(tiles)]


def through(rows, packed_ref, base, tiles):
    total = None
    for t in range(tiles):
        part = dot(
            rows[:, t * lane_tile : (t + 1) * lane_tile], column_tile(packed_ref, base + t), NT
        )
        total = part if total is None else total + part
    return total


def put_weight_grad(packed_ref, base, rows, grads):
    for t in range(grads.shape[1] // lane_tile):
        part = dot(rows, grads[:, t * lane_tile : (t + 1) * lane_tile], TN)
        put_column_tile(packed_ref, base + t, part)


def norm_scale(values):
    return lax.rsqrt(jnp.mean(values * values, axis=-1, keepdims=True) + epsilon)


def norm_pullback(values, gain_row, grad_in):
    inverse = norm_scale(values)
    weighted = grad_in * gain_row
    inner = jnp.mean(weighted * values, axis=-1, keepdims=True)
    grad_values = inverse * weighted - values * (inverse * inverse * inverse * inner)
    grad_gain = jnp.sum(grad_in * values * inverse, axis=0, keepdims=True)
    return grad_values, grad_gain


def memory_kernel(lengths, memory_ref, packed_ref, keys_ref, values_ref):
    seq = pl.program_id(0)
    memory_len = memory_ref.shape[1]

    def fill(count):
        rows = memory_ref[0, :count, :]
        for base, out_ref in ((0, keys_ref), (3, values_ref)):
            for t in range(3):
                out_ref[0, :count, t * lane_tile : (t + 1) * lane_tile] = dot(
                    rows, column_tile(packed_ref, base + t)
                ).astype(bf16)

    @pl.when(lengths[seq] > memory_len // 2)
    def _():
        fill(memory_len)

    @pl.when(lengths[seq] <= memory_len // 2)
    def _():
        fill(memory_len // 2)


def project_memory(mem_lengths, memory, packed):
    batch, memory_len, width = memory.shape
    block = pl.BlockSpec((1, memory_len, width), lambda b, n: (b, 0, 0))
    return pl.pallas_call(
        memory_kernel,
        out_shape=[jax.ShapeDtypeStruct(memory.shape, bf16)] * 2,
        grid_spec=pltpu.PrefetchScalarGridSpec(
            num_scalar_prefetch=1,
            grid=(batch,),
            in_specs=[block, pl.BlockSpec(packed.shape, lambda b, n: (0, 0, 0))],
            out_specs=[block, block],
        ),
        compiler_params=params(),
        name="memory_project",
    )(mem_lengths, memory, packed)


def stacked_pair(rows, half, pad):
    zero = jnp.zeros_like(rows)
    gap = jnp.zeros((pad, pair_width), rows.dtype)
    return jnp.concatenate(
        [jnp.where(half, rows, zero), gap, jnp.where(half, zero, rows), gap], axis=0
    )


def pair_softmax(scores):
    parts = []
    for h in range(2):
        one = scores[:, h * pair_width : (h + 1) * pair_width]
        terms = jnp.exp(one - jnp.max(one, axis=-1, keepdims=True))
        parts.append(terms * (1.0 / jnp.sum(terms, axis=-1, keepdims=True)))
    return parts


def self_forward_kernel(
    target_len,
    targets_ref,
    packed_ref,
    bias_ref,
    gain_self_ref,
    gain_cross_ref,
    normed_one_ref,
    queries_ref,
    keys_ref,
    values_ref,
    context_ref,
    after_ref,
    normed_two_ref,
    side_ref,
):
    inputs = targets_ref[...].astype(f32)
    normed_one = (inputs * norm_scale(inputs) * gain_self_ref[...]).astype(bf16)
    normed_one_ref[...] = normed_one
    for base, out_ref in ((0, queries_ref), (3, keys_ref), (6, values_ref)):
        for t in range(3):
            out_ref[:, t * lane_tile : (t + 1) * lane_tile] = dot(
                normed_one, column_tile(packed_ref, base + t)
            ).astype(bf16)
    half = lane_halves(target_len)
    pad = pair_width - target_len
    pairs = bias_ref.shape[0]

    def attend(seq, carry):
        rows = pl.ds(pl.multiple_of(seq * target_len, 32), target_len)
        for p in range(pairs):
            cols = slice(p * pair_width, (p + 1) * pair_width)
            key_stack = stacked_pair(keys_ref[rows, cols], half, pad)
            value_stack = stacked_pair(values_ref[rows, cols], half, pad)
            scores = dot(queries_ref[rows, cols], key_stack, NT) + bias_ref[p]
            probs = jnp.concatenate(pair_softmax(scores), axis=1)
            context_ref[rows, cols] = dot(probs.astype(bf16), value_stack).astype(bf16)
        return carry

    lax.fori_loop(0, targets_ref.shape[0] // target_len, attend, 0)
    after = inputs + jnp.concatenate(project(context_ref[...], packed_ref, 9, 3), axis=1)
    after_ref[...] = after
    normed_two = (after * norm_scale(after) * gain_cross_ref[...]).astype(bf16)
    normed_two_ref[...] = normed_two
    for t in range(3):
        side_ref[:, t * lane_tile : (t + 1) * lane_tile] = dot(
            normed_two, column_tile(packed_ref, 12 + t)
        ).astype(bf16)


def self_forward(target_len, targets, packed, bias, gain_self, gain_cross):
    low = jax.ShapeDtypeStruct(targets.shape, bf16)
    wide = jax.ShapeDtypeStruct(targets.shape, f32)

    def body(*refs):
        self_forward_kernel(target_len, *refs)

    return pl.pallas_call(
        body,
        out_shape=[low, low, low, low, low, wide, low, low],
        compiler_params=params(),
        name="self_forward",
    )(targets, packed, bias, gain_self, gain_cross)


def masked_stack(rows, half):
    zero = jnp.zeros_like(rows)
    return jnp.concatenate([jnp.where(half, rows, zero), jnp.where(half, zero, rows)], axis=0)


def cross_forward_kernel(lengths, side_ref, keys_ref, values_ref, context_ref, weights_ref):
    seq = pl.program_id(0)
    target_len, width = side_ref.shape
    memory_len = keys_ref.shape[1]
    half = lane_halves(target_len)

    def attend(count):
        for p in range(width // pair_width):
            cols = slice(p * pair_width, (p + 1) * pair_width)
            stack = masked_stack(side_ref[:, cols], half)
            scores = dot(stack, keys_ref[0, :count, cols], NT)
            terms = jnp.exp(scores - jnp.max(scores, axis=-1, keepdims=True))
            scale = 1.0 / jnp.sum(terms, axis=-1, keepdims=True)
            weights = (terms * scale).astype(bf16)
            weights_ref[0, 2 * target_len * p : 2 * target_len * (p + 1), :count] = weights
            both = dot(weights, values_ref[0, :count, cols])
            context_ref[:, cols] = jnp.where(half, both[:target_len], both[target_len:]).astype(
                bf16
            )

    @pl.when(lengths[seq] > memory_len // 2)
    def _():
        attend(memory_len)

    @pl.when(lengths[seq] <= memory_len // 2)
    def _():
        attend(memory_len // 2)


def cross_forward(mem_lengths, side, mem_keys, mem_values, head_count):
    batch, memory_len, width = mem_keys.shape
    target_len = side.shape[0] // batch
    rows = pl.BlockSpec((target_len, width), lambda b, n: (b, 0))
    memory = pl.BlockSpec((1, memory_len, width), lambda b, n: (b, 0, 0))
    weights = pl.BlockSpec((1, head_count * target_len, memory_len), lambda b, n: (b, 0, 0))
    return pl.pallas_call(
        cross_forward_kernel,
        out_shape=[
            jax.ShapeDtypeStruct(side.shape, bf16),
            jax.ShapeDtypeStruct((batch, head_count * target_len, memory_len), bf16),
        ],
        grid_spec=pltpu.PrefetchScalarGridSpec(
            num_scalar_prefetch=1,
            grid=(batch,),
            in_specs=[rows, memory, memory],
            out_specs=[rows, weights],
        ),
        compiler_params=params(),
        name="cross_forward",
    )(mem_lengths, side, mem_keys, mem_values)


def feed_kernel(
    after_ref,
    context_ref,
    cot_ref,
    gain_ref,
    side_output_ref,
    gate_ref,
    up_ref,
    down_ref,
    outputs_ref,
    grad_after_ref,
    grad_context_ref,
    grad_gain_ref,
    packed_ref,
    after_cross_ref,
    normed_ref,
    out_total_ref,
    grad_normed_ref,
):
    step = pl.program_id(0)
    steps = pl.num_programs(0)

    @pl.when(step == 0)
    def _():
        after_cross = after_ref[...] + jnp.concatenate(
            project(context_ref[...], side_output_ref, 0, 3), axis=1
        )
        after_cross_ref[...] = after_cross
        normed_ref[...] = (after_cross * norm_scale(after_cross) * gain_ref[...]).astype(bf16)
        out_total_ref[...] = after_cross
        grad_normed_ref[...] = jnp.zeros_like(grad_normed_ref)

    normed = normed_ref[...]
    cot = cot_ref[...]
    gate_weight = column_tile(gate_ref, 0)
    up_weight = column_tile(up_ref, 0)
    share = down_ref.shape[1] // 3
    owners = down_ref.shape[0]
    down_weight = jnp.concatenate(
        [
            down_ref[:, c * share : (c + 1) * share, :].reshape(owners * share, lane_tile)
            for c in range(3)
        ],
        axis=1,
    )
    gate = dot(normed, gate_weight)
    up = dot(normed, up_weight)
    grad_hidden = dot(cot, down_weight, NT)
    square = gate * gate
    tanh = jnp.tanh(gelu_scale * (gate + gelu_cubic * (square * gate)))
    half_sum = 0.5 * (1.0 + tanh)
    active = gate * half_sum
    slope = half_sum + 0.5 * gate * (1.0 - tanh * tanh) * (
        gelu_scale * (1.0 + 3.0 * gelu_cubic * square)
    )
    hidden = (active * up).astype(bf16)
    grad_gate = (grad_hidden * up * slope).astype(bf16)
    grad_up = (grad_hidden * active).astype(bf16)
    out_total_ref[...] += dot(hidden, down_weight)
    grad_normed_ref[...] += dot(grad_gate, gate_weight, NT) + dot(grad_up, up_weight, NT)
    groups = packed_ref.shape[0]

    def put(base, value):
        packed_ref[:, pl.ds(base + step * group_rows, group_rows), :] = value.reshape(
            groups, group_rows, lane_tile
        ).astype(bf16)

    put(0, dot(normed, grad_gate, TN))
    put(steps * group_rows, dot(normed, grad_up, TN))
    down_base = 2 * steps * group_rows
    for c in range(3):
        part = dot(hidden, cot[:, c * lane_tile : (c + 1) * lane_tile], TN)
        packed_ref[
            pl.ds(step * owners, owners), down_base + c * share : down_base + (c + 1) * share, :
        ] = part.reshape(owners, share, lane_tile).astype(bf16)

    @pl.when(step == steps - 1)
    def _():
        outputs_ref[...] = out_total_ref[...].astype(bf16)
        grad_in, grad_gain = norm_pullback(
            after_cross_ref[...], gain_ref[...], grad_normed_ref[...]
        )
        grad_gain_ref[...] = grad_gain
        grad_after = cot_ref[...].astype(f32) + grad_in
        grad_after_ref[...] = grad_after
        low = grad_after.astype(bf16)
        put_weight_grad(packed_ref, 3 * down_base // (2 * group_rows), context_ref[...], low)
        grad_context_ref[...] = through(low, side_output_ref, 0, 3).astype(bf16)


def feed_both(after_self, context, cotangent, gain, packed_self, packed_feed):
    rows, width = context.shape
    groups, feed_rows, _ = packed_feed.shape
    steps = feed_rows // (3 * group_rows)
    owners = groups // steps
    whole = lambda f: (0, 0)
    full = pl.BlockSpec((rows, width), whole)
    tile = (groups, group_rows, lane_tile)
    out_rows = feed_rows + 3 * group_rows
    return pl.pallas_call(
        feed_kernel,
        out_shape=[
            jax.ShapeDtypeStruct((rows, width), bf16),
            jax.ShapeDtypeStruct((rows, width), f32),
            jax.ShapeDtypeStruct((rows, width), bf16),
            jax.ShapeDtypeStruct((1, width), f32),
            jax.ShapeDtypeStruct((groups, out_rows, lane_tile), bf16),
        ],
        grid=(steps,),
        in_specs=[
            full,
            full,
            full,
            pl.BlockSpec((1, width), whole),
            pl.BlockSpec((groups, 3 * group_rows, lane_tile), lambda f: (0, 5, 0)),
            pl.BlockSpec(tile, lambda f: (0, f, 0)),
            pl.BlockSpec(tile, lambda f: (0, steps + f, 0)),
            pl.BlockSpec((owners, steps * group_rows, lane_tile), lambda f: (f, 2, 0)),
        ],
        out_specs=[
            full,
            full,
            full,
            pl.BlockSpec((1, width), whole),
            pl.BlockSpec((groups, out_rows, lane_tile), lambda f: (0, 0, 0)),
        ],
        scratch_shapes=[
            pltpu.VMEM((rows, width), f32),
            pltpu.VMEM((rows, width), bf16),
            pltpu.VMEM((rows, width), f32),
            pltpu.VMEM((rows, width), f32),
        ],
        compiler_params=params(),
        name="feed_both",
    )(after_self, context, cotangent, gain, packed_self, packed_feed, packed_feed, packed_feed)


def cross_backward_kernel(
    lengths,
    grad_ref,
    context_ref,
    side_ref,
    keys_ref,
    values_ref,
    weights_ref,
    grad_side_ref,
    grad_keys_ref,
    grad_values_ref,
):
    seq = pl.program_id(0)
    target_len, width = side_ref.shape
    memory_len = keys_ref.shape[1]
    half = lane_halves(target_len)

    def attend(count):
        for p in range(width // pair_width):
            cols = slice(p * pair_width, (p + 1) * pair_width)
            grad_rows = grad_ref[:, cols]
            grad_stack = masked_stack(grad_rows, half)
            query_stack = masked_stack(side_ref[:, cols], half)
            product = grad_rows.astype(f32) * context_ref[:, cols].astype(f32)
            inner = jnp.sum(masked_stack(product, half), axis=-1, keepdims=True)
            weights = weights_ref[0, 2 * target_len * p : 2 * target_len * (p + 1), :count]
            grad_probs = dot(grad_stack, values_ref[0, :count, cols], NT)
            grad_scores = (weights.astype(f32) * (grad_probs - inner)).astype(bf16)
            both = dot(grad_scores, keys_ref[0, :count, cols])
            grad_side_ref[:, cols] = jnp.where(half, both[:target_len], both[target_len:]).astype(
                bf16
            )
            grad_keys_ref[0, cols, :count] = dot(query_stack, grad_scores, TN).astype(bf16)
            grad_values_ref[0, cols, :count] = dot(grad_stack, weights, TN).astype(bf16)

    @pl.when(lengths[seq] > memory_len // 2)
    def _():
        attend(memory_len)

    @pl.when(lengths[seq] <= memory_len // 2)
    def _():
        attend(memory_len // 2)


def cross_backward(mem_lengths, grad_context, context, side, mem_keys, mem_values, weights):
    batch, memory_len, width = mem_keys.shape
    target_len = side.shape[0] // batch
    rows = pl.BlockSpec((target_len, width), lambda b, n: (b, 0))
    memory = pl.BlockSpec((1, memory_len, width), lambda b, n: (b, 0, 0))
    turned = pl.BlockSpec((1, width, memory_len), lambda b, n: (b, 0, 0))
    return pl.pallas_call(
        cross_backward_kernel,
        out_shape=[jax.ShapeDtypeStruct(side.shape, bf16)]
        + [jax.ShapeDtypeStruct((batch, width, memory_len), bf16)] * 2,
        grid_spec=pltpu.PrefetchScalarGridSpec(
            num_scalar_prefetch=1,
            grid=(batch,),
            in_specs=[
                rows,
                rows,
                rows,
                memory,
                memory,
                pl.BlockSpec((1,) + weights.shape[1:], lambda b, n: (b, 0, 0)),
            ],
            out_specs=[rows, turned, turned],
        ),
        compiler_params=params(),
        name="cross_backward",
    )(mem_lengths, grad_context, context, side, mem_keys, mem_values, weights)


def memory_weight_kernel(
    lengths, memory_ref, grad_keys_ref, grad_values_ref, packed_ref, key_total_ref, value_total_ref
):
    seq = pl.program_id(0)
    memory_len = memory_ref.shape[1]

    @pl.when(seq == 0)
    def _():
        key_total_ref[...] = jnp.zeros_like(key_total_ref)
        value_total_ref[...] = jnp.zeros_like(value_total_ref)

    def add(count):
        rows = memory_ref[0, :count, :]
        key_total_ref[...] += dot(grad_keys_ref[0, :, :count], rows)
        value_total_ref[...] += dot(grad_values_ref[0, :, :count], rows)

    @pl.when(lengths[seq] > memory_len // 2)
    def _():
        add(memory_len)

    @pl.when(lengths[seq] <= memory_len // 2)
    def _():
        add(memory_len // 2)

    @pl.when(seq == pl.num_programs(0) - 1)
    def _():
        for base, total_ref in ((0, key_total_ref), (3, value_total_ref)):
            for t in range(3):
                put_column_tile(
                    packed_ref,
                    base + t,
                    jnp.transpose(total_ref[t * lane_tile : (t + 1) * lane_tile, :]),
                )


def memory_weight_grads(mem_lengths, memory, grad_keys, grad_values, packed_shape):
    batch, memory_len, width = memory.shape
    block = pl.BlockSpec((1, memory_len, width), lambda b, n: (b, 0, 0))
    turned = pl.BlockSpec((1, width, memory_len), lambda b, n: (b, 0, 0))
    return pl.pallas_call(
        memory_weight_kernel,
        out_shape=jax.ShapeDtypeStruct(packed_shape, bf16),
        grid_spec=pltpu.PrefetchScalarGridSpec(
            num_scalar_prefetch=1,
            grid=(batch,),
            in_specs=[block, turned, turned],
            out_specs=pl.BlockSpec(packed_shape, lambda b, n: (0, 0, 0)),
            scratch_shapes=[pltpu.VMEM((width, width), f32)] * 2,
        ),
        compiler_params=params(),
        name="memory_weight_grads",
    )(mem_lengths, memory, grad_keys, grad_values)


def memory_grad_kernel(
    lengths, grad_keys_ref, grad_values_ref, packed_ref, out_ref, key_turned_ref, value_turned_ref
):
    seq = pl.program_id(0)
    memory_len = out_ref.shape[1]

    @pl.when(seq == 0)
    def _():
        for base, turned_ref in ((0, key_turned_ref), (3, value_turned_ref)):
            for t in range(3):
                turned_ref[t * lane_tile : (t + 1) * lane_tile, :] = jnp.transpose(
                    column_tile(packed_ref, base + t)
                )

    def fill(count):
        out_ref[0, :count, :] = (
            dot(grad_keys_ref[0, :, :count], key_turned_ref[...], TN)
            + dot(grad_values_ref[0, :, :count], value_turned_ref[...], TN)
        ).astype(bf16)

    @pl.when(lengths[seq] > memory_len // 2)
    def _():
        fill(memory_len)

    @pl.when(lengths[seq] <= memory_len // 2)
    def _():
        fill(memory_len // 2)
        out_ref[0, memory_len // 2 :, :] = jnp.zeros_like(out_ref[0, memory_len // 2 :, :])


def memory_gradient(mem_lengths, grad_keys, grad_values, packed):
    batch, width, memory_len = grad_keys.shape
    turned = pl.BlockSpec((1, width, memory_len), lambda b, n: (b, 0, 0))
    return pl.pallas_call(
        memory_grad_kernel,
        out_shape=jax.ShapeDtypeStruct((batch, memory_len, width), bf16),
        grid_spec=pltpu.PrefetchScalarGridSpec(
            num_scalar_prefetch=1,
            grid=(batch,),
            in_specs=[turned, turned, pl.BlockSpec(packed.shape, lambda b, n: (0, 0, 0))],
            out_specs=pl.BlockSpec((1, memory_len, width), lambda b, n: (b, 0, 0)),
            scratch_shapes=[pltpu.VMEM((width, width), bf16)] * 2,
        ),
        compiler_params=params(),
        name="memory_grad",
    )(mem_lengths, grad_keys, grad_values, packed)


def self_backward_kernel(
    target_len,
    grad_side_ref,
    after_ref,
    grad_after_ref,
    normed_two_ref,
    normed_one_ref,
    queries_ref,
    keys_ref,
    values_ref,
    context_ref,
    targets_ref,
    packed_ref,
    bias_ref,
    buckets_ref,
    gain_self_ref,
    gain_cross_ref,
    target_grad_ref,
    grads_ref,
    grad_gains_ref,
    table_ref,
    grad_queries_ref,
    grad_keys_ref,
    grad_values_ref,
    grad_context_ref,
    total_ref,
    score_total_ref,
):
    grad_side = grad_side_ref[...]
    grad_in, grad_gain_cross = norm_pullback(
        after_ref[...], gain_cross_ref[...], through(grad_side, packed_ref, 12, 3)
    )
    put_weight_grad(grads_ref, 12, normed_two_ref[...], grad_side)
    grad_after = grad_after_ref[...] + grad_in
    total_ref[...] = grad_after
    low = grad_after.astype(bf16)
    put_weight_grad(grads_ref, 9, context_ref[...], low)
    grad_context_ref[...] = through(low, packed_ref, 9, 3).astype(bf16)
    half = lane_halves(target_len)
    pad = pair_width - target_len
    pairs = bias_ref.shape[0]
    score_total_ref[...] = jnp.zeros_like(score_total_ref)

    def pick(values):
        return jnp.where(
            half, values[:target_len], values[pair_width : pair_width + target_len]
        ).astype(bf16)

    def attend(seq, carry):
        rows = pl.ds(pl.multiple_of(seq * target_len, 32), target_len)
        for p in range(pairs):
            cols = slice(p * pair_width, (p + 1) * pair_width)
            queries = queries_ref[rows, cols]
            grad_rows = grad_context_ref[rows, cols]
            key_stack = stacked_pair(keys_ref[rows, cols], half, pad)
            value_stack = stacked_pair(values_ref[rows, cols], half, pad)
            scores = dot(queries, key_stack, NT) + bias_ref[p]
            probs = pair_softmax(scores)
            grad_probs = dot(grad_rows, value_stack, NT)
            parts = []
            for h in range(2):
                one = grad_probs[:, h * pair_width : (h + 1) * pair_width]
                inner = jnp.sum(one * probs[h], axis=-1, keepdims=True)
                parts.append(probs[h] * (one - inner))
            grad_scores = jnp.concatenate(parts, axis=1).astype(bf16)
            weights = jnp.concatenate(probs, axis=1).astype(bf16)
            score_total_ref[p] += grad_scores.astype(f32)
            grad_queries_ref[rows, cols] = dot(grad_scores, key_stack).astype(bf16)
            grad_keys_ref[rows, cols] = pick(dot(grad_scores, queries, TN))
            grad_values_ref[rows, cols] = pick(dot(weights, grad_rows, TN))
        return carry

    lax.fori_loop(0, targets_ref.shape[0] // target_len, attend, 0)
    buckets = buckets_ref[...]
    both = jnp.concatenate([buckets, buckets], axis=1)

    def count(bucket, carry):
        chosen = both == bucket
        for p in range(pairs):
            table_ref[bucket, p : p + 1, :] = jnp.sum(
                jnp.where(chosen, score_total_ref[p], 0.0), axis=0, keepdims=True
            )
        return carry

    lax.fori_loop(0, table_ref.shape[0], count, 0)
    normed_one = normed_one_ref[...]
    total = None
    for base, grad_ref in ((0, grad_queries_ref), (3, grad_keys_ref), (6, grad_values_ref)):
        grads = grad_ref[...]
        put_weight_grad(grads_ref, base, normed_one, grads)
        part = through(grads, packed_ref, base, 3)
        total = part if total is None else total + part
    grad_in, grad_gain_self = norm_pullback(
        targets_ref[...].astype(f32), gain_self_ref[...], total
    )
    target_grad_ref[...] = (total_ref[...] + grad_in).astype(bf16)
    grad_gains_ref[0:1, :] = grad_gain_self
    grad_gains_ref[1:2, :] = grad_gain_cross


def self_backward(target_len, bucket_count, operands):
    targets = operands[9]
    packed = operands[10]
    bias = operands[11]
    rows, width = targets.shape

    def body(*refs):
        self_backward_kernel(target_len, *refs)

    return pl.pallas_call(
        body,
        out_shape=[
            jax.ShapeDtypeStruct((rows, width), bf16),
            jax.ShapeDtypeStruct((packed.shape[0], 15 * group_rows, lane_tile), bf16),
            jax.ShapeDtypeStruct((2, width), f32),
            jax.ShapeDtypeStruct((bucket_count, bias.shape[0], bias.shape[2]), f32),
        ],
        scratch_shapes=[pltpu.VMEM((rows, width), bf16)] * 4
        + [pltpu.VMEM((rows, width), f32), pltpu.VMEM(bias.shape, f32)],
        compiler_params=params(),
        name="self_backward",
    )(*operands)


def pack(shard):
    rows, columns = shard.shape
    tiles = columns // lane_tile
    return (
        shard.reshape(rows, tiles, lane_tile)
        .transpose(1, 0, 2)
        .reshape(rows * tiles, lane_tile)
    )


def unpack(packed, rows, columns):
    tiles = columns // lane_tile
    return packed.reshape(tiles, rows, lane_tile).transpose(1, 0, 2).reshape(rows, columns)


def regroup(packed, from_groups, to_groups, shapes):
    if from_groups == to_groups:
        return packed
    parts = []
    offset = 0
    for rows, columns in shapes:
        tiles = columns // lane_tile
        size = rows // from_groups * tiles
        part = packed[:, offset : offset + size, :]
        offset += size
        part = part.reshape(from_groups, tiles, rows // from_groups, lane_tile)
        part = part.transpose(0, 2, 1, 3).reshape(to_groups, rows // to_groups, tiles, lane_tile)
        parts.append(
            part.transpose(0, 2, 1, 3).reshape(to_groups, rows // to_groups * tiles, lane_tile)
        )
    return jnp.concatenate(parts, axis=1)


def gather(shards, shapes, groups, devices):
    packed = jnp.concatenate([pack(shard) for shard in shards], axis=0)
    whole = lax.all_gather(packed, axes, axis=0, tiled=False)
    return regroup(whole, devices, groups, shapes)


def scatter(packed, shapes, groups, devices):
    packed = regroup(packed, groups, devices, shapes)
    share = lax.psum_scatter(packed, axes, scatter_dimension=0, tiled=False)
    parts = []
    offset = 0
    for rows, columns in shapes:
        size = rows // devices * (columns // lane_tile)
        parts.append(
            unpack(share[offset : offset + size], rows // devices, columns).astype(f32)
        )
        offset += size
    return parts


def on_device(
    devices,
    targets,
    memory,
    mem_lengths,
    buckets,
    cotangent,
    gain_self,
    gain_cross,
    gain_feed,
    self_query,
    self_key,
    self_value,
    self_output,
    cross_query,
    cross_key,
    cross_value,
    cross_output,
    gate_weight,
    up_weight,
    down_weight,
    bias_table,
):
    batch, target_len, width = targets.shape
    bucket_count, head_count = bias_table.shape
    row_count = batch * target_len
    groups = width // group_rows
    square = (width, width)
    feed_width = gate_weight.shape[1]
    feed_shapes = [(width, feed_width), (width, feed_width), (feed_width, width)]

    packed_memory = gather([cross_key, cross_value], [square] * 2, groups, devices)
    packed_self = gather(
        [self_query, self_key, self_value, self_output, cross_query, cross_output],
        [square] * 6,
        groups,
        devices,
    )
    gains = lax.all_gather(
        jnp.stack([gain_self, gain_cross, gain_feed]), axes, axis=1, tiled=True
    ).astype(f32)
    packed_feed = gather([gate_weight, up_weight, down_weight], feed_shapes, groups, devices)

    pad = pair_width - target_len
    bucket_hot = (
        buckets[:, :, None] == lax.broadcasted_iota(jnp.int32, (1, 1, bucket_count), 2)
    ).reshape(target_len * target_len, bucket_count)
    bias = (
        dot(bucket_hot.astype(bf16), bias_table)
        .reshape(target_len, target_len, head_count)
        .transpose(2, 0, 1)
    )
    causal = lax.broadcasted_iota(jnp.int32, (target_len, target_len), 1) <= lax.broadcasted_iota(
        jnp.int32, (target_len, target_len), 0
    )
    bias = jnp.where(causal, bias, masked_out)
    bias = jnp.pad(bias, ((0, 0), (0, 0), (0, pad)), constant_values=masked_out)
    bias = (
        bias.reshape(head_count // 2, 2, target_len, pair_width)
        .transpose(0, 2, 1, 3)
        .reshape(head_count // 2, target_len, 2 * pair_width)
    )
    wide_buckets = jnp.pad(buckets, ((0, 0), (0, pad)), constant_values=-1)
    target_rows = targets.reshape(row_count, width)
    cot_rows = cotangent.reshape(row_count, width)

    mem_keys, mem_values = project_memory(mem_lengths, memory, packed_memory)
    normed_one, queries, key_rows, value_rows, self_context, after_self, normed_two, side = (
        self_forward(target_len, target_rows, packed_self, bias, gains[0:1], gains[1:2])
    )
    cross_context, weights = cross_forward(mem_lengths, side, mem_keys, mem_values, head_count)
    outputs, grad_after_cross, grad_context, grad_gain_feed, feed_grads = feed_both(
        after_self, cross_context, cot_rows, gains[2:3], packed_self, packed_feed
    )
    share_gate, share_up, share_down, share_cross_output = scatter(
        feed_grads, feed_shapes + [square], groups, devices
    )
    grad_side, grad_mem_keys, grad_mem_values = cross_backward(
        mem_lengths, grad_context, cross_context, side, mem_keys, mem_values, weights
    )
    target_grad, self_grads, grad_gains, table_parts = self_backward(
        target_len,
        bucket_count,
        (
            grad_side,
            after_self,
            grad_after_cross,
            normed_two,
            normed_one,
            queries,
            key_rows,
            value_rows,
            self_context,
            target_rows,
            packed_self,
            bias,
            wide_buckets,
            gains[0:1],
            gains[1:2],
        ),
    )
    share_query, share_key, share_value, share_output, share_cross_query = scatter(
        self_grads, [square] * 5, groups, devices
    )
    memory_grads = memory_weight_grads(
        mem_lengths, memory, grad_mem_keys, grad_mem_values, packed_memory.shape
    )
    share_cross_key, share_cross_value = scatter(memory_grads, [square] * 2, groups, devices)
    memory_grad = memory_gradient(mem_lengths, grad_mem_keys, grad_mem_values, packed_memory)

    table_part = (
        table_parts.reshape(bucket_count, head_count, pair_width).sum(axis=-1).reshape(-1)
    )
    small = jnp.concatenate(
        [grad_gains[0], grad_gains[1], grad_gain_feed[0], table_part], axis=0
    )
    small = jnp.sum(lax.all_gather(small, axes, axis=0, tiled=False), axis=0)
    table_grad = small[3 * width :].reshape(bucket_count, head_count)
    own = width // devices
    place = lax.axis_index(axes) * own

    def own_gain(index):
        return lax.dynamic_slice(small, (index * width + place,), (own,))

    return (
        outputs.reshape(targets.shape),
        target_grad.reshape(targets.shape),
        memory_grad,
        own_gain(0),
        own_gain(1),
        own_gain(2),
        share_query,
        share_key,
        share_value,
        share_output,
        share_cross_query,
        share_cross_key,
        share_cross_value,
        share_cross_output,
        share_gate,
        share_up,
        share_down,
        table_grad,
    )


def solution(mesh):
    devices = mesh.shape["dp"] * mesh.shape["seq"]
    rows = P(axes, None, None)
    flat = P(axes)
    weight = P(axes, None)

    def body(*arguments):
        return on_device(devices, *arguments)

    return jax.shard_map(
        body,
        mesh=mesh,
        in_specs=(rows, rows, flat, P(), rows, flat, flat, flat) + (weight,) * 11 + (P(),),
        out_specs=(rows, rows, rows, flat, flat, flat) + (weight,) * 11 + (P(),),
        check_vma=False,
    )
```

```python
import math

import jax
import jax.numpy as jnp
from jax import lax
from jax.experimental import pallas as pl
from jax.experimental.pallas import tpu as pltpu
from jax.sharding import PartitionSpec as P

epsilon = 1e-06
masked_out = -1e30
bf16 = jnp.bfloat16
f32 = jnp.float32
axes = ("dp", "seq")
lane_tile = 256
group_rows = 24
pair_width = 128
NN = (((1,), (0,)), ((), ()))
NT = (((1,), (1,)), ((), ()))
TN = (((0,), (0,)), ((), ()))
gelu_scale = math.sqrt(2.0 / math.pi)
gelu_cubic = 0.044715


def dot(left_side, right_side, dims=NN):
    return lax.dot_general(left_side, right_side, dims, preferred_element_type=f32)


def params():
    return pltpu.CompilerParams(vmem_limit_bytes=60 * 1024 * 1024)


def cost(flops, size, exps=0):
    return pl.CostEstimate(
        flops=int(flops), bytes_accessed=int(size), transcendentals=int(exps)
    )


def column_tile(packed_ref, index):
    tile = packed_ref[:, index * group_rows : (index + 1) * group_rows, :]
    return tile.reshape(tile.shape[0] * group_rows, lane_tile)


def put_column_tile(packed_ref, index, values):
    groups = packed_ref.shape[0]
    packed_ref[:, index * group_rows : (index + 1) * group_rows, :] = values.reshape(
        groups, group_rows, lane_tile
    ).astype(bf16)


def lane_halves(rows):
    lanes = lax.broadcasted_iota(jnp.int32, (rows, pair_width), 1)
    return lanes < pair_width // 2


def project(rows, packed_ref, base, tiles):
    return [dot(rows, column_tile(packed_ref, base + t)) for t in range(tiles)]


def through(rows, packed_ref, base, tiles):
    total = None
    for t in range(tiles):
        part = dot(
            rows[:, t * lane_tile : (t + 1) * lane_tile], column_tile(packed_ref, base + t), NT
        )
        total = part if total is None else total + part
    return total


def put_weight_grad(packed_ref, base, rows, grads):
    for t in range(grads.shape[1] // lane_tile):
        part = dot(rows, grads[:, t * lane_tile : (t + 1) * lane_tile], TN)
        put_column_tile(packed_ref, base + t, part)


def put_slots(owners, keep_ref, send_ref, stage_ref, index, values):
    stage_ref[...] = values
    half = keep_ref.shape[0]
    part = slice(index * group_rows, (index + 1) * group_rows)

    def place(slot, carry):
        for offset, out_ref in ((0, keep_ref), (half, send_ref)):
            start = pl.multiple_of(owners[slot + offset] * group_rows, 8)
            out_ref[slot, part, :] = stage_ref[pl.ds(start, group_rows), :].astype(bf16)
        return carry

    lax.fori_loop(0, half, place, 0)


def norm_scale(values):
    return lax.rsqrt(jnp.mean(values * values, axis=-1, keepdims=True) + epsilon)


def norm_pullback(values, gain_row, grad_in):
    inverse = norm_scale(values)
    weighted = grad_in * gain_row
    inner = jnp.mean(weighted * values, axis=-1, keepdims=True)
    grad_values = inverse * weighted - values * (inverse * inverse * inverse * inner)
    grad_gain = jnp.sum(grad_in * values * inverse, axis=0, keepdims=True)
    return grad_values, grad_gain


def memory_kernel(lengths, slots, memory_ref, packed_ref, keys_ref, values_ref, weight_ref):
    seq = pl.program_id(0)
    memory_len = memory_ref.shape[1]
    tiles = weight_ref.shape[1] // lane_tile

    @pl.when(seq == 0)
    def _():
        def place(pair, carry):
            first = slots[2 * pair]
            second = slots[2 * pair + 1]
            rows = pl.ds(pl.multiple_of(2 * group_rows * pair, 16), 2 * group_rows)
            for t in range(tiles):
                part = slice(t * group_rows, (t + 1) * group_rows)
                weight_ref[rows, t * lane_tile : (t + 1) * lane_tile] = jnp.concatenate(
                    [packed_ref[first, part, :], packed_ref[second, part, :]], axis=0
                )
            return carry

        lax.fori_loop(0, weight_ref.shape[0] // (2 * group_rows), place, 0)

    def fill(count):
        rows = memory_ref[0, :count, :]
        for base, out_ref in ((0, keys_ref), (3, values_ref)):
            for t in range(3):
                out_ref[0, :count, t * lane_tile : (t + 1) * lane_tile] = dot(
                    rows, weight_ref[:, (base + t) * lane_tile : (base + t + 1) * lane_tile]
                ).astype(bf16)

    @pl.when(lengths[seq] > memory_len // 2)
    def _():
        fill(memory_len)

    @pl.when(lengths[seq] <= memory_len // 2)
    def _():
        fill(memory_len // 2)


def project_memory(mem_lengths, slots, memory, packed):
    batch, memory_len, width = memory.shape
    block = pl.BlockSpec((1, memory_len, width), lambda b, n, s: (b, 0, 0))
    return pl.pallas_call(
        memory_kernel,
        out_shape=[jax.ShapeDtypeStruct(memory.shape, bf16)] * 2
        + [jax.ShapeDtypeStruct((width, 2 * width), bf16)],
        grid_spec=pltpu.PrefetchScalarGridSpec(
            num_scalar_prefetch=2,
            grid=(batch,),
            in_specs=[block, pl.BlockSpec(packed.shape, lambda b, n, s: (0, 0, 0))],
            out_specs=[block, block, pl.BlockSpec((width, 2 * width), lambda b, n, s: (0, 0))],
        ),
        compiler_params=params(),
        cost_estimate=cost(4 * memory.size * width, 6 * memory.size),
        name="memory_project",
    )(mem_lengths, slots, memory, packed)


def stacked_pair(rows, half, pad):
    zero = jnp.zeros_like(rows)
    gap = jnp.zeros((pad, pair_width), rows.dtype)
    return jnp.concatenate(
        [jnp.where(half, rows, zero), gap, jnp.where(half, zero, rows), gap], axis=0
    )


def pair_softmax(scores):
    parts = []
    for h in range(2):
        one = scores[:, h * pair_width : (h + 1) * pair_width]
        terms = jnp.exp(one - jnp.max(one, axis=-1, keepdims=True))
        parts.append(terms * (1.0 / jnp.sum(terms, axis=-1, keepdims=True)))
    return parts


def self_forward_kernel(
    target_len,
    targets_ref,
    packed_ref,
    bias_ref,
    gain_self_ref,
    gain_cross_ref,
    normed_one_ref,
    queries_ref,
    keys_ref,
    values_ref,
    context_ref,
    after_ref,
    normed_two_ref,
    side_ref,
):
    inputs = targets_ref[...].astype(f32)
    normed_one = (inputs * norm_scale(inputs) * gain_self_ref[...]).astype(bf16)
    normed_one_ref[...] = normed_one
    for base, out_ref in ((0, queries_ref), (3, keys_ref), (6, values_ref)):
        for t in range(3):
            out_ref[:, t * lane_tile : (t + 1) * lane_tile] = dot(
                normed_one, column_tile(packed_ref, base + t)
            ).astype(bf16)
    half = lane_halves(target_len)
    pad = pair_width - target_len
    pairs = bias_ref.shape[0]

    def attend(seq, carry):
        rows = pl.ds(pl.multiple_of(seq * target_len, 32), target_len)
        for p in range(pairs):
            cols = slice(p * pair_width, (p + 1) * pair_width)
            key_stack = stacked_pair(keys_ref[rows, cols], half, pad)
            value_stack = stacked_pair(values_ref[rows, cols], half, pad)
            scores = dot(queries_ref[rows, cols], key_stack, NT) + bias_ref[p]
            probs = jnp.concatenate(pair_softmax(scores), axis=1)
            context_ref[rows, cols] = dot(probs.astype(bf16), value_stack).astype(bf16)
        return carry

    lax.fori_loop(0, targets_ref.shape[0] // target_len, attend, 0)
    after = inputs + jnp.concatenate(project(context_ref[...], packed_ref, 9, 3), axis=1)
    after_ref[...] = after
    normed_two = (after * norm_scale(after) * gain_cross_ref[...]).astype(bf16)
    normed_two_ref[...] = normed_two
    for t in range(3):
        side_ref[:, t * lane_tile : (t + 1) * lane_tile] = dot(
            normed_two, column_tile(packed_ref, 12 + t)
        ).astype(bf16)


def self_forward(target_len, targets, packed, bias, gain_self, gain_cross):
    low = jax.ShapeDtypeStruct(targets.shape, bf16)
    wide = jax.ShapeDtypeStruct(targets.shape, f32)

    def body(*refs):
        self_forward_kernel(target_len, *refs)

    return pl.pallas_call(
        body,
        out_shape=[low, low, low, low, low, wide, low, low],
        compiler_params=params(),
        cost_estimate=cost(20 * targets.size * targets.shape[1], 16 * targets.size),
        name="self_forward",
    )(targets, packed, bias, gain_self, gain_cross)


def masked_stack(rows, half):
    zero = jnp.zeros_like(rows)
    return jnp.concatenate([jnp.where(half, rows, zero), jnp.where(half, zero, rows)], axis=0)


def cross_forward_kernel(lengths, side_ref, keys_ref, values_ref, context_ref, weights_ref):
    seq = pl.program_id(0)
    target_len, width = side_ref.shape
    memory_len = keys_ref.shape[1]
    half = lane_halves(target_len)

    def attend(count):
        for p in range(width // pair_width):
            cols = slice(p * pair_width, (p + 1) * pair_width)
            stack = masked_stack(side_ref[:, cols], half)
            scores = dot(stack, keys_ref[0, :count, cols], NT)
            terms = jnp.exp(scores - jnp.max(scores, axis=-1, keepdims=True))
            scale = 1.0 / jnp.sum(terms, axis=-1, keepdims=True)
            weights = (terms * scale).astype(bf16)
            weights_ref[0, 2 * target_len * p : 2 * target_len * (p + 1), :count] = weights
            both = dot(weights, values_ref[0, :count, cols])
            context_ref[:, cols] = jnp.where(half, both[:target_len], both[target_len:]).astype(
                bf16
            )

    @pl.when(lengths[seq] > memory_len // 2)
    def _():
        attend(memory_len)

    @pl.when(lengths[seq] <= memory_len // 2)
    def _():
        attend(memory_len // 2)


def cross_forward(mem_lengths, side, mem_keys, mem_values, head_count):
    batch, memory_len, width = mem_keys.shape
    target_len = side.shape[0] // batch
    rows = pl.BlockSpec((target_len, width), lambda b, n: (b, 0))
    memory = pl.BlockSpec((1, memory_len, width), lambda b, n: (b, 0, 0))
    weights = pl.BlockSpec((1, head_count * target_len, memory_len), lambda b, n: (b, 0, 0))
    return pl.pallas_call(
        cross_forward_kernel,
        out_shape=[
            jax.ShapeDtypeStruct(side.shape, bf16),
            jax.ShapeDtypeStruct((batch, head_count * target_len, memory_len), bf16),
        ],
        grid_spec=pltpu.PrefetchScalarGridSpec(
            num_scalar_prefetch=1,
            grid=(batch,),
            in_specs=[rows, memory, memory],
            out_specs=[rows, weights],
        ),
        compiler_params=params(),
        cost_estimate=cost(16 * side.size * memory_len, 6 * mem_keys.size, batch * head_count * target_len * memory_len),
        name="cross_forward",
    )(mem_lengths, side, mem_keys, mem_values)


def feed_kernel(
    after_ref,
    context_ref,
    cot_ref,
    gain_ref,
    side_output_ref,
    gate_ref,
    up_ref,
    down_ref,
    outputs_ref,
    grad_after_ref,
    grad_context_ref,
    grad_gain_ref,
    packed_ref,
    after_cross_ref,
    normed_ref,
    out_total_ref,
    grad_normed_ref,
):
    step = pl.program_id(0)
    steps = pl.num_programs(0)

    @pl.when(step == 0)
    def _():
        after_cross = after_ref[...] + jnp.concatenate(
            project(context_ref[...], side_output_ref, 0, 3), axis=1
        )
        after_cross_ref[...] = after_cross
        normed_ref[...] = (after_cross * norm_scale(after_cross) * gain_ref[...]).astype(bf16)
        out_total_ref[...] = after_cross
        grad_normed_ref[...] = jnp.zeros_like(grad_normed_ref)

    normed = normed_ref[...]
    cot = cot_ref[...]
    gate_weight = column_tile(gate_ref, 0)
    up_weight = column_tile(up_ref, 0)
    share = down_ref.shape[1] // 3
    owners = down_ref.shape[0]
    down_weight = jnp.concatenate(
        [
            down_ref[:, c * share : (c + 1) * share, :].reshape(owners * share, lane_tile)
            for c in range(3)
        ],
        axis=1,
    )
    gate = dot(normed, gate_weight)
    up = dot(normed, up_weight)
    grad_hidden = dot(cot, down_weight, NT)
    square = gate * gate
    tanh = jnp.tanh(gelu_scale * (gate + gelu_cubic * (square * gate)))
    half_sum = 0.5 * (1.0 + tanh)
    active = gate * half_sum
    slope = half_sum + 0.5 * gate * (1.0 - tanh * tanh) * (
        gelu_scale * (1.0 + 3.0 * gelu_cubic * square)
    )
    hidden = (active * up).astype(bf16)
    grad_gate = (grad_hidden * up * slope).astype(bf16)
    grad_up = (grad_hidden * active).astype(bf16)
    out_total_ref[...] += dot(hidden, down_weight)
    grad_normed_ref[...] += dot(grad_gate, gate_weight, NT) + dot(grad_up, up_weight, NT)
    groups = packed_ref.shape[0]

    def put(base, value):
        packed_ref[:, pl.ds(base + step * group_rows, group_rows), :] = value.reshape(
            groups, group_rows, lane_tile
        ).astype(bf16)

    put(0, dot(normed, grad_gate, TN))
    put(steps * group_rows, dot(normed, grad_up, TN))
    down_base = 2 * steps * group_rows
    for c in range(3):
        part = dot(hidden, cot[:, c * lane_tile : (c + 1) * lane_tile], TN)
        packed_ref[
            pl.ds(step * owners, owners), down_base + c * share : down_base + (c + 1) * share, :
        ] = part.reshape(owners, share, lane_tile).astype(bf16)

    @pl.when(step == steps - 1)
    def _():
        outputs_ref[...] = out_total_ref[...].astype(bf16)
        grad_in, grad_gain = norm_pullback(
            after_cross_ref[...], gain_ref[...], grad_normed_ref[...]
        )
        grad_gain_ref[...] = grad_gain
        grad_after = cot_ref[...].astype(f32) + grad_in
        grad_after_ref[...] = grad_after
        low = grad_after.astype(bf16)
        put_weight_grad(packed_ref, 3 * down_base // (2 * group_rows), context_ref[...], low)
        grad_context_ref[...] = through(low, side_output_ref, 0, 3).astype(bf16)


def feed_both(after_self, context, cotangent, gain, packed_self, packed_feed):
    rows, width = context.shape
    groups, feed_rows, _ = packed_feed.shape
    steps = feed_rows // (3 * group_rows)
    owners = groups // steps
    whole = lambda f: (0, 0)
    full = pl.BlockSpec((rows, width), whole)
    tile = (groups, group_rows, lane_tile)
    out_rows = feed_rows + 3 * group_rows
    return pl.pallas_call(
        feed_kernel,
        out_shape=[
            jax.ShapeDtypeStruct((rows, width), bf16),
            jax.ShapeDtypeStruct((rows, width), f32),
            jax.ShapeDtypeStruct((rows, width), bf16),
            jax.ShapeDtypeStruct((1, width), f32),
            jax.ShapeDtypeStruct((groups, out_rows, lane_tile), bf16),
        ],
        grid=(steps,),
        in_specs=[
            full,
            full,
            full,
            pl.BlockSpec((1, width), whole),
            pl.BlockSpec((groups, 3 * group_rows, lane_tile), lambda f: (0, 5, 0)),
            pl.BlockSpec(tile, lambda f: (0, f, 0)),
            pl.BlockSpec(tile, lambda f: (0, steps + f, 0)),
            pl.BlockSpec((owners, steps * group_rows, lane_tile), lambda f: (f, 2, 0)),
        ],
        out_specs=[
            full,
            full,
            full,
            pl.BlockSpec((1, width), whole),
            pl.BlockSpec((groups, out_rows, lane_tile), lambda f: (0, 0, 0)),
        ],
        scratch_shapes=[
            pltpu.VMEM((rows, width), f32),
            pltpu.VMEM((rows, width), bf16),
            pltpu.VMEM((rows, width), f32),
            pltpu.VMEM((rows, width), f32),
        ],
        compiler_params=params(),
        cost_estimate=cost(18 * rows * width * steps * lane_tile, 30 * rows * width),
        name="feed_both",
    )(after_self, context, cotangent, gain, packed_self, packed_feed, packed_feed, packed_feed)


def cross_backward_kernel(
    lengths,
    grad_ref,
    context_ref,
    side_ref,
    keys_ref,
    values_ref,
    weights_ref,
    grad_side_ref,
    grad_keys_ref,
    grad_values_ref,
):
    seq = pl.program_id(0)
    target_len, width = side_ref.shape
    memory_len = keys_ref.shape[1]
    half = lane_halves(target_len)

    def attend(count):
        for p in range(width // pair_width):
            cols = slice(p * pair_width, (p + 1) * pair_width)
            grad_rows = grad_ref[:, cols]
            grad_stack = masked_stack(grad_rows, half)
            query_stack = masked_stack(side_ref[:, cols], half)
            product = grad_rows.astype(f32) * context_ref[:, cols].astype(f32)
            inner = jnp.sum(masked_stack(product, half), axis=-1, keepdims=True)
            weights = weights_ref[0, 2 * target_len * p : 2 * target_len * (p + 1), :count]
            grad_probs = dot(grad_stack, values_ref[0, :count, cols], NT)
            grad_scores = (weights.astype(f32) * (grad_probs - inner)).astype(bf16)
            both = dot(grad_scores, keys_ref[0, :count, cols])
            grad_side_ref[:, cols] = jnp.where(half, both[:target_len], both[target_len:]).astype(
                bf16
            )
            grad_keys_ref[0, cols, :count] = dot(query_stack, grad_scores, TN).astype(bf16)
            grad_values_ref[0, cols, :count] = dot(grad_stack, weights, TN).astype(bf16)

    @pl.when(lengths[seq] > memory_len // 2)
    def _():
        attend(memory_len)

    @pl.when(lengths[seq] <= memory_len // 2)
    def _():
        attend(memory_len // 2)


def cross_backward(mem_lengths, grad_context, context, side, mem_keys, mem_values, weights):
    batch, memory_len, width = mem_keys.shape
    target_len = side.shape[0] // batch
    rows = pl.BlockSpec((target_len, width), lambda b, n: (b, 0))
    memory = pl.BlockSpec((1, memory_len, width), lambda b, n: (b, 0, 0))
    turned = pl.BlockSpec((1, width, memory_len), lambda b, n: (b, 0, 0))
    return pl.pallas_call(
        cross_backward_kernel,
        out_shape=[jax.ShapeDtypeStruct(side.shape, bf16)]
        + [jax.ShapeDtypeStruct((batch, width, memory_len), bf16)] * 2,
        grid_spec=pltpu.PrefetchScalarGridSpec(
            num_scalar_prefetch=1,
            grid=(batch,),
            in_specs=[
                rows,
                rows,
                rows,
                memory,
                memory,
                pl.BlockSpec((1,) + weights.shape[1:], lambda b, n: (b, 0, 0)),
            ],
            out_specs=[rows, turned, turned],
        ),
        compiler_params=params(),
        cost_estimate=cost(32 * side.size * memory_len, 10 * mem_keys.size),
        name="cross_backward",
    )(mem_lengths, grad_context, context, side, mem_keys, mem_values, weights)


def memory_weight_kernel(
    lengths,
    owners,
    memory_ref,
    grad_keys_ref,
    grad_values_ref,
    keep_ref,
    send_ref,
    key_total_ref,
    value_total_ref,
    stage_ref,
):
    seq = pl.program_id(0)
    memory_len = memory_ref.shape[1]

    @pl.when(seq == 0)
    def _():
        key_total_ref[...] = jnp.zeros_like(key_total_ref)
        value_total_ref[...] = jnp.zeros_like(value_total_ref)

    def add(count):
        rows = memory_ref[0, :count, :]
        key_total_ref[...] += dot(grad_keys_ref[0, :, :count], rows)
        value_total_ref[...] += dot(grad_values_ref[0, :, :count], rows)

    @pl.when(lengths[seq] > memory_len // 2)
    def _():
        add(memory_len)

    @pl.when(lengths[seq] <= memory_len // 2)
    def _():
        add(memory_len // 2)

    @pl.when(seq == pl.num_programs(0) - 1)
    def _():
        for base, total_ref in ((0, key_total_ref), (3, value_total_ref)):
            for t in range(3):
                put_slots(
                    owners,
                    keep_ref,
                    send_ref,
                    stage_ref,
                    base + t,
                    jnp.transpose(total_ref[t * lane_tile : (t + 1) * lane_tile, :]),
                )


def memory_weight_grads(mem_lengths, owners, memory, grad_keys, grad_values):
    batch, memory_len, width = memory.shape
    block = pl.BlockSpec((1, memory_len, width), lambda b, n, o: (b, 0, 0))
    turned = pl.BlockSpec((1, width, memory_len), lambda b, n, o: (b, 0, 0))
    half = (owners.shape[0] // 2, 2 * width // lane_tile * group_rows, lane_tile)
    return pl.pallas_call(
        memory_weight_kernel,
        out_shape=[jax.ShapeDtypeStruct(half, bf16)] * 2,
        grid_spec=pltpu.PrefetchScalarGridSpec(
            num_scalar_prefetch=2,
            grid=(batch,),
            in_specs=[block, turned, turned],
            out_specs=[pl.BlockSpec(half, lambda b, n, o: (0, 0, 0))] * 2,
            scratch_shapes=[pltpu.VMEM((width, width), f32)] * 2
            + [pltpu.VMEM((width, lane_tile), f32)],
        ),
        compiler_params=params(),
        cost_estimate=cost(4 * memory.size * width, 6 * memory.size),
        name="memory_weight_grads",
    )(mem_lengths, owners, memory, grad_keys, grad_values)


def memory_grad_kernel(
    lengths, grad_keys_ref, grad_values_ref, weight_ref, out_ref, key_turned_ref, value_turned_ref
):
    seq = pl.program_id(0)
    memory_len = out_ref.shape[1]

    @pl.when(seq == 0)
    def _():
        for base, turned_ref in ((0, key_turned_ref), (3, value_turned_ref)):
            for t in range(3):
                turned_ref[t * lane_tile : (t + 1) * lane_tile, :] = jnp.transpose(
                    weight_ref[:, (base + t) * lane_tile : (base + t + 1) * lane_tile]
                )

    def fill(count):
        out_ref[0, :count, :] = (
            dot(grad_keys_ref[0, :, :count], key_turned_ref[...], TN)
            + dot(grad_values_ref[0, :, :count], value_turned_ref[...], TN)
        ).astype(bf16)

    @pl.when(lengths[seq] > memory_len // 2)
    def _():
        fill(memory_len)

    @pl.when(lengths[seq] <= memory_len // 2)
    def _():
        fill(memory_len // 2)
        out_ref[0, memory_len // 2 :, :] = jnp.zeros_like(out_ref[0, memory_len // 2 :, :])


def memory_gradient(mem_lengths, grad_keys, grad_values, weight):
    batch, width, memory_len = grad_keys.shape
    turned = pl.BlockSpec((1, width, memory_len), lambda b, n: (b, 0, 0))
    return pl.pallas_call(
        memory_grad_kernel,
        out_shape=jax.ShapeDtypeStruct((batch, memory_len, width), bf16),
        grid_spec=pltpu.PrefetchScalarGridSpec(
            num_scalar_prefetch=1,
            grid=(batch,),
            in_specs=[turned, turned, pl.BlockSpec(weight.shape, lambda b, n: (0, 0))],
            out_specs=pl.BlockSpec((1, memory_len, width), lambda b, n: (b, 0, 0)),
            scratch_shapes=[pltpu.VMEM((width, width), bf16)] * 2,
        ),
        compiler_params=params(),
        cost_estimate=cost(4 * grad_keys.size * width, 6 * grad_keys.size),
        name="memory_grad",
    )(mem_lengths, grad_keys, grad_values, weight)


def self_backward_kernel(
    target_len,
    owners,
    grad_side_ref,
    after_ref,
    grad_after_ref,
    normed_two_ref,
    normed_one_ref,
    queries_ref,
    keys_ref,
    values_ref,
    context_ref,
    targets_ref,
    packed_ref,
    bias_ref,
    buckets_ref,
    gain_self_ref,
    gain_cross_ref,
    target_grad_ref,
    keep_ref,
    send_ref,
    grad_gains_ref,
    table_ref,
    grad_queries_ref,
    grad_keys_ref,
    grad_values_ref,
    grad_context_ref,
    total_ref,
    score_total_ref,
    stage_ref,
):
    def put(base, rows, grads):
        for t in range(grads.shape[1] // lane_tile):
            part = dot(rows, grads[:, t * lane_tile : (t + 1) * lane_tile], TN)
            put_slots(owners, keep_ref, send_ref, stage_ref, base + t, part)

    grad_side = grad_side_ref[...]
    grad_in, grad_gain_cross = norm_pullback(
        after_ref[...], gain_cross_ref[...], through(grad_side, packed_ref, 12, 3)
    )
    put(12, normed_two_ref[...], grad_side)
    grad_after = grad_after_ref[...] + grad_in
    total_ref[...] = grad_after
    low = grad_after.astype(bf16)
    put(9, context_ref[...], low)
    grad_context_ref[...] = through(low, packed_ref, 9, 3).astype(bf16)
    half = lane_halves(target_len)
    pad = pair_width - target_len
    pairs = bias_ref.shape[0]
    score_total_ref[...] = jnp.zeros_like(score_total_ref)

    def pick(values):
        return jnp.where(
            half, values[:target_len], values[pair_width : pair_width + target_len]
        ).astype(bf16)

    def attend(seq, carry):
        rows = pl.ds(pl.multiple_of(seq * target_len, 32), target_len)
        for p in range(pairs):
            cols = slice(p * pair_width, (p + 1) * pair_width)
            queries = queries_ref[rows, cols]
            grad_rows = grad_context_ref[rows, cols]
            key_stack = stacked_pair(keys_ref[rows, cols], half, pad)
            value_stack = stacked_pair(values_ref[rows, cols], half, pad)
            scores = dot(queries, key_stack, NT) + bias_ref[p]
            probs = pair_softmax(scores)
            grad_probs = dot(grad_rows, value_stack, NT)
            parts = []
            for h in range(2):
                one = grad_probs[:, h * pair_width : (h + 1) * pair_width]
                inner = jnp.sum(one * probs[h], axis=-1, keepdims=True)
                parts.append(probs[h] * (one - inner))
            grad_scores = jnp.concatenate(parts, axis=1).astype(bf16)
            weights = jnp.concatenate(probs, axis=1).astype(bf16)
            score_total_ref[p] += grad_scores.astype(f32)
            grad_queries_ref[rows, cols] = dot(grad_scores, key_stack).astype(bf16)
            grad_keys_ref[rows, cols] = pick(dot(grad_scores, queries, TN))
            grad_values_ref[rows, cols] = pick(dot(weights, grad_rows, TN))
        return carry

    lax.fori_loop(0, targets_ref.shape[0] // target_len, attend, 0)
    buckets = buckets_ref[...]
    both = jnp.concatenate([buckets, buckets], axis=1)

    def count(bucket, carry):
        chosen = both == bucket
        for p in range(pairs):
            table_ref[bucket, p : p + 1, :] = jnp.sum(
                jnp.where(chosen, score_total_ref[p], 0.0), axis=0, keepdims=True
            )
        return carry

    lax.fori_loop(0, table_ref.shape[0], count, 0)
    normed_one = normed_one_ref[...]
    total = None
    for base, grad_ref in ((0, grad_queries_ref), (3, grad_keys_ref), (6, grad_values_ref)):
        grads = grad_ref[...]
        put(base, normed_one, grads)
        part = through(grads, packed_ref, base, 3)
        total = part if total is None else total + part
    grad_in, grad_gain_self = norm_pullback(
        targets_ref[...].astype(f32), gain_self_ref[...], total
    )
    target_grad_ref[...] = (total_ref[...] + grad_in).astype(bf16)
    grad_gains_ref[0:1, :] = grad_gain_self
    grad_gains_ref[1:2, :] = grad_gain_cross


def self_backward(target_len, bucket_count, owners, operands):
    targets = operands[9]
    bias = operands[11]
    rows, width = targets.shape
    half = (owners.shape[0] // 2, 15 * group_rows, lane_tile)
    whole = pl.BlockSpec(memory_space=pltpu.VMEM)

    def body(*refs):
        self_backward_kernel(target_len, *refs)

    return pl.pallas_call(
        body,
        out_shape=[
            jax.ShapeDtypeStruct((rows, width), bf16),
            jax.ShapeDtypeStruct(half, bf16),
            jax.ShapeDtypeStruct(half, bf16),
            jax.ShapeDtypeStruct((2, width), f32),
            jax.ShapeDtypeStruct((bucket_count, bias.shape[0], bias.shape[2]), f32),
        ],
        in_specs=[pl.BlockSpec(memory_space=pltpu.SMEM)] + [whole] * len(operands),
        scratch_shapes=[pltpu.VMEM((rows, width), bf16)] * 4
        + [
            pltpu.VMEM((rows, width), f32),
            pltpu.VMEM(bias.shape, f32),
            pltpu.VMEM((width, lane_tile), f32),
        ],
        compiler_params=params(),
        cost_estimate=cost(40 * targets.size * width, 20 * targets.size),
        name="self_backward",
    )(owners, *operands)


def pack(shard):
    rows, columns = shard.shape
    tiles = columns // lane_tile
    return (
        shard.reshape(rows, tiles, lane_tile)
        .transpose(1, 0, 2)
        .reshape(rows * tiles, lane_tile)
    )


def unpack(packed, rows, columns):
    tiles = columns // lane_tile
    return packed.reshape(tiles, rows, lane_tile).transpose(1, 0, 2).reshape(rows, columns)


def regroup(packed, from_groups, to_groups, shapes):
    if from_groups == to_groups:
        return packed
    parts = []
    offset = 0
    for rows, columns in shapes:
        tiles = columns // lane_tile
        size = rows // from_groups * tiles
        part = packed[:, offset : offset + size, :]
        offset += size
        part = part.reshape(from_groups, tiles, rows // from_groups, lane_tile)
        part = part.transpose(0, 2, 1, 3).reshape(to_groups, rows // to_groups, tiles, lane_tile)
        parts.append(
            part.transpose(0, 2, 1, 3).reshape(to_groups, rows // to_groups * tiles, lane_tile)
        )
    return jnp.concatenate(parts, axis=1)


def gather(shards, shapes, groups, devices):
    packed = jnp.concatenate([pack(shard) for shard in shards], axis=0)
    whole = lax.all_gather(packed, axes, axis=0, tiled=False)
    return regroup(whole, devices, groups, shapes)


def scatter(packed, shapes, groups, devices):
    packed = regroup(packed, groups, devices, shapes)
    share = lax.psum_scatter(packed, axes, scatter_dimension=0, tiled=False)
    return split_share(share, shapes, devices)


core_step = (2,)
plane_steps = (1, 4, 5)
line_steps = (8, 16, 24)


def exchange(values, step):
    return lax.ppermute(values, axes, [(i, i ^ step) for i in range(32)])


def slot_tables():
    here = lax.axis_index(axes)
    device = jnp.arange(32, dtype=jnp.int32)
    gap = device ^ here
    slots = ((gap >> 1) & 1) * 16 + ((gap & 1) + ((gap >> 2) & 1) * 2) * 4 + (gap >> 3)
    far = device & 15
    owners = here ^ ((device >> 4) * 2 + (far >> 2 & 1) + (far >> 3) * 4 + (far & 3) * 8)
    return slots.astype(jnp.int32), owners.astype(jnp.int32)


def permute_gather(shard):
    line = jnp.stack([shard] + [exchange(shard, step) for step in line_steps])
    plane = jnp.concatenate([line] + [exchange(line, step) for step in plane_steps])
    return jnp.concatenate([plane, exchange(plane, core_step[0])])


def pair_sum(keep, send):
    return (keep.astype(f32) + exchange(send, core_step[0]).astype(f32)).astype(bf16)


def permute_scatter(pair):
    parts = [pair[4 * j : 4 * j + 4] for j in range(4)]
    total = parts[0].astype(f32)
    for part, step in zip(parts[1:], plane_steps):
        total = total + exchange(part, step).astype(f32)
    total = total.astype(bf16)
    final = total[0].astype(f32)
    for k, step in enumerate(line_steps):
        final = final + exchange(total[k + 1], step).astype(f32)
    return final


def permute_sum(values):
    values = values + exchange(values, core_step[0])
    for steps in (plane_steps, line_steps):
        first, second, third = (exchange(values, step) for step in steps)
        values = (values + first) + (second + third)
    return values


def split_share(share, shapes, devices):
    parts = []
    offset = 0
    for rows, columns in shapes:
        size = rows // devices * (columns // lane_tile)
        parts.append(unpack(share[offset : offset + size], rows // devices, columns).astype(f32))
        offset += size
    return parts


def on_device(
    devices,
    direct,
    targets,
    memory,
    mem_lengths,
    buckets,
    cotangent,
    gain_self,
    gain_cross,
    gain_feed,
    self_query,
    self_key,
    self_value,
    self_output,
    cross_query,
    cross_key,
    cross_value,
    cross_output,
    gate_weight,
    up_weight,
    down_weight,
    bias_table,
):
    batch, target_len, width = targets.shape
    bucket_count, head_count = bias_table.shape
    row_count = batch * target_len
    groups = width // group_rows
    square = (width, width)
    feed_width = gate_weight.shape[1]
    feed_shapes = [(width, feed_width), (width, feed_width), (feed_width, width)]

    own_gains = jnp.stack([gain_self, gain_cross, gain_feed])
    if direct:
        slots, owners = slot_tables()
        extra = jnp.pad(own_gains.reshape(1, -1), ((0, 15), (0, lane_tile - own_gains.size)))
        packed_memory = permute_gather(
            jnp.concatenate([pack(cross_key), pack(cross_value), extra], axis=0)
        )
        hot = (slots[:, None] == jnp.arange(groups)[None, :]).astype(bf16)
        gains = (
            dot(hot, packed_memory[:, -16, : own_gains.size])
            .reshape(groups, 3, group_rows)
            .transpose(1, 0, 2)
            .reshape(3, width)
        )
    else:
        slots = owners = jnp.arange(groups, dtype=jnp.int32)
        packed_memory = gather([cross_key, cross_value], [square] * 2, groups, devices)
        gains = lax.all_gather(own_gains, axes, axis=1, tiled=True).astype(f32)
    packed_self = gather(
        [self_query, self_key, self_value, self_output, cross_query, cross_output],
        [square] * 6,
        groups,
        devices,
    )
    packed_feed = gather([gate_weight, up_weight, down_weight], feed_shapes, groups, devices)

    pad = pair_width - target_len
    bucket_hot = (
        buckets[:, :, None] == lax.broadcasted_iota(jnp.int32, (1, 1, bucket_count), 2)
    ).reshape(target_len * target_len, bucket_count)
    bias = (
        dot(bucket_hot.astype(bf16), bias_table)
        .reshape(target_len, target_len, head_count)
        .transpose(2, 0, 1)
    )
    causal = lax.broadcasted_iota(jnp.int32, (target_len, target_len), 1) <= lax.broadcasted_iota(
        jnp.int32, (target_len, target_len), 0
    )
    bias = jnp.where(causal, bias, masked_out)
    bias = jnp.pad(bias, ((0, 0), (0, 0), (0, pad)), constant_values=masked_out)
    bias = (
        bias.reshape(head_count // 2, 2, target_len, pair_width)
        .transpose(0, 2, 1, 3)
        .reshape(head_count // 2, target_len, 2 * pair_width)
    )
    wide_buckets = jnp.pad(buckets, ((0, 0), (0, pad)), constant_values=-1)
    target_rows = targets.reshape(row_count, width)
    cot_rows = cotangent.reshape(row_count, width)

    mem_keys, mem_values, memory_weight = project_memory(
        mem_lengths, slots, memory, packed_memory
    )
    normed_one, queries, key_rows, value_rows, self_context, after_self, normed_two, side = (
        self_forward(target_len, target_rows, packed_self, bias, gains[0:1], gains[1:2])
    )
    cross_context, weights = cross_forward(mem_lengths, side, mem_keys, mem_values, head_count)
    outputs, grad_after_cross, grad_context, grad_gain_feed, feed_grads = feed_both(
        after_self, cross_context, cot_rows, gains[2:3], packed_self, packed_feed
    )
    share_gate, share_up, share_down, share_cross_output = scatter(
        feed_grads, feed_shapes + [square], groups, devices
    )
    grad_side, grad_mem_keys, grad_mem_values = cross_backward(
        mem_lengths, grad_context, cross_context, side, mem_keys, mem_values, weights
    )
    target_grad, self_keep, self_send, grad_gains, table_parts = self_backward(
        target_len,
        bucket_count,
        owners,
        (
            grad_side,
            after_self,
            grad_after_cross,
            normed_two,
            normed_one,
            queries,
            key_rows,
            value_rows,
            self_context,
            target_rows,
            packed_self,
            bias,
            wide_buckets,
            gains[0:1],
            gains[1:2],
        ),
    )
    grad_mem_keys, grad_mem_values, self_keep = lax.optimization_barrier(
        (grad_mem_keys, grad_mem_values, self_keep)
    )
    memory_keep, memory_send = memory_weight_grads(
        mem_lengths, owners, memory, grad_mem_keys, grad_mem_values
    )
    table_part = (
        table_parts.reshape(bucket_count, head_count, pair_width).sum(axis=-1).reshape(-1)
    )
    small = jnp.concatenate(
        [grad_gains[0], grad_gains[1], grad_gain_feed[0], table_part], axis=0
    )
    if direct:
        self_pair = pair_sum(self_keep, self_send)
        memory_weight, self_pair = lax.optimization_barrier((memory_weight, self_pair))
    memory_grad = memory_gradient(mem_lengths, grad_mem_keys, grad_mem_values, memory_weight)
    if direct:
        self_shares = permute_scatter(self_pair)
        memory_grad, memory_keep, memory_send, small = lax.optimization_barrier(
            (memory_grad, memory_keep, memory_send, small)
        )
        memory_shares = permute_scatter(pair_sum(memory_keep, memory_send))
        share_cross_key, share_cross_value = split_share(memory_shares, [square] * 2, devices)
        share_query, share_key, share_value, share_output, share_cross_query = split_share(
            self_shares, [square] * 5, devices
        )
        small = permute_sum(small)
    else:
        share_cross_key, share_cross_value = scatter(
            jnp.concatenate([memory_keep, memory_send]), [square] * 2, groups, devices
        )
        share_query, share_key, share_value, share_output, share_cross_query = scatter(
            jnp.concatenate([self_keep, self_send]), [square] * 5, groups, devices
        )
        small = jnp.sum(lax.all_gather(small, axes, axis=0, tiled=False), axis=0)
    table_grad = small[3 * width :].reshape(bucket_count, head_count)
    own = width // devices
    place = lax.axis_index(axes) * own

    def own_gain(index):
        return lax.dynamic_slice(small, (index * width + place,), (own,))

    return (
        outputs.reshape(targets.shape),
        target_grad.reshape(targets.shape),
        memory_grad,
        own_gain(0),
        own_gain(1),
        own_gain(2),
        share_query,
        share_key,
        share_value,
        share_output,
        share_cross_query,
        share_cross_key,
        share_cross_value,
        share_cross_output,
        share_gate,
        share_up,
        share_down,
        table_grad,
    )


def solution(mesh):
    devices = mesh.shape["dp"] * mesh.shape["seq"]
    direct = mesh.shape["dp"] == 16 and mesh.shape["seq"] == 2
    rows = P(axes, None, None)
    flat = P(axes)
    weight = P(axes, None)

    def body(*arguments):
        return on_device(devices, direct, *arguments)

    return jax.shard_map(
        body,
        mesh=mesh,
        in_specs=(rows, rows, flat, P(), rows, flat, flat, flat) + (weight,) * 11 + (P(),),
        out_specs=(rows, rows, rows, flat, flat, flat) + (weight,) * 11 + (P(),),
        check_vma=False,
    )
```

```python
import math

import jax
import jax.numpy as jnp
from jax import lax
from jax.experimental import pallas as pl
from jax.experimental.pallas import tpu as pltpu
from jax.sharding import PartitionSpec as P

epsilon = 1e-06
masked_out = -1e30
bf16 = jnp.bfloat16
f32 = jnp.float32
axes = ("dp", "seq")
lane_tile = 256
group_rows = 24
pair_width = 128
pair_group = 3
NN = (((1,), (0,)), ((), ()))
NT = (((1,), (1,)), ((), ()))
TN = (((0,), (0,)), ((), ()))
gelu_scale = math.sqrt(2.0 / math.pi)
gelu_cubic = 0.044715


def dot(left_side, right_side, dims=NN):
    return lax.dot_general(left_side, right_side, dims, preferred_element_type=f32)


def params():
    return pltpu.CompilerParams(vmem_limit_bytes=60 * 1024 * 1024)


def cost(flops, size, exps=0):
    return pl.CostEstimate(
        flops=int(flops), bytes_accessed=int(size), transcendentals=int(exps)
    )


def column_tile(packed_ref, index):
    tile = packed_ref[:, index * group_rows : (index + 1) * group_rows, :]
    return tile.reshape(tile.shape[0] * group_rows, lane_tile)


def lane_halves(rows):
    lanes = lax.broadcasted_iota(jnp.int32, (rows, pair_width), 1)
    return lanes < pair_width // 2


def project(rows, packed_ref, base, tiles):
    return [dot(rows, column_tile(packed_ref, base + t)) for t in range(tiles)]


def through(rows, packed_ref, base, tiles):
    total = None
    for t in range(tiles):
        part = dot(
            rows[:, t * lane_tile : (t + 1) * lane_tile], column_tile(packed_ref, base + t), NT
        )
        total = part if total is None else total + part
    return total


def assemble(owners, near_ref, far_ref, weight_ref):
    half = near_ref.shape[0]
    for offset, packed_ref in ((0, near_ref), (half, far_ref)):

        def place(pair, carry):
            slot = (pair >> 2) * 8 + (pair & 3)
            owner = owners[offset + slot]
            odd = owner & 1
            rows = pl.ds(pl.multiple_of((owner >> 1) * (2 * group_rows), 16), 2 * group_rows)
            for t in range(weight_ref.shape[1] // lane_tile):
                part = slice(t * group_rows, (t + 1) * group_rows)
                weight_ref[rows, t * lane_tile : (t + 1) * lane_tile] = jnp.concatenate(
                    [
                        packed_ref[slot + 4 * odd, part, :],
                        packed_ref[slot + 4 - 4 * odd, part, :],
                    ],
                    axis=0,
                )
            return carry

        lax.fori_loop(0, half // 2, place, 0)


def put_slots(owners, keep_ref, send_ref, stage_ref, extra=None):
    half = keep_ref.shape[0]
    tiles = stage_ref.shape[1] // lane_tile

    def place(slot, carry):
        for offset, out_ref in ((0, keep_ref), (half, send_ref)):
            owner = owners[slot + offset]
            rows = pl.ds(pl.multiple_of(owner * group_rows, 8), group_rows)
            parts = [
                stage_ref[rows, t * lane_tile : (t + 1) * lane_tile] for t in range(tiles)
            ]
            if extra is not None:
                parts.append(extra(owner))
            for t in range(0, len(parts), 2):
                both = jnp.concatenate(parts[t : t + 2], axis=0).astype(bf16)
                start = t * group_rows
                out_ref[slot, start : start + both.shape[0], :] = both
        return carry

    lax.fori_loop(0, half, place, 0)


def norm_scale(values):
    return lax.rsqrt(jnp.mean(values * values, axis=-1, keepdims=True) + epsilon)


def norm_pullback(values, gain_row, grad_in):
    inverse = norm_scale(values)
    weighted = grad_in * gain_row
    inner = jnp.mean(weighted * values, axis=-1, keepdims=True)
    grad_values = inverse * weighted - values * (inverse * inverse * inverse * inner)
    grad_gain = jnp.sum(grad_in * values * inverse, axis=0, keepdims=True)
    return grad_values, grad_gain


def memory_kernel(
    lengths, owners, memory_ref, near_ref, far_ref, keys_ref, values_ref, weight_ref
):
    seq = pl.program_id(0)
    memory_len = memory_ref.shape[1]

    @pl.when(seq == 0)
    def _():
        assemble(owners, near_ref, far_ref, weight_ref)

    def fill(count):
        rows = memory_ref[0, :count, :]
        for base, out_ref in ((0, keys_ref), (3, values_ref)):
            for t in range(3):
                out_ref[0, :count, t * lane_tile : (t + 1) * lane_tile] = dot(
                    rows, weight_ref[:, (base + t) * lane_tile : (base + t + 1) * lane_tile]
                ).astype(bf16)

    @pl.when(lengths[seq] > memory_len // 2)
    def _():
        fill(memory_len)

    @pl.when(lengths[seq] <= memory_len // 2)
    def _():
        fill(memory_len // 2)


def project_memory(mem_lengths, owners, memory, near, far):
    batch, memory_len, width = memory.shape
    block = pl.BlockSpec((1, memory_len, width), lambda b, n, s: (b, 0, 0))
    return pl.pallas_call(
        memory_kernel,
        out_shape=[jax.ShapeDtypeStruct(memory.shape, bf16)] * 2
        + [jax.ShapeDtypeStruct((width, 2 * width), bf16)],
        grid_spec=pltpu.PrefetchScalarGridSpec(
            num_scalar_prefetch=2,
            grid=(batch,),
            in_specs=[block] + [pl.BlockSpec(near.shape, lambda b, n, s: (0, 0, 0))] * 2,
            out_specs=[block, block, pl.BlockSpec((width, 2 * width), lambda b, n, s: (0, 0))],
        ),
        compiler_params=params(),
        cost_estimate=cost(4 * memory.size * width, 6 * memory.size),
        name="memory_project",
    )(mem_lengths, owners, memory, near, far)


def stacked_pair(rows, half, pad):
    zero = jnp.zeros_like(rows)
    gap = jnp.zeros((pad, pair_width), rows.dtype)
    return jnp.concatenate(
        [jnp.where(half, rows, zero), gap, jnp.where(half, zero, rows), gap], axis=0
    )


def pair_softmax(scores):
    parts = []
    for h in range(2):
        one = scores[:, h * pair_width : (h + 1) * pair_width]
        terms = jnp.exp(one - jnp.max(one, axis=-1, keepdims=True))
        parts.append(terms * (1.0 / jnp.sum(terms, axis=-1, keepdims=True)))
    return parts


def self_forward_kernel(
    target_len,
    owners,
    targets_ref,
    near_ref,
    far_ref,
    bias_ref,
    gain_self_ref,
    gain_cross_ref,
    normed_one_ref,
    queries_ref,
    keys_ref,
    values_ref,
    context_ref,
    after_ref,
    normed_two_ref,
    side_ref,
    weight_ref,
):
    width = targets_ref.shape[1]

    def weight(index):
        return weight_ref[:, index * width : (index + 1) * width]

    assemble(owners, near_ref, far_ref, weight_ref)
    inputs = targets_ref[...].astype(f32)
    normed_one = (inputs * norm_scale(inputs) * gain_self_ref[...]).astype(bf16)
    normed_one_ref[...] = normed_one
    for index, out_ref in ((0, queries_ref), (1, keys_ref), (2, values_ref)):
        out_ref[...] = dot(normed_one, weight(index)).astype(bf16)
    half = lane_halves(target_len)
    pad = pair_width - target_len
    pairs = bias_ref.shape[0]
    columns = [slice(p * pair_width, (p + 1) * pair_width) for p in range(pairs)]

    def attend(seq, carry):
        rows = pl.ds(pl.multiple_of(seq * target_len, 32), target_len)
        scores = [
            dot(queries_ref[rows, cols], stacked_pair(keys_ref[rows, cols], half, pad), NT)
            + bias_ref[p]
            for p, cols in enumerate(columns)
        ]
        probs = [
            jnp.concatenate(pair_softmax(score), axis=1).astype(bf16) for score in scores
        ]
        for p, cols in enumerate(columns):
            value_stack = stacked_pair(values_ref[rows, cols], half, pad)
            context_ref[rows, cols] = dot(probs[p], value_stack).astype(bf16)
        return carry

    lax.fori_loop(0, targets_ref.shape[0] // target_len, attend, 0)
    after = inputs + dot(context_ref[...], weight(3))
    after_ref[...] = after
    normed_two = (after * norm_scale(after) * gain_cross_ref[...]).astype(bf16)
    normed_two_ref[...] = normed_two
    side_ref[...] = dot(normed_two, weight(4)).astype(bf16)


def self_forward(target_len, owners, targets, near, far, bias, gain_self, gain_cross):
    width = targets.shape[1]
    whole = pl.BlockSpec(memory_space=pltpu.VMEM)
    low = jax.ShapeDtypeStruct(targets.shape, bf16)
    wide = jax.ShapeDtypeStruct(targets.shape, f32)

    def body(*refs):
        self_forward_kernel(target_len, *refs)

    return pl.pallas_call(
        body,
        out_shape=[low, low, low, low, low, wide, low, low]
        + [jax.ShapeDtypeStruct((width, 5 * width), bf16)],
        in_specs=[pl.BlockSpec(memory_space=pltpu.SMEM)] + [whole] * 6,
        compiler_params=params(),
        cost_estimate=cost(20 * targets.size * targets.shape[1], 16 * targets.size),
        name="self_forward",
    )(owners, targets, near, far, bias, gain_self, gain_cross)


def masked_stack(rows, half):
    zero = jnp.zeros_like(rows)
    return jnp.concatenate([jnp.where(half, rows, zero), jnp.where(half, zero, rows)], axis=0)


def cross_forward_kernel(lengths, side_ref, keys_ref, values_ref, context_ref, weights_ref):
    seq = pl.program_id(0)
    target_len, width = side_ref.shape
    memory_len = keys_ref.shape[1]
    half = lane_halves(target_len)

    def attend(count):
        for p in range(width // pair_width):
            cols = slice(p * pair_width, (p + 1) * pair_width)
            stack = masked_stack(side_ref[:, cols], half)
            scores = dot(stack, keys_ref[0, :count, cols], NT)
            terms = jnp.exp(scores - jnp.max(scores, axis=-1, keepdims=True))
            scale = 1.0 / jnp.sum(terms, axis=-1, keepdims=True)
            weights = (terms * scale).astype(bf16)
            weights_ref[0, 2 * target_len * p : 2 * target_len * (p + 1), :count] = weights
            both = dot(weights, values_ref[0, :count, cols])
            context_ref[:, cols] = jnp.where(half, both[:target_len], both[target_len:]).astype(
                bf16
            )

    @pl.when(lengths[seq] > memory_len // 2)
    def _():
        attend(memory_len)

    @pl.when(lengths[seq] <= memory_len // 2)
    def _():
        attend(memory_len // 2)


def cross_forward(mem_lengths, side, mem_keys, mem_values, head_count):
    batch, memory_len, width = mem_keys.shape
    target_len = side.shape[0] // batch
    rows = pl.BlockSpec((target_len, width), lambda b, n: (b, 0))
    memory = pl.BlockSpec((1, memory_len, width), lambda b, n: (b, 0, 0))
    weights = pl.BlockSpec((1, head_count * target_len, memory_len), lambda b, n: (b, 0, 0))
    return pl.pallas_call(
        cross_forward_kernel,
        out_shape=[
            jax.ShapeDtypeStruct(side.shape, bf16),
            jax.ShapeDtypeStruct((batch, head_count * target_len, memory_len), bf16),
        ],
        grid_spec=pltpu.PrefetchScalarGridSpec(
            num_scalar_prefetch=1,
            grid=(batch,),
            in_specs=[rows, memory, memory],
            out_specs=[rows, weights],
        ),
        compiler_params=params(),
        cost_estimate=cost(16 * side.size * memory_len, 6 * mem_keys.size, batch * head_count * target_len * memory_len),
        name="cross_forward",
    )(mem_lengths, side, mem_keys, mem_values)


def feed_kernel(
    after_ref,
    context_ref,
    cot_ref,
    gain_ref,
    side_output_ref,
    gate_ref,
    up_ref,
    down_ref,
    outputs_ref,
    grad_after_ref,
    grad_context_ref,
    grad_gain_ref,
    packed_ref,
    after_cross_ref,
    normed_ref,
    out_total_ref,
    grad_normed_ref,
):
    step = pl.program_id(0)
    steps = pl.num_programs(0)

    @pl.when(step == 0)
    def _():
        after_cross = after_ref[...] + jnp.concatenate(
            project(context_ref[...], side_output_ref, 0, 3), axis=1
        )
        after_cross_ref[...] = after_cross
        normed_ref[...] = (after_cross * norm_scale(after_cross) * gain_ref[...]).astype(bf16)
        out_total_ref[...] = after_cross
        grad_normed_ref[...] = jnp.zeros_like(grad_normed_ref)

    normed = normed_ref[...]
    cot = cot_ref[...]
    gate_weight = column_tile(gate_ref, 0)
    up_weight = column_tile(up_ref, 0)
    share = down_ref.shape[1] // 3
    owners = down_ref.shape[0]
    down_weight = jnp.concatenate(
        [
            down_ref[:, c * share : (c + 1) * share, :].reshape(owners * share, lane_tile)
            for c in range(3)
        ],
        axis=1,
    )
    gate = dot(normed, gate_weight)
    up = dot(normed, up_weight)
    grad_hidden = dot(cot, down_weight, NT)
    square = gate * gate
    tanh = jnp.tanh(gelu_scale * (gate + gelu_cubic * (square * gate)))
    half_sum = 0.5 * (1.0 + tanh)
    active = gate * half_sum
    slope = half_sum + 0.5 * gate * (1.0 - tanh * tanh) * (
        gelu_scale * (1.0 + 3.0 * gelu_cubic * square)
    )
    hidden = (active * up).astype(bf16)
    grad_gate = (grad_hidden * up * slope).astype(bf16)
    grad_up = (grad_hidden * active).astype(bf16)
    out_total_ref[...] += dot(hidden, down_weight)
    grad_normed_ref[...] += dot(grad_gate, gate_weight, NT) + dot(grad_up, up_weight, NT)
    groups = packed_ref.shape[0]

    def put(base, value):
        packed_ref[:, pl.ds(base + step * group_rows, group_rows), :] = value.reshape(
            groups, group_rows, lane_tile
        ).astype(bf16)

    put(0, dot(normed, grad_gate, TN))
    put(steps * group_rows, dot(normed, grad_up, TN))
    down_base = 2 * steps * group_rows
    for c in range(3):
        part = dot(hidden, cot[:, c * lane_tile : (c + 1) * lane_tile], TN)
        packed_ref[
            pl.ds(step * owners, owners), down_base + c * share : down_base + (c + 1) * share, :
        ] = part.reshape(owners, share, lane_tile).astype(bf16)

    @pl.when(step == steps - 1)
    def _():
        outputs_ref[...] = out_total_ref[...].astype(bf16)
        grad_in, grad_gain = norm_pullback(
            after_cross_ref[...], gain_ref[...], grad_normed_ref[...]
        )
        grad_gain_ref[...] = grad_gain
        grad_after = cot_ref[...].astype(f32) + grad_in
        grad_after_ref[...] = grad_after
        low = grad_after.astype(bf16)
        for c in range(3):
            cols = slice(c * lane_tile, (c + 1) * lane_tile)
            start = 3 * down_base // 2 + c * group_rows
            packed_ref[:, start : start + group_rows, :] = (
                dot(context_ref[...], low[:, cols], TN)
                .reshape(groups, group_rows, lane_tile)
                .astype(bf16)
            )
        grad_context_ref[...] = through(low, side_output_ref, 0, 3).astype(bf16)


def feed_both(after_self, context, cotangent, gain, packed_feed):
    rows, width = context.shape
    groups, feed_rows, _ = packed_feed.shape
    steps = feed_rows // (3 * group_rows) - 1
    owners = groups // steps
    whole = lambda f: (0, 0)
    full = pl.BlockSpec((rows, width), whole)
    tile = (groups, group_rows, lane_tile)
    return pl.pallas_call(
        feed_kernel,
        out_shape=[
            jax.ShapeDtypeStruct((rows, width), bf16),
            jax.ShapeDtypeStruct((rows, width), f32),
            jax.ShapeDtypeStruct((rows, width), bf16),
            jax.ShapeDtypeStruct((1, width), f32),
            jax.ShapeDtypeStruct((groups, feed_rows, lane_tile), bf16),
        ],
        grid=(steps,),
        in_specs=[
            full,
            full,
            full,
            pl.BlockSpec((1, width), whole),
            pl.BlockSpec((groups, 3 * group_rows, lane_tile), lambda f: (0, steps, 0)),
            pl.BlockSpec(tile, lambda f: (0, f, 0)),
            pl.BlockSpec(tile, lambda f: (0, steps + f, 0)),
            pl.BlockSpec((owners, steps * group_rows, lane_tile), lambda f: (f, 2, 0)),
        ],
        out_specs=[
            full,
            full,
            full,
            pl.BlockSpec((1, width), whole),
            pl.BlockSpec((groups, feed_rows, lane_tile), lambda f: (0, 0, 0)),
        ],
        scratch_shapes=[
            pltpu.VMEM((rows, width), f32),
            pltpu.VMEM((rows, width), bf16),
            pltpu.VMEM((rows, width), f32),
            pltpu.VMEM((rows, width), f32),
        ],
        compiler_params=params(),
        cost_estimate=cost(18 * rows * width * steps * lane_tile, 30 * rows * width),
        name="feed_both",
    )(after_self, context, cotangent, gain, packed_feed, packed_feed, packed_feed, packed_feed)


def cross_backward_kernel(
    lengths,
    grad_ref,
    context_ref,
    side_ref,
    keys_ref,
    values_ref,
    weights_ref,
    grad_side_ref,
    grad_keys_ref,
    grad_values_ref,
):
    seq = pl.program_id(0)
    target_len, width = side_ref.shape
    memory_len = keys_ref.shape[1]
    half = lane_halves(target_len)

    def attend(count):
        for p in range(width // pair_width):
            cols = slice(p * pair_width, (p + 1) * pair_width)
            grad_rows = grad_ref[:, cols]
            grad_stack = masked_stack(grad_rows, half)
            query_stack = masked_stack(side_ref[:, cols], half)
            product = grad_rows.astype(f32) * context_ref[:, cols].astype(f32)
            inner = jnp.sum(masked_stack(product, half), axis=-1, keepdims=True)
            weights = weights_ref[0, 2 * target_len * p : 2 * target_len * (p + 1), :count]
            grad_probs = dot(grad_stack, values_ref[0, :count, cols], NT)
            grad_scores = (weights.astype(f32) * (grad_probs - inner)).astype(bf16)
            both = dot(grad_scores, keys_ref[0, :count, cols])
            grad_side_ref[:, cols] = jnp.where(half, both[:target_len], both[target_len:]).astype(
                bf16
            )
            grad_keys_ref[0, cols, :count] = dot(query_stack, grad_scores, TN).astype(bf16)
            grad_values_ref[0, cols, :count] = dot(grad_stack, weights, TN).astype(bf16)

    @pl.when(lengths[seq] > memory_len // 2)
    def _():
        attend(memory_len)

    @pl.when(lengths[seq] <= memory_len // 2)
    def _():
        attend(memory_len // 2)


def cross_backward(mem_lengths, grad_context, context, side, mem_keys, mem_values, weights):
    batch, memory_len, width = mem_keys.shape
    target_len = side.shape[0] // batch
    rows = pl.BlockSpec((target_len, width), lambda b, n: (b, 0))
    memory = pl.BlockSpec((1, memory_len, width), lambda b, n: (b, 0, 0))
    turned = pl.BlockSpec((1, width, memory_len), lambda b, n: (b, 0, 0))
    return pl.pallas_call(
        cross_backward_kernel,
        out_shape=[jax.ShapeDtypeStruct(side.shape, bf16)]
        + [jax.ShapeDtypeStruct((batch, width, memory_len), bf16)] * 2,
        grid_spec=pltpu.PrefetchScalarGridSpec(
            num_scalar_prefetch=1,
            grid=(batch,),
            in_specs=[
                rows,
                rows,
                rows,
                memory,
                memory,
                pl.BlockSpec((1,) + weights.shape[1:], lambda b, n: (b, 0, 0)),
            ],
            out_specs=[rows, turned, turned],
        ),
        compiler_params=params(),
        cost_estimate=cost(32 * side.size * memory_len, 10 * mem_keys.size),
        name="cross_backward",
    )(mem_lengths, grad_context, context, side, mem_keys, mem_values, weights)


def memory_weight_kernel(
    lengths,
    owners,
    memory_ref,
    grad_keys_ref,
    grad_values_ref,
    keep_ref,
    send_ref,
    key_total_ref,
    value_total_ref,
    stage_ref,
):
    seq = pl.program_id(0)
    memory_len = memory_ref.shape[1]

    @pl.when(seq == 0)
    def _():
        key_total_ref[...] = jnp.zeros_like(key_total_ref)
        value_total_ref[...] = jnp.zeros_like(value_total_ref)

    def add(count):
        rows = memory_ref[0, :count, :]
        key_total_ref[...] += dot(grad_keys_ref[0, :, :count], rows)
        value_total_ref[...] += dot(grad_values_ref[0, :, :count], rows)

    @pl.when(lengths[seq] > memory_len // 2)
    def _():
        add(memory_len)

    @pl.when(lengths[seq] <= memory_len // 2)
    def _():
        add(memory_len // 2)

    @pl.when(seq == pl.num_programs(0) - 1)
    def _():
        width = key_total_ref.shape[0]
        for base, total_ref in ((0, key_total_ref), (width, value_total_ref)):
            for start in range(0, width, lane_tile):
                stage_ref[:, base + start : base + start + lane_tile] = jnp.transpose(
                    total_ref[start : start + lane_tile, :]
                )
        put_slots(owners, keep_ref, send_ref, stage_ref)


def memory_weight_grads(mem_lengths, owners, memory, grad_keys, grad_values):
    batch, memory_len, width = memory.shape
    block = pl.BlockSpec((1, memory_len, width), lambda b, n, o: (b, 0, 0))
    turned = pl.BlockSpec((1, width, memory_len), lambda b, n, o: (b, 0, 0))
    half = (owners.shape[0] // 2, 2 * width // lane_tile * group_rows, lane_tile)
    return pl.pallas_call(
        memory_weight_kernel,
        out_shape=[jax.ShapeDtypeStruct(half, bf16)] * 2,
        grid_spec=pltpu.PrefetchScalarGridSpec(
            num_scalar_prefetch=2,
            grid=(batch,),
            in_specs=[block, turned, turned],
            out_specs=[pl.BlockSpec(half, lambda b, n, o: (0, 0, 0))] * 2,
            scratch_shapes=[pltpu.VMEM((width, width), f32)] * 2
            + [pltpu.VMEM((width, 2 * width), f32)],
        ),
        compiler_params=params(),
        cost_estimate=cost(4 * memory.size * width, 6 * memory.size),
        name="memory_weight_grads",
    )(mem_lengths, owners, memory, grad_keys, grad_values)


def memory_grad_kernel(
    lengths, grad_keys_ref, grad_values_ref, weight_ref, out_ref, key_turned_ref, value_turned_ref
):
    seq = pl.program_id(0)
    memory_len = out_ref.shape[1]

    @pl.when(seq == 0)
    def _():
        for base, turned_ref in ((0, key_turned_ref), (3, value_turned_ref)):
            for t in range(3):
                turned_ref[t * lane_tile : (t + 1) * lane_tile, :] = jnp.transpose(
                    weight_ref[:, (base + t) * lane_tile : (base + t + 1) * lane_tile]
                )

    def fill(count):
        out_ref[0, :count, :] = (
            dot(grad_keys_ref[0, :, :count], key_turned_ref[...], TN)
            + dot(grad_values_ref[0, :, :count], value_turned_ref[...], TN)
        ).astype(bf16)

    @pl.when(lengths[seq] > memory_len // 2)
    def _():
        fill(memory_len)

    @pl.when(lengths[seq] <= memory_len // 2)
    def _():
        fill(memory_len // 2)
        out_ref[0, memory_len // 2 :, :] = jnp.zeros_like(out_ref[0, memory_len // 2 :, :])


def memory_gradient(mem_lengths, grad_keys, grad_values, weight):
    batch, width, memory_len = grad_keys.shape
    turned = pl.BlockSpec((1, width, memory_len), lambda b, n: (b, 0, 0))
    return pl.pallas_call(
        memory_grad_kernel,
        out_shape=jax.ShapeDtypeStruct((batch, memory_len, width), bf16),
        grid_spec=pltpu.PrefetchScalarGridSpec(
            num_scalar_prefetch=1,
            grid=(batch,),
            in_specs=[turned, turned, pl.BlockSpec(weight.shape, lambda b, n: (0, 0))],
            out_specs=pl.BlockSpec((1, memory_len, width), lambda b, n: (b, 0, 0)),
            scratch_shapes=[pltpu.VMEM((width, width), bf16)] * 2,
        ),
        compiler_params=params(),
        cost_estimate=cost(4 * grad_keys.size * width, 6 * grad_keys.size),
        name="memory_grad",
    )(mem_lengths, grad_keys, grad_values, weight)


def self_output_kernel(
    owners,
    grad_side_ref,
    after_ref,
    grad_after_ref,
    normed_two_ref,
    context_ref,
    weight_ref,
    gain_cross_ref,
    grad_total_ref,
    grad_context_ref,
    grad_gain_ref,
    keep_ref,
    send_ref,
    stage_ref,
):
    width = after_ref.shape[1]
    grad_side = grad_side_ref[...]
    grad_normed = dot(grad_side, weight_ref[:, 4 * width :], NT)
    grad_in, grad_gain = norm_pullback(after_ref[...], gain_cross_ref[...], grad_normed)
    grad_gain_ref[...] = grad_gain
    grad_total = grad_after_ref[...] + grad_in
    grad_total_ref[...] = grad_total
    low = grad_total.astype(bf16)
    stage_ref[:, :width] = dot(context_ref[...], low, TN)
    stage_ref[:, width:] = dot(normed_two_ref[...], grad_side, TN)
    grad_context_ref[...] = dot(low, weight_ref[:, 3 * width : 4 * width], NT).astype(bf16)
    put_slots(owners, keep_ref, send_ref, stage_ref)


def self_output_backward(
    owners, grad_side, after, grad_after, normed_two, context, weight, gain_cross
):
    rows, width = after.shape
    half = (owners.shape[0] // 2, 2 * width // lane_tile * group_rows, lane_tile)
    whole = pl.BlockSpec(memory_space=pltpu.VMEM)
    return pl.pallas_call(
        self_output_kernel,
        out_shape=[
            jax.ShapeDtypeStruct((rows, width), f32),
            jax.ShapeDtypeStruct((rows, width), bf16),
            jax.ShapeDtypeStruct((1, width), f32),
            jax.ShapeDtypeStruct(half, bf16),
            jax.ShapeDtypeStruct(half, bf16),
        ],
        in_specs=[pl.BlockSpec(memory_space=pltpu.SMEM)] + [whole] * 7,
        scratch_shapes=[pltpu.VMEM((width, 2 * width), f32)],
        compiler_params=params(),
        cost_estimate=cost(8 * after.size * width, 20 * after.size),
        name="self_output_backward",
    )(owners, grad_side, after, grad_after, normed_two, context, weight, gain_cross)


def self_backward_kernel(
    target_len,
    bucket_count,
    owners,
    grad_context_ref,
    grad_total_ref,
    normed_one_ref,
    queries_ref,
    keys_ref,
    values_ref,
    targets_ref,
    weight_ref,
    bias_ref,
    buckets_ref,
    gain_self_ref,
    grad_gain_cross_ref,
    grad_gain_feed_ref,
    target_grad_ref,
    keep_ref,
    send_ref,
    grad_queries_ref,
    grad_keys_ref,
    grad_values_ref,
    score_total_ref,
    stage_ref,
    table_ref,
    gains_ref,
):
    width = targets_ref.shape[1]
    half = lane_halves(target_len)
    pad = pair_width - target_len
    pairs = bias_ref.shape[0]
    columns = [slice(p * pair_width, (p + 1) * pair_width) for p in range(pairs)]
    score_total_ref[...] = jnp.zeros_like(score_total_ref)

    def pick(values):
        return jnp.where(
            half, values[:target_len], values[pair_width : pair_width + target_len]
        ).astype(bf16)

    def attend(seq, carry):
        rows = pl.ds(pl.multiple_of(seq * target_len, 32), target_len)
        for first in range(0, pairs, pair_group):
            chosen = range(first, first + pair_group)
            key_stacks = [stacked_pair(keys_ref[rows, columns[p]], half, pad) for p in chosen]
            scores = [
                dot(queries_ref[rows, columns[p]], stack, NT) + bias_ref[p]
                for p, stack in zip(chosen, key_stacks)
            ]
            grad_probs = [
                dot(
                    grad_context_ref[rows, columns[p]],
                    stacked_pair(values_ref[rows, columns[p]], half, pad),
                    NT,
                )
                for p in chosen
            ]
            probs = [pair_softmax(score) for score in scores]
            grad_scores = []
            for prob, grad_prob in zip(probs, grad_probs):
                parts = []
                for h in range(2):
                    one = grad_prob[:, h * pair_width : (h + 1) * pair_width]
                    inner = jnp.sum(one * prob[h], axis=-1, keepdims=True)
                    parts.append(prob[h] * (one - inner))
                grad_scores.append(jnp.concatenate(parts, axis=1).astype(bf16))
            for p, stack, prob, grad_score in zip(chosen, key_stacks, probs, grad_scores):
                cols = columns[p]
                weights = jnp.concatenate(prob, axis=1).astype(bf16)
                score_total_ref[p] += grad_score.astype(f32)
                grad_queries_ref[rows, cols] = dot(grad_score, stack).astype(bf16)
                grad_keys_ref[rows, cols] = pick(dot(grad_score, queries_ref[rows, cols], TN))
                grad_values_ref[rows, cols] = pick(
                    dot(weights, grad_context_ref[rows, cols], TN)
                )
        return carry

    lax.fori_loop(0, targets_ref.shape[0] // target_len, attend, 0)
    buckets = buckets_ref[...]
    both = jnp.concatenate([buckets, buckets], axis=1)

    def count(bucket, carry):
        chosen = both == bucket
        for p in range(pairs):
            table_ref[pl.ds(p * bucket_count + bucket, 1), :] = jnp.sum(
                jnp.where(chosen, score_total_ref[p], 0.0), axis=0, keepdims=True
            )
        return carry

    lax.fori_loop(0, bucket_count, count, 0)
    lanes = lax.broadcasted_iota(jnp.int32, (8, lane_tile), 1) >> 7
    head = (lanes == lax.broadcasted_iota(jnp.int32, (8, lane_tile), 0)).astype(f32)
    table = lax.dot_general(
        head, table_ref[...], NT, precision=lax.Precision.HIGHEST, preferred_element_type=f32
    )

    normed_one = normed_one_ref[...]
    total = None
    for index, grad_ref in enumerate((grad_queries_ref, grad_keys_ref, grad_values_ref)):
        cols = slice(index * width, (index + 1) * width)
        grads = grad_ref[...]
        stage_ref[:, cols] = dot(normed_one, grads, TN)
        part = dot(grads, weight_ref[:, cols], NT)
        total = part if total is None else total + part
    grad_in, grad_gain_self = norm_pullback(
        targets_ref[...].astype(f32), gain_self_ref[...], total
    )
    target_grad_ref[...] = (grad_total_ref[...] + grad_in).astype(bf16)
    gains_ref[...] = jnp.concatenate(
        [grad_gain_self, grad_gain_cross_ref[...], grad_gain_feed_ref[...]]
        + [jnp.zeros((5, width), f32)],
        axis=0,
    )
    tail = jnp.concatenate([table, jnp.zeros((8, lane_tile - table.shape[1]), f32)], axis=1)
    tail = jnp.concatenate([tail, jnp.zeros_like(tail)], axis=0)

    def extra(owner):
        shift = lax.rem(width - owner * group_rows, width)
        own = pltpu.roll(gains_ref[...], shift, 1)[:, :lane_tile]
        return jnp.concatenate([own, tail], axis=0)

    put_slots(owners, keep_ref, send_ref, stage_ref, extra)


def self_backward(target_len, bucket_count, owners, operands):
    targets = operands[6]
    bias = operands[8]
    rows, width = targets.shape
    half = (owners.shape[0] // 2, 10 * group_rows, lane_tile)
    whole = pl.BlockSpec(memory_space=pltpu.VMEM)

    def body(*refs):
        self_backward_kernel(target_len, bucket_count, *refs)

    return pl.pallas_call(
        body,
        out_shape=[
            jax.ShapeDtypeStruct((rows, width), bf16),
            jax.ShapeDtypeStruct(half, bf16),
            jax.ShapeDtypeStruct(half, bf16),
        ],
        in_specs=[pl.BlockSpec(memory_space=pltpu.SMEM)] + [whole] * len(operands),
        scratch_shapes=[pltpu.VMEM((rows, width), bf16)] * 3
        + [
            pltpu.VMEM(bias.shape, f32),
            pltpu.VMEM((width, 3 * width), f32),
            pltpu.VMEM((bias.shape[0] * bucket_count, lane_tile), f32),
            pltpu.VMEM((8, width), f32),
        ],
        compiler_params=params(),
        cost_estimate=cost(32 * targets.size * width, 20 * targets.size),
        name="self_backward",
    )(owners, *operands)


def pack(shard):
    rows, columns = shard.shape
    tiles = columns // lane_tile
    return (
        shard.reshape(rows, tiles, lane_tile)
        .transpose(1, 0, 2)
        .reshape(rows * tiles, lane_tile)
    )


def unpack(packed, rows, columns):
    tiles = columns // lane_tile
    return packed.reshape(tiles, rows, lane_tile).transpose(1, 0, 2).reshape(rows, columns)


def regroup(packed, from_groups, to_groups, shapes):
    if from_groups == to_groups:
        return packed
    parts = []
    offset = 0
    for rows, columns in shapes:
        tiles = columns // lane_tile
        size = rows // from_groups * tiles
        part = packed[:, offset : offset + size, :]
        offset += size
        part = part.reshape(from_groups, tiles, rows // from_groups, lane_tile)
        part = part.transpose(0, 2, 1, 3).reshape(to_groups, rows // to_groups, tiles, lane_tile)
        parts.append(
            part.transpose(0, 2, 1, 3).reshape(to_groups, rows // to_groups * tiles, lane_tile)
        )
    return jnp.concatenate(parts, axis=1)


def gather(shards, shapes, groups, devices):
    packed = jnp.concatenate([pack(shard) for shard in shards], axis=0)
    whole = lax.all_gather(packed, axes, axis=0, tiled=False)
    return regroup(whole, devices, groups, shapes)


def scatter(packed, shapes, groups, devices):
    packed = regroup(packed, groups, devices, shapes)
    share = lax.psum_scatter(packed, axes, scatter_dimension=0, tiled=False)
    return split_share(share, shapes, devices)


core_step = 2
plane_steps = (1, 4, 5)
line_steps = (8, 16, 24)


def exchange(values, step):
    return lax.ppermute(values, axes, [(i, i ^ step) for i in range(32)])


def slot_tables(here):
    device = jnp.arange(32, dtype=jnp.int32)
    gap = device ^ here
    slots = ((gap >> 1) & 1) * 16 + ((gap & 1) + ((gap >> 2) & 1) * 2) * 4 + (gap >> 3)
    far = device & 15
    owners = here ^ ((device >> 4) * 2 + (far >> 2 & 1) + (far >> 3) * 4 + (far & 3) * 8)
    return slots.astype(jnp.int32), owners.astype(jnp.int32)


def line_gather(shard):
    return [shard] + [exchange(shard, step) for step in line_steps]


def plane_gather(line):
    line = jnp.stack(line)
    return [line] + [exchange(line, step) for step in plane_steps]


def core_gather(blocks):
    plane = jnp.concatenate(blocks)
    return plane, exchange(plane, core_step)


def tree_sum(parts):
    first, second, third, fourth = (part.astype(f32) for part in parts)
    return (first + second) + (third + fourth)


def pair_sums(keep, received):
    return [
        (keep[4 * j : 4 * j + 4].astype(f32) + received[4 * j : 4 * j + 4].astype(f32)).astype(
            bf16
        )
        for j in range(4)
    ]


def plane_exchange(parts):
    return [parts[0]] + [exchange(part, step) for part, step in zip(parts[1:], plane_steps)]


def line_sum(parts):
    moved = [exchange(parts[k + 1], step) for k, step in enumerate(line_steps)]
    return tree_sum([parts[0]] + moved)


def split_share(share, shapes, devices):
    parts = []
    offset = 0
    for rows, columns in shapes:
        size = rows // devices * (columns // lane_tile)
        parts.append(unpack(share[offset : offset + size], rows // devices, columns).astype(f32))
        offset += size
    return parts


def on_device(
    devices,
    direct,
    targets,
    memory,
    mem_lengths,
    buckets,
    cotangent,
    gain_self,
    gain_cross,
    gain_feed,
    self_query,
    self_key,
    self_value,
    self_output,
    cross_query,
    cross_key,
    cross_value,
    cross_output,
    gate_weight,
    up_weight,
    down_weight,
    bias_table,
):
    batch, target_len, width = targets.shape
    bucket_count, head_count = bias_table.shape
    row_count = batch * target_len
    groups = width // group_rows
    square = (width, width)
    feed_width = gate_weight.shape[1]
    feed_shapes = [(width, feed_width), (width, feed_width), (feed_width, width)]

    own_gains = jnp.stack([gain_self, gain_cross, gain_feed])
    self_shards = [self_query, self_key, self_value, self_output, cross_query]
    if direct:
        slots, owners = slot_tables(lax.axis_index(axes))
        extra = jnp.pad(own_gains.reshape(1, -1), ((0, 15), (0, lane_tile - own_gains.size)))
        memory_blocks = plane_gather(
            line_gather(jnp.concatenate([pack(cross_key), pack(cross_value), extra], axis=0))
        )
        self_line = line_gather(jnp.concatenate([pack(shard) for shard in self_shards], axis=0))
        memory_blocks, self_line = lax.optimization_barrier((memory_blocks, self_line))
        memory_near, memory_far = core_gather(memory_blocks)
        self_blocks = plane_gather(self_line)
        hot = (slots[:, None] == jnp.arange(groups)[None, :]).astype(bf16)
        small = [part[:, -16, : own_gains.size] for part in (memory_near, memory_far)]
        gains = (
            dot(hot, jnp.concatenate(small)).reshape(groups, 3, group_rows).transpose(1, 0, 2)
        ).reshape(3, width)
    else:
        slots, owners = slot_tables(0)

        def halves(shards):
            packed = gather(shards, [square] * len(shards), groups, devices)
            packed = jnp.take(packed, owners, axis=0)
            return packed[: groups // 2], packed[groups // 2 :]

        memory_near, memory_far = halves([cross_key, cross_value])
        self_near, self_far = halves(self_shards)
        gains = lax.all_gather(own_gains, axes, axis=1, tiled=True).astype(f32)
    packed_feed = gather(
        [gate_weight, up_weight, down_weight, cross_output],
        feed_shapes + [square],
        groups,
        devices,
    )

    pad = pair_width - target_len
    bucket_hot = (
        buckets[:, :, None] == lax.broadcasted_iota(jnp.int32, (1, 1, bucket_count), 2)
    ).reshape(target_len * target_len, bucket_count)
    bias = (
        dot(bucket_hot.astype(bf16), bias_table)
        .reshape(target_len, target_len, head_count)
        .transpose(2, 0, 1)
    )
    causal = lax.broadcasted_iota(jnp.int32, (target_len, target_len), 1) <= lax.broadcasted_iota(
        jnp.int32, (target_len, target_len), 0
    )
    bias = jnp.where(causal, bias, masked_out)
    bias = jnp.pad(bias, ((0, 0), (0, 0), (0, pad)), constant_values=masked_out)
    bias = (
        bias.reshape(head_count // 2, 2, target_len, pair_width)
        .transpose(0, 2, 1, 3)
        .reshape(head_count // 2, target_len, 2 * pair_width)
    )
    wide_buckets = jnp.pad(buckets, ((0, 0), (0, pad)), constant_values=-1)
    target_rows = targets.reshape(row_count, width)
    cot_rows = cotangent.reshape(row_count, width)

    mem_keys, mem_values, memory_weight = project_memory(
        mem_lengths, owners, memory, memory_near, memory_far
    )
    if direct:
        self_blocks, memory_weight = lax.optimization_barrier((self_blocks, memory_weight))
        self_near, self_far = core_gather(self_blocks)
    (
        normed_one,
        queries,
        key_rows,
        value_rows,
        self_context,
        after_self,
        normed_two,
        side,
        self_weight,
    ) = self_forward(
        target_len, owners, target_rows, self_near, self_far, bias, gains[0:1], gains[1:2]
    )
    cross_context, weights = cross_forward(mem_lengths, side, mem_keys, mem_values, head_count)
    outputs, grad_after_cross, grad_context, grad_gain_feed, feed_grads = feed_both(
        after_self, cross_context, cot_rows, gains[2:3], packed_feed
    )
    share_gate, share_up, share_down, share_cross_output = scatter(
        feed_grads, feed_shapes + [square], groups, devices
    )
    grad_side, grad_mem_keys, grad_mem_values = cross_backward(
        mem_lengths, grad_context, cross_context, side, mem_keys, mem_values, weights
    )
    grad_total, grad_self_context, grad_gain_cross, output_keep, output_send = (
        self_output_backward(
            owners,
            grad_side,
            after_self,
            grad_after_cross,
            normed_two,
            self_context,
            self_weight,
            gains[1:2],
        )
    )
    target_grad, self_keep, self_send = self_backward(
        target_len,
        bucket_count,
        owners,
        (
            grad_self_context,
            grad_total,
            normed_one,
            queries,
            key_rows,
            value_rows,
            target_rows,
            self_weight,
            bias,
            wide_buckets,
            gains[0:1],
            grad_gain_cross,
            grad_gain_feed,
        ),
    )
    if direct:
        output_parts = pair_sums(output_keep, exchange(output_send, core_step))
        grad_mem_keys, self_keep, output_parts = lax.optimization_barrier(
            (grad_mem_keys, self_keep, output_parts)
        )
    memory_keep, memory_send = memory_weight_grads(
        mem_lengths, owners, memory, grad_mem_keys, grad_mem_values
    )
    if direct:
        output_parts = plane_exchange(output_parts)
        self_parts = pair_sums(self_keep, exchange(self_send, core_step))
        memory_weight, memory_keep, self_parts, output_parts = lax.optimization_barrier(
            (memory_weight, memory_keep, self_parts, output_parts)
        )
    memory_grad = memory_gradient(mem_lengths, grad_mem_keys, grad_mem_values, memory_weight)
    if direct:
        self_parts = plane_exchange(self_parts)
        memory_received = exchange(memory_send, core_step)
        memory_grad, memory_received = lax.optimization_barrier((memory_grad, memory_received))
        memory_grad, self_parts = lax.optimization_barrier((memory_grad, self_parts))
        memory_parts = plane_exchange(pair_sums(memory_keep, memory_received))
        joint = line_sum(
            jnp.concatenate(
                [tree_sum(output_parts).astype(bf16), tree_sum(self_parts).astype(bf16)], axis=1
            )
        )
        output_share = joint[: 6 * group_rows]
        self_share = joint[6 * group_rows :]
        memory_share = line_sum(tree_sum(memory_parts).astype(bf16))
        share_output, share_cross_query = split_share(output_share, [square] * 2, devices)
        share_query, share_key, share_value = split_share(self_share, [square] * 3, devices)
        share_cross_key, share_cross_value = split_share(memory_share, [square] * 2, devices)
        own_grads = self_share[9 * group_rows : 9 * group_rows + 3, : width // devices]
        table = self_share[9 * group_rows + 8 : 9 * group_rows + 10]
    else:

        def reduced(keep, send, count):
            packed = jnp.take(jnp.concatenate([keep, send]), slots, axis=0)
            return scatter(
                packed[:, : 3 * count * group_rows], [square] * count, groups, devices
            )

        share_output, share_cross_query = reduced(output_keep, output_send, 2)
        share_query, share_key, share_value = reduced(self_keep, self_send, 3)
        share_cross_key, share_cross_value = reduced(memory_keep, memory_send, 2)
        small = jnp.take(jnp.concatenate([self_keep, self_send]), slots, axis=0)
        small = small[:, 9 * group_rows :].astype(f32)
        grad_gains = small[:, :3, :group_rows].transpose(1, 0, 2).reshape(-1)
        small = jnp.concatenate([grad_gains, small[0, 8:10].reshape(-1)])
        small = jnp.sum(lax.all_gather(small, axes, axis=0, tiled=False), axis=0)
        own_grads = lax.dynamic_index_in_dim(
            small[: 3 * width].reshape(3, devices, -1), lax.axis_index(axes), 1, False
        )
        table = small[3 * width :].reshape(2, lane_tile)
    table_grad = (
        table[:, : bucket_count * head_count // 2]
        .reshape(2, head_count // 2, bucket_count)
        .transpose(2, 1, 0)
        .reshape(bucket_count, head_count)
    )

    return (
        outputs.reshape(targets.shape),
        target_grad.reshape(targets.shape),
        memory_grad,
        own_grads[0],
        own_grads[1],
        own_grads[2],
        share_query,
        share_key,
        share_value,
        share_output,
        share_cross_query,
        share_cross_key,
        share_cross_value,
        share_cross_output,
        share_gate,
        share_up,
        share_down,
        table_grad,
    )


def solution(mesh):
    devices = mesh.shape["dp"] * mesh.shape["seq"]
    direct = mesh.shape["dp"] == 16 and mesh.shape["seq"] == 2
    rows = P(axes, None, None)
    flat = P(axes)
    weight = P(axes, None)

    def body(*arguments):
        return on_device(devices, direct, *arguments)

    return jax.shard_map(
        body,
        mesh=mesh,
        in_specs=(rows, rows, flat, P(), rows, flat, flat, flat) + (weight,) * 11 + (P(),),
        out_specs=(rows, rows, rows, flat, flat, flat) + (weight,) * 11 + (P(),),
        check_vma=False,
    )
```

```python
import math

import jax
import jax.numpy as jnp
from jax import lax
from jax.experimental import pallas as pl
from jax.experimental.pallas import tpu as pltpu
from jax.sharding import PartitionSpec as P

epsilon = 1e-06
masked_out = -1e30
bf16 = jnp.bfloat16
f32 = jnp.float32
axes = ("dp", "seq")
lane_tile = 256
group_rows = 24
pair_width = 128
pair_group = 3
NN = (((1,), (0,)), ((), ()))
NT = (((1,), (1,)), ((), ()))
TN = (((0,), (0,)), ((), ()))
gelu_scale = math.sqrt(2.0 / math.pi)
gelu_cubic = 0.044715


def dot(left_side, right_side, dims=NN):
    return lax.dot_general(left_side, right_side, dims, preferred_element_type=f32)


def params():
    return pltpu.CompilerParams(vmem_limit_bytes=60 * 1024 * 1024)


def cost(flops, size, exps=0):
    return pl.CostEstimate(
        flops=int(flops), bytes_accessed=int(size), transcendentals=int(exps)
    )


def column_tile(packed_ref, index):
    tile = packed_ref[:, index * group_rows : (index + 1) * group_rows, :]
    return tile.reshape(tile.shape[0] * group_rows, lane_tile)


def lane_halves(rows):
    lanes = lax.broadcasted_iota(jnp.int32, (rows, pair_width), 1)
    return lanes < pair_width // 2


def project(rows, packed_ref, base, tiles):
    return [dot(rows, column_tile(packed_ref, base + t)) for t in range(tiles)]


def through(rows, packed_ref, base, tiles):
    total = None
    for t in range(tiles):
        part = dot(
            rows[:, t * lane_tile : (t + 1) * lane_tile], column_tile(packed_ref, base + t), NT
        )
        total = part if total is None else total + part
    return total


def assemble(owners, block_refs, weight_ref):
    slots = block_refs[0].shape[0]
    for first in range(0, len(block_refs), 2):
        even_ref, odd_ref = block_refs[first : first + 2]

        def place(slot, carry):
            owner = owners[first * slots + slot]
            swap = (owner & 1) == 1
            rows = pl.ds(pl.multiple_of((owner >> 1) * (2 * group_rows), 16), 2 * group_rows)
            for t in range(weight_ref.shape[1] // lane_tile):
                part = slice(t * group_rows, (t + 1) * group_rows)
                cols = slice(t * lane_tile, (t + 1) * lane_tile)
                one = even_ref[slot, part, :]
                two = odd_ref[slot, part, :]
                weight_ref[rows, cols] = jnp.concatenate(
                    [jnp.where(swap, two, one), jnp.where(swap, one, two)], axis=0
                )
            return carry

        lax.fori_loop(0, slots, place, 0)


def put_slots(owners, keep_ref, send_ref, stage_ref, extra=None):
    half = keep_ref.shape[0]
    tiles = stage_ref.shape[1] // lane_tile

    def place(slot, carry):
        for offset, out_ref in ((0, keep_ref), (half, send_ref)):
            owner = owners[slot + offset]
            rows = pl.ds(pl.multiple_of(owner * group_rows, 8), group_rows)
            parts = [
                stage_ref[rows, t * lane_tile : (t + 1) * lane_tile] for t in range(tiles)
            ]
            if extra is not None:
                parts.append(extra(owner))
            for t in range(0, len(parts), 2):
                both = jnp.concatenate(parts[t : t + 2], axis=0).astype(bf16)
                start = t * group_rows
                out_ref[slot, start : start + both.shape[0], :] = both
        return carry

    lax.fori_loop(0, half, place, 0)


def norm_scale(values):
    return lax.rsqrt(jnp.mean(values * values, axis=-1, keepdims=True) + epsilon)


def norm_pullback(values, gain_row, grad_in):
    inverse = norm_scale(values)
    weighted = grad_in * gain_row
    inner = jnp.mean(weighted * values, axis=-1, keepdims=True)
    grad_values = inverse * weighted - values * (inverse * inverse * inverse * inner)
    grad_gain = jnp.sum(grad_in * values * inverse, axis=0, keepdims=True)
    return grad_values, grad_gain


def memory_kernel(lengths, owners, memory_ref, *refs):
    block_refs = refs[:-3]
    keys_ref, values_ref, weight_ref = refs[-3:]
    seq = pl.program_id(0)
    memory_len = memory_ref.shape[1]

    @pl.when(seq == 0)
    def _():
        assemble(owners, block_refs, weight_ref)

    def fill(count):
        rows = memory_ref[0, :count, :]
        for base, out_ref in ((0, keys_ref), (3, values_ref)):
            for t in range(3):
                out_ref[0, :count, t * lane_tile : (t + 1) * lane_tile] = dot(
                    rows, weight_ref[:, (base + t) * lane_tile : (base + t + 1) * lane_tile]
                ).astype(bf16)

    @pl.when(lengths[seq] > memory_len // 2)
    def _():
        fill(memory_len)

    @pl.when(lengths[seq] <= memory_len // 2)
    def _():
        fill(memory_len // 2)


def project_memory(mem_lengths, owners, memory, blocks):
    batch, memory_len, width = memory.shape
    block = pl.BlockSpec((1, memory_len, width), lambda b, n, s: (b, 0, 0))
    return pl.pallas_call(
        memory_kernel,
        out_shape=[jax.ShapeDtypeStruct(memory.shape, bf16)] * 2
        + [jax.ShapeDtypeStruct((width, 2 * width), bf16)],
        grid_spec=pltpu.PrefetchScalarGridSpec(
            num_scalar_prefetch=2,
            grid=(batch,),
            in_specs=[block] + [pl.BlockSpec(blocks[0].shape, lambda b, n, s: (0, 0, 0))] * len(blocks),
            out_specs=[block, block, pl.BlockSpec((width, 2 * width), lambda b, n, s: (0, 0))],
        ),
        compiler_params=params(),
        cost_estimate=cost(4 * memory.size * width, 6 * memory.size),
        name="memory_project",
    )(mem_lengths, owners, memory, *blocks)


def stacked_pair(rows, half, pad):
    zero = jnp.zeros_like(rows)
    gap = jnp.zeros((pad, pair_width), rows.dtype)
    return jnp.concatenate(
        [jnp.where(half, rows, zero), gap, jnp.where(half, zero, rows), gap], axis=0
    )


def pair_softmax(scores):
    parts = []
    for h in range(2):
        one = scores[:, h * pair_width : (h + 1) * pair_width]
        terms = jnp.exp(one - jnp.max(one, axis=-1, keepdims=True))
        parts.append(terms * (1.0 / jnp.sum(terms, axis=-1, keepdims=True)))
    return parts


def self_attend_kernel(
    target_len,
    block_refs,
    owners,
    targets_ref,
    bias_ref,
    gain_self_ref,
    normed_one_ref,
    queries_ref,
    keys_ref,
    values_ref,
    context_ref,
    weight_ref,
):
    width = targets_ref.shape[1]
    assemble(owners, block_refs, weight_ref)
    inputs = targets_ref[...].astype(f32)
    normed_one = (inputs * norm_scale(inputs) * gain_self_ref[...]).astype(bf16)
    normed_one_ref[...] = normed_one
    for index, out_ref in ((0, queries_ref), (1, keys_ref), (2, values_ref)):
        out_ref[...] = dot(
            normed_one, weight_ref[:, index * width : (index + 1) * width]
        ).astype(bf16)
    half = lane_halves(target_len)
    pad = pair_width - target_len
    pairs = bias_ref.shape[0]
    columns = [slice(p * pair_width, (p + 1) * pair_width) for p in range(pairs)]

    def attend(seq, carry):
        rows = pl.ds(pl.multiple_of(seq * target_len, 32), target_len)
        scores = [
            dot(queries_ref[rows, cols], stacked_pair(keys_ref[rows, cols], half, pad), NT)
            + bias_ref[p]
            for p, cols in enumerate(columns)
        ]
        probs = [
            jnp.concatenate(pair_softmax(score), axis=1).astype(bf16) for score in scores
        ]
        for p, cols in enumerate(columns):
            value_stack = stacked_pair(values_ref[rows, cols], half, pad)
            context_ref[rows, cols] = dot(probs[p], value_stack).astype(bf16)
        return carry

    lax.fori_loop(0, targets_ref.shape[0] // target_len, attend, 0)


def self_attend(target_len, owners, targets, bias, gain_self, blocks):
    width = targets.shape[1]
    whole = pl.BlockSpec(memory_space=pltpu.VMEM)
    low = jax.ShapeDtypeStruct(targets.shape, bf16)

    def body(*refs):
        stop = 4 + len(blocks)
        self_attend_kernel(target_len, refs[4:stop], *refs[:4], *refs[stop:])

    return pl.pallas_call(
        body,
        out_shape=[low] * 5 + [jax.ShapeDtypeStruct((width, 3 * width), bf16)],
        in_specs=[pl.BlockSpec(memory_space=pltpu.SMEM)] + [whole] * (3 + len(blocks)),
        compiler_params=params(),
        cost_estimate=cost(16 * targets.size * width, 12 * targets.size),
        name="self_attend",
    )(owners, targets, bias, gain_self, *blocks)


def self_project_kernel(
    block_refs,
    owners,
    targets_ref,
    context_ref,
    gain_cross_ref,
    after_ref,
    normed_two_ref,
    side_ref,
    weight_ref,
):
    width = targets_ref.shape[1]
    assemble(owners, block_refs, weight_ref)
    after = targets_ref[...].astype(f32) + dot(context_ref[...], weight_ref[:, :width])
    after_ref[...] = after
    normed_two = (after * norm_scale(after) * gain_cross_ref[...]).astype(bf16)
    normed_two_ref[...] = normed_two
    side_ref[...] = dot(normed_two, weight_ref[:, width:]).astype(bf16)


def self_project(owners, targets, context, gain_cross, blocks):
    width = targets.shape[1]
    whole = pl.BlockSpec(memory_space=pltpu.VMEM)
    low = jax.ShapeDtypeStruct(targets.shape, bf16)

    def body(*refs):
        stop = 4 + len(blocks)
        self_project_kernel(refs[4:stop], *refs[:4], *refs[stop:])

    return pl.pallas_call(
        body,
        out_shape=[
            jax.ShapeDtypeStruct(targets.shape, f32),
            low,
            low,
            jax.ShapeDtypeStruct((width, 2 * width), bf16),
        ],
        in_specs=[pl.BlockSpec(memory_space=pltpu.SMEM)] + [whole] * (3 + len(blocks)),
        compiler_params=params(),
        cost_estimate=cost(4 * targets.size * width, 12 * targets.size),
        name="self_project",
    )(owners, targets, context, gain_cross, *blocks)


def masked_stack(rows, half):
    zero = jnp.zeros_like(rows)
    return jnp.concatenate([jnp.where(half, rows, zero), jnp.where(half, zero, rows)], axis=0)


def cross_forward_kernel(lengths, side_ref, keys_ref, values_ref, context_ref, weights_ref):
    seq = pl.program_id(0)
    target_len, width = side_ref.shape
    memory_len = keys_ref.shape[1]
    half = lane_halves(target_len)

    def attend(count):
        for p in range(width // pair_width):
            cols = slice(p * pair_width, (p + 1) * pair_width)
            stack = masked_stack(side_ref[:, cols], half)
            scores = dot(stack, keys_ref[0, :count, cols], NT)
            terms = jnp.exp(scores - jnp.max(scores, axis=-1, keepdims=True))
            scale = 1.0 / jnp.sum(terms, axis=-1, keepdims=True)
            weights = (terms * scale).astype(bf16)
            weights_ref[0, 2 * target_len * p : 2 * target_len * (p + 1), :count] = weights
            both = dot(weights, values_ref[0, :count, cols])
            context_ref[:, cols] = jnp.where(half, both[:target_len], both[target_len:]).astype(
                bf16
            )

    @pl.when(lengths[seq] > memory_len // 2)
    def _():
        attend(memory_len)

    @pl.when(lengths[seq] <= memory_len // 2)
    def _():
        attend(memory_len // 2)


def cross_forward(mem_lengths, side, mem_keys, mem_values, head_count):
    batch, memory_len, width = mem_keys.shape
    target_len = side.shape[0] // batch
    rows = pl.BlockSpec((target_len, width), lambda b, n: (b, 0))
    memory = pl.BlockSpec((1, memory_len, width), lambda b, n: (b, 0, 0))
    weights = pl.BlockSpec((1, head_count * target_len, memory_len), lambda b, n: (b, 0, 0))
    return pl.pallas_call(
        cross_forward_kernel,
        out_shape=[
            jax.ShapeDtypeStruct(side.shape, bf16),
            jax.ShapeDtypeStruct((batch, head_count * target_len, memory_len), bf16),
        ],
        grid_spec=pltpu.PrefetchScalarGridSpec(
            num_scalar_prefetch=1,
            grid=(batch,),
            in_specs=[rows, memory, memory],
            out_specs=[rows, weights],
        ),
        compiler_params=params(),
        cost_estimate=cost(16 * side.size * memory_len, 6 * mem_keys.size, batch * head_count * target_len * memory_len),
        name="cross_forward",
    )(mem_lengths, side, mem_keys, mem_values)


def feed_kernel(
    after_ref,
    context_ref,
    cot_ref,
    gain_ref,
    side_output_ref,
    gate_ref,
    up_ref,
    down_ref,
    outputs_ref,
    grad_after_ref,
    grad_context_ref,
    grad_gain_ref,
    packed_ref,
    after_cross_ref,
    normed_ref,
    out_total_ref,
    grad_normed_ref,
):
    step = pl.program_id(0)
    steps = pl.num_programs(0)

    @pl.when(step == 0)
    def _():
        after_cross = after_ref[...] + jnp.concatenate(
            project(context_ref[...], side_output_ref, 0, 3), axis=1
        )
        after_cross_ref[...] = after_cross
        normed_ref[...] = (after_cross * norm_scale(after_cross) * gain_ref[...]).astype(bf16)
        out_total_ref[...] = after_cross
        grad_normed_ref[...] = jnp.zeros_like(grad_normed_ref)

    normed = normed_ref[...]
    cot = cot_ref[...]
    gate_weight = column_tile(gate_ref, 0)
    up_weight = column_tile(up_ref, 0)
    share = down_ref.shape[1] // 3
    owners = down_ref.shape[0]
    down_weight = jnp.concatenate(
        [
            down_ref[:, c * share : (c + 1) * share, :].reshape(owners * share, lane_tile)
            for c in range(3)
        ],
        axis=1,
    )
    gate = dot(normed, gate_weight)
    up = dot(normed, up_weight)
    grad_hidden = dot(cot, down_weight, NT)
    square = gate * gate
    tanh = jnp.tanh(gelu_scale * (gate + gelu_cubic * (square * gate)))
    half_sum = 0.5 * (1.0 + tanh)
    active = gate * half_sum
    slope = half_sum + 0.5 * gate * (1.0 - tanh * tanh) * (
        gelu_scale * (1.0 + 3.0 * gelu_cubic * square)
    )
    hidden = (active * up).astype(bf16)
    grad_gate = (grad_hidden * up * slope).astype(bf16)
    grad_up = (grad_hidden * active).astype(bf16)
    out_total_ref[...] += dot(hidden, down_weight)
    grad_normed_ref[...] += dot(grad_gate, gate_weight, NT) + dot(grad_up, up_weight, NT)
    groups = packed_ref.shape[0]

    def put(base, value):
        packed_ref[:, pl.ds(base + step * group_rows, group_rows), :] = value.reshape(
            groups, group_rows, lane_tile
        ).astype(bf16)

    put(0, dot(normed, grad_gate, TN))
    put(steps * group_rows, dot(normed, grad_up, TN))
    down_base = 2 * steps * group_rows
    for c in range(3):
        part = dot(hidden, cot[:, c * lane_tile : (c + 1) * lane_tile], TN)
        packed_ref[
            pl.ds(step * owners, owners), down_base + c * share : down_base + (c + 1) * share, :
        ] = part.reshape(owners, share, lane_tile).astype(bf16)

    @pl.when(step == steps - 1)
    def _():
        outputs_ref[...] = out_total_ref[...].astype(bf16)
        grad_in, grad_gain = norm_pullback(
            after_cross_ref[...], gain_ref[...], grad_normed_ref[...]
        )
        grad_gain_ref[...] = grad_gain
        grad_after = cot_ref[...].astype(f32) + grad_in
        grad_after_ref[...] = grad_after
        low = grad_after.astype(bf16)
        for c in range(3):
            cols = slice(c * lane_tile, (c + 1) * lane_tile)
            start = 3 * down_base // 2 + c * group_rows
            packed_ref[:, start : start + group_rows, :] = (
                dot(context_ref[...], low[:, cols], TN)
                .reshape(groups, group_rows, lane_tile)
                .astype(bf16)
            )
        grad_context_ref[...] = through(low, side_output_ref, 0, 3).astype(bf16)


def feed_both(after_self, context, cotangent, gain, packed_feed):
    rows, width = context.shape
    groups, feed_rows, _ = packed_feed.shape
    steps = feed_rows // (3 * group_rows) - 1
    owners = groups // steps
    whole = lambda f: (0, 0)
    full = pl.BlockSpec((rows, width), whole)
    tile = (groups, group_rows, lane_tile)
    return pl.pallas_call(
        feed_kernel,
        out_shape=[
            jax.ShapeDtypeStruct((rows, width), bf16),
            jax.ShapeDtypeStruct((rows, width), f32),
            jax.ShapeDtypeStruct((rows, width), bf16),
            jax.ShapeDtypeStruct((1, width), f32),
            jax.ShapeDtypeStruct((groups, feed_rows, lane_tile), bf16),
        ],
        grid=(steps,),
        in_specs=[
            full,
            full,
            full,
            pl.BlockSpec((1, width), whole),
            pl.BlockSpec((groups, 3 * group_rows, lane_tile), lambda f: (0, steps, 0)),
            pl.BlockSpec(tile, lambda f: (0, f, 0)),
            pl.BlockSpec(tile, lambda f: (0, steps + f, 0)),
            pl.BlockSpec((owners, steps * group_rows, lane_tile), lambda f: (f, 2, 0)),
        ],
        out_specs=[
            full,
            full,
            full,
            pl.BlockSpec((1, width), whole),
            pl.BlockSpec((groups, feed_rows, lane_tile), lambda f: (0, 0, 0)),
        ],
        scratch_shapes=[
            pltpu.VMEM((rows, width), f32),
            pltpu.VMEM((rows, width), bf16),
            pltpu.VMEM((rows, width), f32),
            pltpu.VMEM((rows, width), f32),
        ],
        compiler_params=params(),
        cost_estimate=cost(18 * rows * width * steps * lane_tile, 30 * rows * width),
        name="feed_both",
    )(after_self, context, cotangent, gain, packed_feed, packed_feed, packed_feed, packed_feed)


def cross_backward_kernel(
    lengths,
    grad_ref,
    context_ref,
    side_ref,
    keys_ref,
    values_ref,
    weights_ref,
    grad_side_ref,
    grad_keys_ref,
    grad_values_ref,
):
    seq = pl.program_id(0)
    target_len, width = side_ref.shape
    memory_len = keys_ref.shape[1]
    half = lane_halves(target_len)

    def attend(count):
        for p in range(width // pair_width):
            cols = slice(p * pair_width, (p + 1) * pair_width)
            grad_rows = grad_ref[:, cols]
            grad_stack = masked_stack(grad_rows, half)
            query_stack = masked_stack(side_ref[:, cols], half)
            product = grad_rows.astype(f32) * context_ref[:, cols].astype(f32)
            inner = jnp.sum(masked_stack(product, half), axis=-1, keepdims=True)
            weights = weights_ref[0, 2 * target_len * p : 2 * target_len * (p + 1), :count]
            grad_probs = dot(grad_stack, values_ref[0, :count, cols], NT)
            grad_scores = (weights.astype(f32) * (grad_probs - inner)).astype(bf16)
            both = dot(grad_scores, keys_ref[0, :count, cols])
            grad_side_ref[:, cols] = jnp.where(half, both[:target_len], both[target_len:]).astype(
                bf16
            )
            grad_keys_ref[0, cols, :count] = dot(query_stack, grad_scores, TN).astype(bf16)
            grad_values_ref[0, cols, :count] = dot(grad_stack, weights, TN).astype(bf16)

    @pl.when(lengths[seq] > memory_len // 2)
    def _():
        attend(memory_len)

    @pl.when(lengths[seq] <= memory_len // 2)
    def _():
        attend(memory_len // 2)


def cross_backward(mem_lengths, grad_context, context, side, mem_keys, mem_values, weights):
    batch, memory_len, width = mem_keys.shape
    target_len = side.shape[0] // batch
    rows = pl.BlockSpec((target_len, width), lambda b, n: (b, 0))
    memory = pl.BlockSpec((1, memory_len, width), lambda b, n: (b, 0, 0))
    turned = pl.BlockSpec((1, width, memory_len), lambda b, n: (b, 0, 0))
    return pl.pallas_call(
        cross_backward_kernel,
        out_shape=[jax.ShapeDtypeStruct(side.shape, bf16)]
        + [jax.ShapeDtypeStruct((batch, width, memory_len), bf16)] * 2,
        grid_spec=pltpu.PrefetchScalarGridSpec(
            num_scalar_prefetch=1,
            grid=(batch,),
            in_specs=[
                rows,
                rows,
                rows,
                memory,
                memory,
                pl.BlockSpec((1,) + weights.shape[1:], lambda b, n: (b, 0, 0)),
            ],
            out_specs=[rows, turned, turned],
        ),
        compiler_params=params(),
        cost_estimate=cost(32 * side.size * memory_len, 10 * mem_keys.size),
        name="cross_backward",
    )(mem_lengths, grad_context, context, side, mem_keys, mem_values, weights)


def memory_weight_kernel(
    lengths,
    owners,
    memory_ref,
    grad_keys_ref,
    grad_values_ref,
    keep_ref,
    send_ref,
    key_total_ref,
    value_total_ref,
    stage_ref,
):
    seq = pl.program_id(0)
    memory_len = memory_ref.shape[1]

    @pl.when(seq == 0)
    def _():
        key_total_ref[...] = jnp.zeros_like(key_total_ref)
        value_total_ref[...] = jnp.zeros_like(value_total_ref)

    def add(count):
        rows = memory_ref[0, :count, :]
        key_total_ref[...] += dot(grad_keys_ref[0, :, :count], rows)
        value_total_ref[...] += dot(grad_values_ref[0, :, :count], rows)

    @pl.when(lengths[seq] > memory_len // 2)
    def _():
        add(memory_len)

    @pl.when(lengths[seq] <= memory_len // 2)
    def _():
        add(memory_len // 2)

    @pl.when(seq == pl.num_programs(0) - 1)
    def _():
        width = key_total_ref.shape[0]
        for base, total_ref in ((0, key_total_ref), (width, value_total_ref)):
            for start in range(0, width, lane_tile):
                stage_ref[:, base + start : base + start + lane_tile] = jnp.transpose(
                    total_ref[start : start + lane_tile, :]
                )
        put_slots(owners, keep_ref, send_ref, stage_ref)


def memory_weight_grads(mem_lengths, owners, memory, grad_keys, grad_values):
    batch, memory_len, width = memory.shape
    block = pl.BlockSpec((1, memory_len, width), lambda b, n, o: (b, 0, 0))
    turned = pl.BlockSpec((1, width, memory_len), lambda b, n, o: (b, 0, 0))
    half = (owners.shape[0] // 2, 2 * width // lane_tile * group_rows, lane_tile)
    return pl.pallas_call(
        memory_weight_kernel,
        out_shape=[jax.ShapeDtypeStruct(half, bf16)] * 2,
        grid_spec=pltpu.PrefetchScalarGridSpec(
            num_scalar_prefetch=2,
            grid=(batch,),
            in_specs=[block, turned, turned],
            out_specs=[pl.BlockSpec(half, lambda b, n, o: (0, 0, 0))] * 2,
            scratch_shapes=[pltpu.VMEM((width, width), f32)] * 2
            + [pltpu.VMEM((width, 2 * width), f32)],
        ),
        compiler_params=params(),
        cost_estimate=cost(4 * memory.size * width, 6 * memory.size),
        name="memory_weight_grads",
    )(mem_lengths, owners, memory, grad_keys, grad_values)


def memory_grad_kernel(
    lengths, grad_keys_ref, grad_values_ref, weight_ref, out_ref, key_turned_ref, value_turned_ref
):
    seq = pl.program_id(0)
    memory_len = out_ref.shape[1]

    @pl.when(seq == 0)
    def _():
        for base, turned_ref in ((0, key_turned_ref), (3, value_turned_ref)):
            for t in range(3):
                turned_ref[t * lane_tile : (t + 1) * lane_tile, :] = jnp.transpose(
                    weight_ref[:, (base + t) * lane_tile : (base + t + 1) * lane_tile]
                )

    def fill(count):
        out_ref[0, :count, :] = (
            dot(grad_keys_ref[0, :, :count], key_turned_ref[...], TN)
            + dot(grad_values_ref[0, :, :count], value_turned_ref[...], TN)
        ).astype(bf16)

    @pl.when(lengths[seq] > memory_len // 2)
    def _():
        fill(memory_len)

    @pl.when(lengths[seq] <= memory_len // 2)
    def _():
        fill(memory_len // 2)
        out_ref[0, memory_len // 2 :, :] = jnp.zeros_like(out_ref[0, memory_len // 2 :, :])


def memory_gradient(mem_lengths, grad_keys, grad_values, weight):
    batch, width, memory_len = grad_keys.shape
    turned = pl.BlockSpec((1, width, memory_len), lambda b, n: (b, 0, 0))
    return pl.pallas_call(
        memory_grad_kernel,
        out_shape=jax.ShapeDtypeStruct((batch, memory_len, width), bf16),
        grid_spec=pltpu.PrefetchScalarGridSpec(
            num_scalar_prefetch=1,
            grid=(batch,),
            in_specs=[turned, turned, pl.BlockSpec(weight.shape, lambda b, n: (0, 0))],
            out_specs=pl.BlockSpec((1, memory_len, width), lambda b, n: (b, 0, 0)),
            scratch_shapes=[pltpu.VMEM((width, width), bf16)] * 2,
        ),
        compiler_params=params(),
        cost_estimate=cost(4 * grad_keys.size * width, 6 * grad_keys.size),
        name="memory_grad",
    )(mem_lengths, grad_keys, grad_values, weight)


def self_output_kernel(
    owners,
    grad_side_ref,
    after_ref,
    grad_after_ref,
    normed_two_ref,
    context_ref,
    weight_ref,
    gain_cross_ref,
    grad_total_ref,
    grad_context_ref,
    grad_gain_ref,
    keep_ref,
    send_ref,
    stage_ref,
):
    width = after_ref.shape[1]
    grad_side = grad_side_ref[...]
    grad_normed = dot(grad_side, weight_ref[:, width:], NT)
    grad_in, grad_gain = norm_pullback(after_ref[...], gain_cross_ref[...], grad_normed)
    grad_gain_ref[...] = grad_gain
    grad_total = grad_after_ref[...] + grad_in
    grad_total_ref[...] = grad_total
    low = grad_total.astype(bf16)
    stage_ref[:, :width] = dot(context_ref[...], low, TN)
    stage_ref[:, width:] = dot(normed_two_ref[...], grad_side, TN)
    grad_context_ref[...] = dot(low, weight_ref[:, :width], NT).astype(bf16)
    put_slots(owners, keep_ref, send_ref, stage_ref)


def self_output_backward(
    owners, grad_side, after, grad_after, normed_two, context, weight, gain_cross
):
    rows, width = after.shape
    half = (owners.shape[0] // 2, 2 * width // lane_tile * group_rows, lane_tile)
    whole = pl.BlockSpec(memory_space=pltpu.VMEM)
    return pl.pallas_call(
        self_output_kernel,
        out_shape=[
            jax.ShapeDtypeStruct((rows, width), f32),
            jax.ShapeDtypeStruct((rows, width), bf16),
            jax.ShapeDtypeStruct((1, width), f32),
            jax.ShapeDtypeStruct(half, bf16),
            jax.ShapeDtypeStruct(half, bf16),
        ],
        in_specs=[pl.BlockSpec(memory_space=pltpu.SMEM)] + [whole] * 7,
        scratch_shapes=[pltpu.VMEM((width, 2 * width), f32)],
        compiler_params=params(),
        cost_estimate=cost(8 * after.size * width, 20 * after.size),
        name="self_output_backward",
    )(owners, grad_side, after, grad_after, normed_two, context, weight, gain_cross)


def self_backward_kernel(
    target_len,
    bucket_count,
    owners,
    grad_context_ref,
    grad_total_ref,
    normed_one_ref,
    queries_ref,
    keys_ref,
    values_ref,
    targets_ref,
    weight_ref,
    bias_ref,
    buckets_ref,
    gain_self_ref,
    grad_gain_cross_ref,
    grad_gain_feed_ref,
    target_grad_ref,
    keep_ref,
    send_ref,
    grad_queries_ref,
    grad_keys_ref,
    grad_values_ref,
    score_total_ref,
    stage_ref,
    table_ref,
    gains_ref,
):
    width = targets_ref.shape[1]
    half = lane_halves(target_len)
    pad = pair_width - target_len
    pairs = bias_ref.shape[0]
    columns = [slice(p * pair_width, (p + 1) * pair_width) for p in range(pairs)]
    score_total_ref[...] = jnp.zeros_like(score_total_ref)

    def pick(values):
        return jnp.where(
            half, values[:target_len], values[pair_width : pair_width + target_len]
        ).astype(bf16)

    def attend(seq, carry):
        rows = pl.ds(pl.multiple_of(seq * target_len, 32), target_len)
        for first in range(0, pairs, pair_group):
            chosen = range(first, first + pair_group)
            key_stacks = [stacked_pair(keys_ref[rows, columns[p]], half, pad) for p in chosen]
            scores = [
                dot(queries_ref[rows, columns[p]], stack, NT) + bias_ref[p]
                for p, stack in zip(chosen, key_stacks)
            ]
            grad_probs = [
                dot(
                    grad_context_ref[rows, columns[p]],
                    stacked_pair(values_ref[rows, columns[p]], half, pad),
                    NT,
                )
                for p in chosen
            ]
            probs = [pair_softmax(score) for score in scores]
            grad_scores = []
            for prob, grad_prob in zip(probs, grad_probs):
                parts = []
                for h in range(2):
                    one = grad_prob[:, h * pair_width : (h + 1) * pair_width]
                    inner = jnp.sum(one * prob[h], axis=-1, keepdims=True)
                    parts.append(prob[h] * (one - inner))
                grad_scores.append(jnp.concatenate(parts, axis=1).astype(bf16))
            for p, stack, prob, grad_score in zip(chosen, key_stacks, probs, grad_scores):
                cols = columns[p]
                weights = jnp.concatenate(prob, axis=1).astype(bf16)
                score_total_ref[p] += grad_score.astype(f32)
                grad_queries_ref[rows, cols] = dot(grad_score, stack).astype(bf16)
                grad_keys_ref[rows, cols] = pick(dot(grad_score, queries_ref[rows, cols], TN))
                grad_values_ref[rows, cols] = pick(
                    dot(weights, grad_context_ref[rows, cols], TN)
                )
        return carry

    lax.fori_loop(0, targets_ref.shape[0] // target_len, attend, 0)
    buckets = buckets_ref[...]
    both = jnp.concatenate([buckets, buckets], axis=1)

    def count(bucket, carry):
        chosen = both == bucket
        for p in range(pairs):
            table_ref[pl.ds(p * bucket_count + bucket, 1), :] = jnp.sum(
                jnp.where(chosen, score_total_ref[p], 0.0), axis=0, keepdims=True
            )
        return carry

    lax.fori_loop(0, bucket_count, count, 0)
    lanes = lax.broadcasted_iota(jnp.int32, (8, lane_tile), 1) >> 7
    head = (lanes == lax.broadcasted_iota(jnp.int32, (8, lane_tile), 0)).astype(f32)
    table = lax.dot_general(
        head, table_ref[...], NT, precision=lax.Precision.HIGHEST, preferred_element_type=f32
    )

    normed_one = normed_one_ref[...]
    total = None
    for index, grad_ref in enumerate((grad_queries_ref, grad_keys_ref, grad_values_ref)):
        cols = slice(index * width, (index + 1) * width)
        grads = grad_ref[...]
        stage_ref[:, cols] = dot(normed_one, grads, TN)
        part = dot(grads, weight_ref[:, cols], NT)
        total = part if total is None else total + part
    grad_in, grad_gain_self = norm_pullback(
        targets_ref[...].astype(f32), gain_self_ref[...], total
    )
    target_grad_ref[...] = (grad_total_ref[...] + grad_in).astype(bf16)
    gains_ref[...] = jnp.concatenate(
        [grad_gain_self, grad_gain_cross_ref[...], grad_gain_feed_ref[...]]
        + [jnp.zeros((5, width), f32)],
        axis=0,
    )
    tail = jnp.concatenate([table, jnp.zeros((8, lane_tile - table.shape[1]), f32)], axis=1)
    tail = jnp.concatenate([tail, jnp.zeros_like(tail)], axis=0)

    def extra(owner):
        shift = lax.rem(width - owner * group_rows, width)
        own = pltpu.roll(gains_ref[...], shift, 1)[:, :lane_tile]
        return jnp.concatenate([own, tail], axis=0)

    put_slots(owners, keep_ref, send_ref, stage_ref, extra)


def self_backward(target_len, bucket_count, owners, operands):
    targets = operands[6]
    bias = operands[8]
    rows, width = targets.shape
    half = (owners.shape[0] // 2, 10 * group_rows, lane_tile)
    whole = pl.BlockSpec(memory_space=pltpu.VMEM)

    def body(*refs):
        self_backward_kernel(target_len, bucket_count, *refs)

    return pl.pallas_call(
        body,
        out_shape=[
            jax.ShapeDtypeStruct((rows, width), bf16),
            jax.ShapeDtypeStruct(half, bf16),
            jax.ShapeDtypeStruct(half, bf16),
        ],
        in_specs=[pl.BlockSpec(memory_space=pltpu.SMEM)] + [whole] * len(operands),
        scratch_shapes=[pltpu.VMEM((rows, width), bf16)] * 3
        + [
            pltpu.VMEM(bias.shape, f32),
            pltpu.VMEM((width, 3 * width), f32),
            pltpu.VMEM((bias.shape[0] * bucket_count, lane_tile), f32),
            pltpu.VMEM((8, width), f32),
        ],
        compiler_params=params(),
        cost_estimate=cost(32 * targets.size * width, 20 * targets.size),
        name="self_backward",
    )(owners, *operands)


def pack(shard):
    rows, columns = shard.shape
    tiles = columns // lane_tile
    return (
        shard.reshape(rows, tiles, lane_tile)
        .transpose(1, 0, 2)
        .reshape(rows * tiles, lane_tile)
    )


def unpack(packed, rows, columns):
    tiles = columns // lane_tile
    return packed.reshape(tiles, rows, lane_tile).transpose(1, 0, 2).reshape(rows, columns)


def regroup(packed, from_groups, to_groups, shapes):
    if from_groups == to_groups:
        return packed
    parts = []
    offset = 0
    for rows, columns in shapes:
        tiles = columns // lane_tile
        size = rows // from_groups * tiles
        part = packed[:, offset : offset + size, :]
        offset += size
        part = part.reshape(from_groups, tiles, rows // from_groups, lane_tile)
        part = part.transpose(0, 2, 1, 3).reshape(to_groups, rows // to_groups, tiles, lane_tile)
        parts.append(
            part.transpose(0, 2, 1, 3).reshape(to_groups, rows // to_groups * tiles, lane_tile)
        )
    return jnp.concatenate(parts, axis=1)


def gather(shards, shapes, groups, devices):
    packed = jnp.concatenate([pack(shard) for shard in shards], axis=0)
    whole = lax.all_gather(packed, axes, axis=0, tiled=False)
    return regroup(whole, devices, groups, shapes)


def scatter(packed, shapes, groups, devices):
    packed = regroup(packed, groups, devices, shapes)
    share = lax.psum_scatter(packed, axes, scatter_dimension=0, tiled=False)
    return split_share(share, shapes, devices)


core_step = 2
plane_steps = (1, 4, 5)
line_steps = (8, 16, 24)


def exchange(values, step):
    return lax.ppermute(values, axes, [(i, i ^ step) for i in range(32)])


def slot_tables(here):
    device = jnp.arange(32, dtype=jnp.int32)
    gap = device ^ here
    slots = ((gap >> 1) & 1) * 16 + ((gap & 1) + ((gap >> 2) & 1) * 2) * 4 + (gap >> 3)
    far = device & 15
    owners = here ^ ((device >> 4) * 2 + (far >> 2 & 1) + (far >> 3) * 4 + (far & 3) * 8)
    return slots.astype(jnp.int32), owners.astype(jnp.int32)


def line_gather(shard):
    return [shard] + [exchange(shard, step) for step in line_steps]


def plane_gather(line):
    line = jnp.stack(line)
    return [line] + [exchange(line, step) for step in plane_steps]


def core_gather(blocks):
    return list(blocks) + [exchange(block, core_step) for block in blocks]


def tree_sum(parts):
    first, second, third, fourth = (part.astype(f32) for part in parts)
    return (first + second) + (third + fourth)


def pair_sums(keep, received):
    return [
        (keep[4 * j : 4 * j + 4].astype(f32) + received[4 * j : 4 * j + 4].astype(f32)).astype(
            bf16
        )
        for j in range(4)
    ]


def plane_exchange(parts):
    return [parts[0]] + [exchange(part, step) for part, step in zip(parts[1:], plane_steps)]


def line_sum(parts):
    moved = [exchange(parts[k + 1], step) for k, step in enumerate(line_steps)]
    return tree_sum([parts[0]] + moved)


def split_share(share, shapes, devices):
    parts = []
    offset = 0
    for rows, columns in shapes:
        size = rows // devices * (columns // lane_tile)
        parts.append(unpack(share[offset : offset + size], rows // devices, columns).astype(f32))
        offset += size
    return parts


def on_device(
    devices,
    direct,
    targets,
    memory,
    mem_lengths,
    buckets,
    cotangent,
    gain_self,
    gain_cross,
    gain_feed,
    self_query,
    self_key,
    self_value,
    self_output,
    cross_query,
    cross_key,
    cross_value,
    cross_output,
    gate_weight,
    up_weight,
    down_weight,
    bias_table,
):
    batch, target_len, width = targets.shape
    bucket_count, head_count = bias_table.shape
    row_count = batch * target_len
    groups = width // group_rows
    square = (width, width)
    feed_width = gate_weight.shape[1]
    feed_shapes = [(width, feed_width), (width, feed_width), (feed_width, width)]

    own_gains = jnp.stack([gain_self, gain_cross, gain_feed])
    output_shards = [self_output, cross_query]
    self_shards = [self_query, self_key, self_value]
    if direct:
        slots, owners = slot_tables(lax.axis_index(axes))
        extra = jnp.pad(own_gains.reshape(1, -1), ((0, 15), (0, lane_tile - own_gains.size)))
        self_line = line_gather(
            jnp.concatenate([pack(shard) for shard in output_shards + self_shards], axis=0)
        )
        memory_line = line_gather(
            jnp.concatenate([pack(cross_key), pack(cross_value), extra], axis=0)
        )
        gate_weight, memory_line = lax.optimization_barrier((gate_weight, memory_line))
        memory_blocks = plane_gather(memory_line)
        memory_blocks, self_line = lax.optimization_barrier((memory_blocks, self_line))
        memory_blocks = core_gather(memory_blocks)
        output_line = [part[: 6 * group_rows] for part in self_line]
        self_blocks = plane_gather([part[6 * group_rows :] for part in self_line])
        hot = (slots[:, None] == jnp.arange(groups)[None, :]).astype(bf16)
        small = [part[:, -16, : own_gains.size] for part in memory_blocks]
        gains = (
            dot(hot, jnp.concatenate(small)).reshape(groups, 3, group_rows).transpose(1, 0, 2)
        ).reshape(3, width)
    else:
        slots, owners = slot_tables(0)

        def halves(shards):
            packed = gather(shards, [square] * len(shards), groups, devices)
            packed = jnp.take(packed, owners, axis=0)
            return [packed[4 * b : 4 * b + 4] for b in range(8)]

        memory_blocks = halves([cross_key, cross_value])
        self_blocks = halves(self_shards)
        output_blocks = halves(output_shards)
        gains = lax.all_gather(own_gains, axes, axis=1, tiled=True).astype(f32)
    packed_feed = gather(
        [gate_weight, up_weight, down_weight, cross_output],
        feed_shapes + [square],
        groups,
        devices,
    )

    pad = pair_width - target_len
    bucket_hot = (
        buckets[:, :, None] == lax.broadcasted_iota(jnp.int32, (1, 1, bucket_count), 2)
    ).reshape(target_len * target_len, bucket_count)
    bias = (
        dot(bucket_hot.astype(bf16), bias_table)
        .reshape(target_len, target_len, head_count)
        .transpose(2, 0, 1)
    )
    causal = lax.broadcasted_iota(jnp.int32, (target_len, target_len), 1) <= lax.broadcasted_iota(
        jnp.int32, (target_len, target_len), 0
    )
    bias = jnp.where(causal, bias, masked_out)
    bias = jnp.pad(bias, ((0, 0), (0, 0), (0, pad)), constant_values=masked_out)
    bias = (
        bias.reshape(head_count // 2, 2, target_len, pair_width)
        .transpose(0, 2, 1, 3)
        .reshape(head_count // 2, target_len, 2 * pair_width)
    )
    wide_buckets = jnp.pad(buckets, ((0, 0), (0, pad)), constant_values=-1)
    target_rows = targets.reshape(row_count, width)
    cot_rows = cotangent.reshape(row_count, width)

    mem_keys, mem_values, memory_weight = project_memory(
        mem_lengths, owners, memory, memory_blocks
    )
    if direct:
        received, output_line, memory_weight = lax.optimization_barrier(
            (self_blocks[1:], output_line, memory_weight)
        )
        self_blocks = core_gather(self_blocks[:1] + received)
        output_blocks = plane_gather(output_line)
    normed_one, queries, key_rows, value_rows, self_context, self_weight = self_attend(
        target_len, owners, target_rows, bias, gains[0:1], self_blocks
    )
    if direct:
        received, self_context = lax.optimization_barrier((output_blocks[1:], self_context))
        output_blocks = core_gather(output_blocks[:1] + received)
    after_self, normed_two, side, output_weight = self_project(
        owners, target_rows, self_context, gains[1:2], output_blocks
    )
    cross_context, weights = cross_forward(mem_lengths, side, mem_keys, mem_values, head_count)
    outputs, grad_after_cross, grad_context, grad_gain_feed, feed_grads = feed_both(
        after_self, cross_context, cot_rows, gains[2:3], packed_feed
    )
    share_gate, share_up, share_down, share_cross_output = scatter(
        feed_grads, feed_shapes + [square], groups, devices
    )
    grad_side, grad_mem_keys, grad_mem_values = cross_backward(
        mem_lengths, grad_context, cross_context, side, mem_keys, mem_values, weights
    )
    grad_total, grad_self_context, grad_gain_cross, output_keep, output_send = (
        self_output_backward(
            owners,
            grad_side,
            after_self,
            grad_after_cross,
            normed_two,
            self_context,
            output_weight,
            gains[1:2],
        )
    )
    target_grad, self_keep, self_send = self_backward(
        target_len,
        bucket_count,
        owners,
        (
            grad_self_context,
            grad_total,
            normed_one,
            queries,
            key_rows,
            value_rows,
            target_rows,
            self_weight,
            bias,
            wide_buckets,
            gains[0:1],
            grad_gain_cross,
            grad_gain_feed,
        ),
    )
    if direct:
        output_parts = pair_sums(output_keep, exchange(output_send, core_step))
        grad_mem_keys, self_keep, output_parts = lax.optimization_barrier(
            (grad_mem_keys, self_keep, output_parts)
        )
    memory_keep, memory_send = memory_weight_grads(
        mem_lengths, owners, memory, grad_mem_keys, grad_mem_values
    )
    if direct:
        output_parts = plane_exchange(output_parts)
        self_parts = pair_sums(self_keep, exchange(self_send, core_step))
        memory_weight, memory_keep, self_parts, output_parts = lax.optimization_barrier(
            (memory_weight, memory_keep, self_parts, output_parts)
        )
    memory_grad = memory_gradient(mem_lengths, grad_mem_keys, grad_mem_values, memory_weight)
    if direct:
        self_parts = plane_exchange(self_parts)
        memory_received = exchange(memory_send, core_step)
        memory_grad, memory_received = lax.optimization_barrier((memory_grad, memory_received))
        memory_grad, self_parts = lax.optimization_barrier((memory_grad, self_parts))
        memory_parts = plane_exchange(pair_sums(memory_keep, memory_received))
        joint = line_sum(
            jnp.concatenate(
                [tree_sum(output_parts).astype(bf16), tree_sum(self_parts).astype(bf16)], axis=1
            )
        )
        output_share = joint[: 6 * group_rows]
        self_share = joint[6 * group_rows :]
        memory_share = line_sum(tree_sum(memory_parts).astype(bf16))
        share_output, share_cross_query = split_share(output_share, [square] * 2, devices)
        share_query, share_key, share_value = split_share(self_share, [square] * 3, devices)
        share_cross_key, share_cross_value = split_share(memory_share, [square] * 2, devices)
        own_grads = self_share[9 * group_rows : 9 * group_rows + 3, : width // devices]
        table = self_share[9 * group_rows + 8 : 9 * group_rows + 10]
    else:

        def reduced(keep, send, count):
            packed = jnp.take(jnp.concatenate([keep, send]), slots, axis=0)
            return scatter(
                packed[:, : 3 * count * group_rows], [square] * count, groups, devices
            )

        share_output, share_cross_query = reduced(output_keep, output_send, 2)
        share_query, share_key, share_value = reduced(self_keep, self_send, 3)
        share_cross_key, share_cross_value = reduced(memory_keep, memory_send, 2)
        small = jnp.take(jnp.concatenate([self_keep, self_send]), slots, axis=0)
        small = small[:, 9 * group_rows :].astype(f32)
        grad_gains = small[:, :3, :group_rows].transpose(1, 0, 2).reshape(-1)
        small = jnp.concatenate([grad_gains, small[0, 8:10].reshape(-1)])
        small = jnp.sum(lax.all_gather(small, axes, axis=0, tiled=False), axis=0)
        own_grads = lax.dynamic_index_in_dim(
            small[: 3 * width].reshape(3, devices, -1), lax.axis_index(axes), 1, False
        )
        table = small[3 * width :].reshape(2, lane_tile)
    table_grad = (
        table[:, : bucket_count * head_count // 2]
        .reshape(2, head_count // 2, bucket_count)
        .transpose(2, 1, 0)
        .reshape(bucket_count, head_count)
    )

    return (
        outputs.reshape(targets.shape),
        target_grad.reshape(targets.shape),
        memory_grad,
        own_grads[0],
        own_grads[1],
        own_grads[2],
        share_query,
        share_key,
        share_value,
        share_output,
        share_cross_query,
        share_cross_key,
        share_cross_value,
        share_cross_output,
        share_gate,
        share_up,
        share_down,
        table_grad,
    )


def solution(mesh):
    devices = mesh.shape["dp"] * mesh.shape["seq"]
    direct = mesh.shape["dp"] == 16 and mesh.shape["seq"] == 2
    rows = P(axes, None, None)
    flat = P(axes)
    weight = P(axes, None)

    def body(*arguments):
        return on_device(devices, direct, *arguments)

    return jax.shard_map(
        body,
        mesh=mesh,
        in_specs=(rows, rows, flat, P(), rows, flat, flat, flat) + (weight,) * 11 + (P(),),
        out_specs=(rows, rows, rows, flat, flat, flat) + (weight,) * 11 + (P(),),
        check_vma=False,
    )
```

```python
import math

import jax
import jax.numpy as jnp
from jax import lax
from jax.experimental import pallas as pl
from jax.experimental.pallas import tpu as pltpu
from jax.sharding import PartitionSpec as P

epsilon = 1e-06
masked_out = -1e30
bf16 = jnp.bfloat16
f32 = jnp.float32
axes = ("dp", "seq")
lane_tile = 256
group_rows = 24
pair_width = 128
pair_group = 3
NN = (((1,), (0,)), ((), ()))
NT = (((1,), (1,)), ((), ()))
TN = (((0,), (0,)), ((), ()))
gelu_scale = math.sqrt(2.0 / math.pi)
gelu_cubic = 0.044715


def dot(left_side, right_side, dims=NN):
    return lax.dot_general(left_side, right_side, dims, preferred_element_type=f32)


def params():
    return pltpu.CompilerParams(vmem_limit_bytes=60 * 1024 * 1024)


def cost(flops, size, exps=0):
    return pl.CostEstimate(
        flops=int(flops), bytes_accessed=int(size), transcendentals=int(exps)
    )


def column_tile(packed_ref, index):
    tile = packed_ref[:, index * group_rows : (index + 1) * group_rows, :]
    return tile.reshape(tile.shape[0] * group_rows, lane_tile)


def lane_halves(rows):
    lanes = lax.broadcasted_iota(jnp.int32, (rows, pair_width), 1)
    return lanes < pair_width // 2


def project(rows, packed_ref, base, tiles):
    return [dot(rows, column_tile(packed_ref, base + t)) for t in range(tiles)]


def through(rows, packed_ref, base, tiles):
    total = None
    for t in range(tiles):
        part = dot(
            rows[:, t * lane_tile : (t + 1) * lane_tile], column_tile(packed_ref, base + t), NT
        )
        total = part if total is None else total + part
    return total


def assemble(owners, block_refs, weight_ref):
    slots = block_refs[0].shape[0]
    for first in range(0, len(block_refs), 2):
        even_ref, odd_ref = block_refs[first : first + 2]

        def place(slot, carry):
            owner = owners[first * slots + slot]
            swap = (owner & 1) == 1
            rows = pl.ds(pl.multiple_of((owner >> 1) * (2 * group_rows), 16), 2 * group_rows)
            for t in range(weight_ref.shape[1] // lane_tile):
                part = slice(t * group_rows, (t + 1) * group_rows)
                cols = slice(t * lane_tile, (t + 1) * lane_tile)
                one = even_ref[slot, part, :]
                two = odd_ref[slot, part, :]
                weight_ref[rows, cols] = jnp.concatenate(
                    [jnp.where(swap, two, one), jnp.where(swap, one, two)], axis=0
                )
            return carry

        lax.fori_loop(0, slots, place, 0)


def put_slots(owners, keep_ref, send_ref, stage_ref, extra=None):
    half = keep_ref.shape[0]
    tiles = stage_ref.shape[1] // lane_tile

    def place(slot, carry):
        for offset, out_ref in ((0, keep_ref), (half, send_ref)):
            owner = owners[slot + offset]
            rows = pl.ds(pl.multiple_of(owner * group_rows, 8), group_rows)
            parts = [
                stage_ref[rows, t * lane_tile : (t + 1) * lane_tile] for t in range(tiles)
            ]
            if extra is not None:
                parts.append(extra(owner))
            for t in range(0, len(parts), 2):
                both = jnp.concatenate(parts[t : t + 2], axis=0).astype(bf16)
                start = t * group_rows
                out_ref[slot, start : start + both.shape[0], :] = both
        return carry

    lax.fori_loop(0, half, place, 0)


def norm_scale(values):
    return lax.rsqrt(jnp.mean(values * values, axis=-1, keepdims=True) + epsilon)


def norm_pullback(values, gain_row, grad_in):
    inverse = norm_scale(values)
    weighted = grad_in * gain_row
    inner = jnp.mean(weighted * values, axis=-1, keepdims=True)
    grad_values = inverse * weighted - values * (inverse * inverse * inverse * inner)
    grad_gain = jnp.sum(grad_in * values * inverse, axis=0, keepdims=True)
    return grad_values, grad_gain


def memory_kernel(lengths, owners, memory_ref, *refs):
    block_refs = refs[:-3]
    keys_ref, values_ref, weight_ref = refs[-3:]
    seq = pl.program_id(0)
    memory_len = memory_ref.shape[1]

    @pl.when(seq == 0)
    def _():
        assemble(owners, block_refs, weight_ref)

    def fill(count):
        rows = memory_ref[0, :count, :]
        for base, out_ref in ((0, keys_ref), (3, values_ref)):
            for t in range(3):
                out_ref[0, :count, t * lane_tile : (t + 1) * lane_tile] = dot(
                    rows, weight_ref[:, (base + t) * lane_tile : (base + t + 1) * lane_tile]
                ).astype(bf16)

    @pl.when(lengths[seq] > memory_len // 2)
    def _():
        fill(memory_len)

    @pl.when(lengths[seq] <= memory_len // 2)
    def _():
        fill(memory_len // 2)


def project_memory(mem_lengths, owners, memory, blocks):
    batch, memory_len, width = memory.shape
    block = pl.BlockSpec((1, memory_len, width), lambda b, n, s: (b, 0, 0))
    return pl.pallas_call(
        memory_kernel,
        out_shape=[jax.ShapeDtypeStruct(memory.shape, bf16)] * 2
        + [jax.ShapeDtypeStruct((width, 2 * width), bf16)],
        grid_spec=pltpu.PrefetchScalarGridSpec(
            num_scalar_prefetch=2,
            grid=(batch,),
            in_specs=[block] + [pl.BlockSpec(blocks[0].shape, lambda b, n, s: (0, 0, 0))] * len(blocks),
            out_specs=[block, block, pl.BlockSpec((width, 2 * width), lambda b, n, s: (0, 0))],
        ),
        compiler_params=params(),
        cost_estimate=cost(4 * memory.size * width, 6 * memory.size),
        name="memory_project",
    )(mem_lengths, owners, memory, *blocks)


def stacked_pair(rows, half, pad):
    zero = jnp.zeros_like(rows)
    gap = jnp.zeros((pad, pair_width), rows.dtype)
    return jnp.concatenate(
        [jnp.where(half, rows, zero), gap, jnp.where(half, zero, rows), gap], axis=0
    )


def pair_softmax(scores):
    parts = []
    for h in range(2):
        one = scores[:, h * pair_width : (h + 1) * pair_width]
        terms = jnp.exp(one - jnp.max(one, axis=-1, keepdims=True))
        parts.append(terms * (1.0 / jnp.sum(terms, axis=-1, keepdims=True)))
    return parts


def self_attend_kernel(
    target_len,
    block_refs,
    owners,
    targets_ref,
    bias_ref,
    gain_self_ref,
    normed_one_ref,
    queries_ref,
    keys_ref,
    values_ref,
    context_ref,
    weight_ref,
):
    width = targets_ref.shape[1]
    assemble(owners, block_refs, weight_ref)
    inputs = targets_ref[...].astype(f32)
    normed_one = (inputs * norm_scale(inputs) * gain_self_ref[...]).astype(bf16)
    normed_one_ref[...] = normed_one
    for index, out_ref in ((0, queries_ref), (1, keys_ref), (2, values_ref)):
        out_ref[...] = dot(
            normed_one, weight_ref[:, index * width : (index + 1) * width]
        ).astype(bf16)
    half = lane_halves(target_len)
    pad = pair_width - target_len
    pairs = bias_ref.shape[0]
    columns = [slice(p * pair_width, (p + 1) * pair_width) for p in range(pairs)]

    def attend(seq, carry):
        rows = pl.ds(pl.multiple_of(seq * target_len, 32), target_len)
        scores = [
            dot(queries_ref[rows, cols], stacked_pair(keys_ref[rows, cols], half, pad), NT)
            + bias_ref[p]
            for p, cols in enumerate(columns)
        ]
        probs = [
            jnp.concatenate(pair_softmax(score), axis=1).astype(bf16) for score in scores
        ]
        for p, cols in enumerate(columns):
            value_stack = stacked_pair(values_ref[rows, cols], half, pad)
            context_ref[rows, cols] = dot(probs[p], value_stack).astype(bf16)
        return carry

    lax.fori_loop(0, targets_ref.shape[0] // target_len, attend, 0)


def self_attend(target_len, owners, targets, bias, gain_self, blocks):
    width = targets.shape[1]
    whole = pl.BlockSpec(memory_space=pltpu.VMEM)
    low = jax.ShapeDtypeStruct(targets.shape, bf16)

    def body(*refs):
        stop = 4 + len(blocks)
        self_attend_kernel(target_len, refs[4:stop], *refs[:4], *refs[stop:])

    return pl.pallas_call(
        body,
        out_shape=[low] * 5 + [jax.ShapeDtypeStruct((width, 3 * width), bf16)],
        in_specs=[pl.BlockSpec(memory_space=pltpu.SMEM)] + [whole] * (3 + len(blocks)),
        compiler_params=params(),
        cost_estimate=cost(16 * targets.size * width, 12 * targets.size),
        name="self_attend",
    )(owners, targets, bias, gain_self, *blocks)


def self_project_kernel(
    block_refs,
    owners,
    targets_ref,
    context_ref,
    gain_cross_ref,
    after_ref,
    normed_two_ref,
    side_ref,
    weight_ref,
):
    width = targets_ref.shape[1]
    assemble(owners, block_refs, weight_ref)
    after = targets_ref[...].astype(f32) + dot(context_ref[...], weight_ref[:, :width])
    after_ref[...] = after
    normed_two = (after * norm_scale(after) * gain_cross_ref[...]).astype(bf16)
    normed_two_ref[...] = normed_two
    side_ref[...] = dot(normed_two, weight_ref[:, width:]).astype(bf16)


def self_project(owners, targets, context, gain_cross, blocks):
    width = targets.shape[1]
    whole = pl.BlockSpec(memory_space=pltpu.VMEM)
    low = jax.ShapeDtypeStruct(targets.shape, bf16)

    def body(*refs):
        stop = 4 + len(blocks)
        self_project_kernel(refs[4:stop], *refs[:4], *refs[stop:])

    return pl.pallas_call(
        body,
        out_shape=[
            jax.ShapeDtypeStruct(targets.shape, f32),
            low,
            low,
            jax.ShapeDtypeStruct((width, 2 * width), bf16),
        ],
        in_specs=[pl.BlockSpec(memory_space=pltpu.SMEM)] + [whole] * (3 + len(blocks)),
        compiler_params=params(),
        cost_estimate=cost(4 * targets.size * width, 12 * targets.size),
        name="self_project",
    )(owners, targets, context, gain_cross, *blocks)


def masked_stack(rows, half):
    zero = jnp.zeros_like(rows)
    return jnp.concatenate([jnp.where(half, rows, zero), jnp.where(half, zero, rows)], axis=0)


def cross_forward_kernel(lengths, side_ref, keys_ref, values_ref, context_ref, weights_ref):
    seq = pl.program_id(0)
    target_len, width = side_ref.shape
    memory_len = keys_ref.shape[1]
    half = lane_halves(target_len)

    pairs = width // pair_width
    columns = [slice(p * pair_width, (p + 1) * pair_width) for p in range(pairs)]

    def attend(count):
        def pair_scores(p):
            stack = masked_stack(side_ref[:, columns[p]], half)
            return dot(stack, keys_ref[0, :count, columns[p]], NT)

        coming = pair_scores(0)
        for p, cols in enumerate(columns):
            scores = coming
            if p + 1 < pairs:
                coming = pair_scores(p + 1)
            terms = jnp.exp(scores - jnp.max(scores, axis=-1, keepdims=True))
            scale = 1.0 / jnp.sum(terms, axis=-1, keepdims=True)
            weights = (terms * scale).astype(bf16)
            weights_ref[0, 2 * target_len * p : 2 * target_len * (p + 1), :count] = weights
            both = dot(weights, values_ref[0, :count, cols])
            context_ref[:, cols] = jnp.where(half, both[:target_len], both[target_len:]).astype(
                bf16
            )

    @pl.when(lengths[seq] > memory_len // 2)
    def _():
        attend(memory_len)

    @pl.when(lengths[seq] <= memory_len // 2)
    def _():
        attend(memory_len // 2)


def cross_forward(mem_lengths, side, mem_keys, mem_values, head_count):
    batch, memory_len, width = mem_keys.shape
    target_len = side.shape[0] // batch
    rows = pl.BlockSpec((target_len, width), lambda b, n: (b, 0))
    memory = pl.BlockSpec((1, memory_len, width), lambda b, n: (b, 0, 0))
    weights = pl.BlockSpec((1, head_count * target_len, memory_len), lambda b, n: (b, 0, 0))
    return pl.pallas_call(
        cross_forward_kernel,
        out_shape=[
            jax.ShapeDtypeStruct(side.shape, bf16),
            jax.ShapeDtypeStruct((batch, head_count * target_len, memory_len), bf16),
        ],
        grid_spec=pltpu.PrefetchScalarGridSpec(
            num_scalar_prefetch=1,
            grid=(batch,),
            in_specs=[rows, memory, memory],
            out_specs=[rows, weights],
        ),
        compiler_params=params(),
        cost_estimate=cost(16 * side.size * memory_len, 6 * mem_keys.size, batch * head_count * target_len * memory_len),
        name="cross_forward",
    )(mem_lengths, side, mem_keys, mem_values)


def feed_kernel(
    after_ref,
    context_ref,
    cot_ref,
    gain_ref,
    side_output_ref,
    gate_ref,
    up_ref,
    down_ref,
    outputs_ref,
    grad_after_ref,
    grad_context_ref,
    grad_gain_ref,
    packed_ref,
    after_cross_ref,
    normed_ref,
    out_total_ref,
    grad_normed_ref,
):
    step = pl.program_id(0)
    steps = pl.num_programs(0)

    @pl.when(step == 0)
    def _():
        after_cross = after_ref[...] + jnp.concatenate(
            project(context_ref[...], side_output_ref, 0, 3), axis=1
        )
        after_cross_ref[...] = after_cross
        normed_ref[...] = (after_cross * norm_scale(after_cross) * gain_ref[...]).astype(bf16)
        out_total_ref[...] = after_cross
        grad_normed_ref[...] = jnp.zeros_like(grad_normed_ref)

    normed = normed_ref[...]
    cot = cot_ref[...]
    gate_weight = column_tile(gate_ref, 0)
    up_weight = column_tile(up_ref, 0)
    share = down_ref.shape[1] // 3
    owners = down_ref.shape[0]
    down_weight = jnp.concatenate(
        [
            down_ref[:, c * share : (c + 1) * share, :].reshape(owners * share, lane_tile)
            for c in range(3)
        ],
        axis=1,
    )
    gate = dot(normed, gate_weight)
    up = dot(normed, up_weight)
    grad_hidden = dot(cot, down_weight, NT)
    square = gate * gate
    tanh = jnp.tanh(gelu_scale * (gate + gelu_cubic * (square * gate)))
    half_sum = 0.5 * (1.0 + tanh)
    active = gate * half_sum
    slope = half_sum + 0.5 * gate * (1.0 - tanh * tanh) * (
        gelu_scale * (1.0 + 3.0 * gelu_cubic * square)
    )
    hidden = (active * up).astype(bf16)
    grad_gate = (grad_hidden * up * slope).astype(bf16)
    grad_up = (grad_hidden * active).astype(bf16)
    out_total_ref[...] += dot(hidden, down_weight)
    grad_normed_ref[...] += dot(grad_gate, gate_weight, NT) + dot(grad_up, up_weight, NT)
    groups = packed_ref.shape[0]

    def put(base, value):
        packed_ref[:, pl.ds(base + step * group_rows, group_rows), :] = value.reshape(
            groups, group_rows, lane_tile
        ).astype(bf16)

    put(0, dot(normed, grad_gate, TN))
    put(steps * group_rows, dot(normed, grad_up, TN))
    down_base = 2 * steps * group_rows
    for c in range(3):
        part = dot(hidden, cot[:, c * lane_tile : (c + 1) * lane_tile], TN)
        packed_ref[
            pl.ds(step * owners, owners), down_base + c * share : down_base + (c + 1) * share, :
        ] = part.reshape(owners, share, lane_tile).astype(bf16)

    @pl.when(step == steps - 1)
    def _():
        outputs_ref[...] = out_total_ref[...].astype(bf16)
        grad_in, grad_gain = norm_pullback(
            after_cross_ref[...], gain_ref[...], grad_normed_ref[...]
        )
        grad_gain_ref[...] = grad_gain
        grad_after = cot_ref[...].astype(f32) + grad_in
        grad_after_ref[...] = grad_after
        low = grad_after.astype(bf16)
        for c in range(3):
            cols = slice(c * lane_tile, (c + 1) * lane_tile)
            start = 3 * down_base // 2 + c * group_rows
            packed_ref[:, start : start + group_rows, :] = (
                dot(context_ref[...], low[:, cols], TN)
                .reshape(groups, group_rows, lane_tile)
                .astype(bf16)
            )
        grad_context_ref[...] = through(low, side_output_ref, 0, 3).astype(bf16)


def feed_both(after_self, context, cotangent, gain, packed_feed):
    rows, width = context.shape
    groups, feed_rows, _ = packed_feed.shape
    steps = feed_rows // (3 * group_rows) - 1
    owners = groups // steps
    whole = lambda f: (0, 0)
    full = pl.BlockSpec((rows, width), whole)
    tile = (groups, group_rows, lane_tile)
    return pl.pallas_call(
        feed_kernel,
        out_shape=[
            jax.ShapeDtypeStruct((rows, width), bf16),
            jax.ShapeDtypeStruct((rows, width), f32),
            jax.ShapeDtypeStruct((rows, width), bf16),
            jax.ShapeDtypeStruct((1, width), f32),
            jax.ShapeDtypeStruct((groups, feed_rows, lane_tile), bf16),
        ],
        grid=(steps,),
        in_specs=[
            full,
            full,
            full,
            pl.BlockSpec((1, width), whole),
            pl.BlockSpec((groups, 3 * group_rows, lane_tile), lambda f: (0, steps, 0)),
            pl.BlockSpec(tile, lambda f: (0, f, 0)),
            pl.BlockSpec(tile, lambda f: (0, steps + f, 0)),
            pl.BlockSpec((owners, steps * group_rows, lane_tile), lambda f: (f, 2, 0)),
        ],
        out_specs=[
            full,
            full,
            full,
            pl.BlockSpec((1, width), whole),
            pl.BlockSpec((groups, feed_rows, lane_tile), lambda f: (0, 0, 0)),
        ],
        scratch_shapes=[
            pltpu.VMEM((rows, width), f32),
            pltpu.VMEM((rows, width), bf16),
            pltpu.VMEM((rows, width), f32),
            pltpu.VMEM((rows, width), f32),
        ],
        compiler_params=params(),
        cost_estimate=cost(18 * rows * width * steps * lane_tile, 30 * rows * width),
        name="feed_both",
    )(after_self, context, cotangent, gain, packed_feed, packed_feed, packed_feed, packed_feed)


def cross_backward_kernel(
    lengths,
    grad_ref,
    context_ref,
    side_ref,
    keys_ref,
    values_ref,
    weights_ref,
    grad_side_ref,
    grad_keys_ref,
    grad_values_ref,
):
    seq = pl.program_id(0)
    target_len, width = side_ref.shape
    memory_len = keys_ref.shape[1]
    half = lane_halves(target_len)

    pairs = width // pair_width
    columns = [slice(p * pair_width, (p + 1) * pair_width) for p in range(pairs)]

    def attend(count):
        def pair_start(p):
            cols = columns[p]
            grad_stack = masked_stack(grad_ref[:, cols], half)
            return grad_stack, dot(grad_stack, values_ref[0, :count, cols], NT)

        coming = pair_start(0)
        for p, cols in enumerate(columns):
            grad_stack, grad_probs = coming
            weights = weights_ref[0, 2 * target_len * p : 2 * target_len * (p + 1), :count]
            if p + 1 < pairs:
                coming = pair_start(p + 1)
            query_stack = masked_stack(side_ref[:, cols], half)
            product = grad_ref[:, cols].astype(f32) * context_ref[:, cols].astype(f32)
            inner = jnp.sum(masked_stack(product, half), axis=-1, keepdims=True)
            grad_scores = (weights.astype(f32) * (grad_probs - inner)).astype(bf16)
            grad_values_ref[0, cols, :count] = dot(grad_stack, weights, TN).astype(bf16)
            both = dot(grad_scores, keys_ref[0, :count, cols])
            grad_side_ref[:, cols] = jnp.where(half, both[:target_len], both[target_len:]).astype(
                bf16
            )
            grad_keys_ref[0, cols, :count] = dot(query_stack, grad_scores, TN).astype(bf16)

    @pl.when(lengths[seq] > memory_len // 2)
    def _():
        attend(memory_len)

    @pl.when(lengths[seq] <= memory_len // 2)
    def _():
        attend(memory_len // 2)


def cross_backward(mem_lengths, grad_context, context, side, mem_keys, mem_values, weights):
    batch, memory_len, width = mem_keys.shape
    target_len = side.shape[0] // batch
    rows = pl.BlockSpec((target_len, width), lambda b, n: (b, 0))
    memory = pl.BlockSpec((1, memory_len, width), lambda b, n: (b, 0, 0))
    turned = pl.BlockSpec((1, width, memory_len), lambda b, n: (b, 0, 0))
    return pl.pallas_call(
        cross_backward_kernel,
        out_shape=[jax.ShapeDtypeStruct(side.shape, bf16)]
        + [jax.ShapeDtypeStruct((batch, width, memory_len), bf16)] * 2,
        grid_spec=pltpu.PrefetchScalarGridSpec(
            num_scalar_prefetch=1,
            grid=(batch,),
            in_specs=[
                rows,
                rows,
                rows,
                memory,
                memory,
                pl.BlockSpec((1,) + weights.shape[1:], lambda b, n: (b, 0, 0)),
            ],
            out_specs=[rows, turned, turned],
        ),
        compiler_params=params(),
        cost_estimate=cost(32 * side.size * memory_len, 10 * mem_keys.size),
        name="cross_backward",
    )(mem_lengths, grad_context, context, side, mem_keys, mem_values, weights)


def memory_weight_kernel(
    lengths,
    owners,
    memory_ref,
    grad_keys_ref,
    grad_values_ref,
    keep_ref,
    send_ref,
    key_total_ref,
    value_total_ref,
    stage_ref,
):
    seq = pl.program_id(0)
    memory_len = memory_ref.shape[1]

    @pl.when(seq == 0)
    def _():
        key_total_ref[...] = jnp.zeros_like(key_total_ref)
        value_total_ref[...] = jnp.zeros_like(value_total_ref)

    def add(count):
        rows = memory_ref[0, :count, :]
        key_total_ref[...] += dot(grad_keys_ref[0, :, :count], rows)
        value_total_ref[...] += dot(grad_values_ref[0, :, :count], rows)

    @pl.when(lengths[seq] > memory_len // 2)
    def _():
        add(memory_len)

    @pl.when(lengths[seq] <= memory_len // 2)
    def _():
        add(memory_len // 2)

    @pl.when(seq == pl.num_programs(0) - 1)
    def _():
        width = key_total_ref.shape[0]
        for base, total_ref in ((0, key_total_ref), (width, value_total_ref)):
            for start in range(0, width, lane_tile):
                stage_ref[:, base + start : base + start + lane_tile] = jnp.transpose(
                    total_ref[start : start + lane_tile, :]
                )
        put_slots(owners, keep_ref, send_ref, stage_ref)


def memory_weight_grads(mem_lengths, owners, memory, grad_keys, grad_values):
    batch, memory_len, width = memory.shape
    block = pl.BlockSpec((1, memory_len, width), lambda b, n, o: (b, 0, 0))
    turned = pl.BlockSpec((1, width, memory_len), lambda b, n, o: (b, 0, 0))
    half = (owners.shape[0] // 2, 2 * width // lane_tile * group_rows, lane_tile)
    return pl.pallas_call(
        memory_weight_kernel,
        out_shape=[jax.ShapeDtypeStruct(half, bf16)] * 2,
        grid_spec=pltpu.PrefetchScalarGridSpec(
            num_scalar_prefetch=2,
            grid=(batch,),
            in_specs=[block, turned, turned],
            out_specs=[pl.BlockSpec(half, lambda b, n, o: (0, 0, 0))] * 2,
            scratch_shapes=[pltpu.VMEM((width, width), f32)] * 2
            + [pltpu.VMEM((width, 2 * width), f32)],
        ),
        compiler_params=params(),
        cost_estimate=cost(4 * memory.size * width, 6 * memory.size),
        name="memory_weight_grads",
    )(mem_lengths, owners, memory, grad_keys, grad_values)


def memory_grad_kernel(
    lengths, grad_keys_ref, grad_values_ref, weight_ref, out_ref, key_turned_ref, value_turned_ref
):
    seq = pl.program_id(0)
    memory_len = out_ref.shape[1]

    @pl.when(seq == 0)
    def _():
        for base, turned_ref in ((0, key_turned_ref), (3, value_turned_ref)):
            for t in range(3):
                turned_ref[t * lane_tile : (t + 1) * lane_tile, :] = jnp.transpose(
                    weight_ref[:, (base + t) * lane_tile : (base + t + 1) * lane_tile]
                )

    def fill(count):
        out_ref[0, :count, :] = (
            dot(grad_keys_ref[0, :, :count], key_turned_ref[...], TN)
            + dot(grad_values_ref[0, :, :count], value_turned_ref[...], TN)
        ).astype(bf16)

    @pl.when(lengths[seq] > memory_len // 2)
    def _():
        fill(memory_len)

    @pl.when(lengths[seq] <= memory_len // 2)
    def _():
        fill(memory_len // 2)
        out_ref[0, memory_len // 2 :, :] = jnp.zeros_like(out_ref[0, memory_len // 2 :, :])


def memory_gradient(mem_lengths, grad_keys, grad_values, weight):
    batch, width, memory_len = grad_keys.shape
    turned = pl.BlockSpec((1, width, memory_len), lambda b, n: (b, 0, 0))
    return pl.pallas_call(
        memory_grad_kernel,
        out_shape=jax.ShapeDtypeStruct((batch, memory_len, width), bf16),
        grid_spec=pltpu.PrefetchScalarGridSpec(
            num_scalar_prefetch=1,
            grid=(batch,),
            in_specs=[turned, turned, pl.BlockSpec(weight.shape, lambda b, n: (0, 0))],
            out_specs=pl.BlockSpec((1, memory_len, width), lambda b, n: (b, 0, 0)),
            scratch_shapes=[pltpu.VMEM((width, width), bf16)] * 2,
        ),
        compiler_params=params(),
        cost_estimate=cost(4 * grad_keys.size * width, 6 * grad_keys.size),
        name="memory_grad",
    )(mem_lengths, grad_keys, grad_values, weight)


def self_output_kernel(
    owners,
    grad_side_ref,
    after_ref,
    grad_after_ref,
    normed_two_ref,
    context_ref,
    weight_ref,
    gain_cross_ref,
    grad_total_ref,
    grad_context_ref,
    grad_gain_ref,
    keep_ref,
    send_ref,
    stage_ref,
):
    width = after_ref.shape[1]
    grad_side = grad_side_ref[...]
    grad_normed = dot(grad_side, weight_ref[:, width:], NT)
    grad_in, grad_gain = norm_pullback(after_ref[...], gain_cross_ref[...], grad_normed)
    grad_gain_ref[...] = grad_gain
    grad_total = grad_after_ref[...] + grad_in
    grad_total_ref[...] = grad_total
    low = grad_total.astype(bf16)
    stage_ref[:, :width] = dot(context_ref[...], low, TN)
    stage_ref[:, width:] = dot(normed_two_ref[...], grad_side, TN)
    grad_context_ref[...] = dot(low, weight_ref[:, :width], NT).astype(bf16)
    put_slots(owners, keep_ref, send_ref, stage_ref)


def self_output_backward(
    owners, grad_side, after, grad_after, normed_two, context, weight, gain_cross
):
    rows, width = after.shape
    half = (owners.shape[0] // 2, 2 * width // lane_tile * group_rows, lane_tile)
    whole = pl.BlockSpec(memory_space=pltpu.VMEM)
    return pl.pallas_call(
        self_output_kernel,
        out_shape=[
            jax.ShapeDtypeStruct((rows, width), f32),
            jax.ShapeDtypeStruct((rows, width), bf16),
            jax.ShapeDtypeStruct((1, width), f32),
            jax.ShapeDtypeStruct(half, bf16),
            jax.ShapeDtypeStruct(half, bf16),
        ],
        in_specs=[pl.BlockSpec(memory_space=pltpu.SMEM)] + [whole] * 7,
        scratch_shapes=[pltpu.VMEM((width, 2 * width), f32)],
        compiler_params=params(),
        cost_estimate=cost(8 * after.size * width, 20 * after.size),
        name="self_output_backward",
    )(owners, grad_side, after, grad_after, normed_two, context, weight, gain_cross)


def self_backward_kernel(
    target_len,
    bucket_count,
    owners,
    grad_context_ref,
    grad_total_ref,
    normed_one_ref,
    queries_ref,
    keys_ref,
    values_ref,
    targets_ref,
    weight_ref,
    bias_ref,
    buckets_ref,
    gain_self_ref,
    grad_gain_cross_ref,
    grad_gain_feed_ref,
    target_grad_ref,
    keep_ref,
    send_ref,
    grad_queries_ref,
    grad_keys_ref,
    grad_values_ref,
    score_total_ref,
    stage_ref,
    table_ref,
    gains_ref,
):
    width = targets_ref.shape[1]
    half = lane_halves(target_len)
    pad = pair_width - target_len
    pairs = bias_ref.shape[0]
    columns = [slice(p * pair_width, (p + 1) * pair_width) for p in range(pairs)]
    score_total_ref[...] = jnp.zeros_like(score_total_ref)

    def pick(values):
        return jnp.where(
            half, values[:target_len], values[pair_width : pair_width + target_len]
        ).astype(bf16)

    def attend(seq, carry):
        rows = pl.ds(pl.multiple_of(seq * target_len, 32), target_len)
        for first in range(0, pairs, pair_group):
            chosen = range(first, first + pair_group)
            key_stacks = [stacked_pair(keys_ref[rows, columns[p]], half, pad) for p in chosen]
            scores = [
                dot(queries_ref[rows, columns[p]], stack, NT) + bias_ref[p]
                for p, stack in zip(chosen, key_stacks)
            ]
            grad_probs = [
                dot(
                    grad_context_ref[rows, columns[p]],
                    stacked_pair(values_ref[rows, columns[p]], half, pad),
                    NT,
                )
                for p in chosen
            ]
            probs = [pair_softmax(score) for score in scores]
            grad_scores = []
            for prob, grad_prob in zip(probs, grad_probs):
                parts = []
                for h in range(2):
                    one = grad_prob[:, h * pair_width : (h + 1) * pair_width]
                    inner = jnp.sum(one * prob[h], axis=-1, keepdims=True)
                    parts.append(prob[h] * (one - inner))
                grad_scores.append(jnp.concatenate(parts, axis=1).astype(bf16))
            for p, stack, prob, grad_score in zip(chosen, key_stacks, probs, grad_scores):
                cols = columns[p]
                weights = jnp.concatenate(prob, axis=1).astype(bf16)
                score_total_ref[p] += grad_score.astype(f32)
                grad_queries_ref[rows, cols] = dot(grad_score, stack).astype(bf16)
                grad_keys_ref[rows, cols] = pick(dot(grad_score, queries_ref[rows, cols], TN))
                grad_values_ref[rows, cols] = pick(
                    dot(weights, grad_context_ref[rows, cols], TN)
                )
        return carry

    lax.fori_loop(0, targets_ref.shape[0] // target_len, attend, 0)
    buckets = buckets_ref[...]
    both = jnp.concatenate([buckets, buckets], axis=1)

    def count(bucket, carry):
        chosen = both == bucket
        for p in range(pairs):
            table_ref[pl.ds(p * bucket_count + bucket, 1), :] = jnp.sum(
                jnp.where(chosen, score_total_ref[p], 0.0), axis=0, keepdims=True
            )
        return carry

    lax.fori_loop(0, bucket_count, count, 0)
    lanes = lax.broadcasted_iota(jnp.int32, (8, lane_tile), 1) >> 7
    head = (lanes == lax.broadcasted_iota(jnp.int32, (8, lane_tile), 0)).astype(f32)
    table = lax.dot_general(
        head, table_ref[...], NT, precision=lax.Precision.HIGHEST, preferred_element_type=f32
    )

    normed_one = normed_one_ref[...]
    total = None
    for index, grad_ref in enumerate((grad_queries_ref, grad_keys_ref, grad_values_ref)):
        cols = slice(index * width, (index + 1) * width)
        grads = grad_ref[...]
        stage_ref[:, cols] = dot(normed_one, grads, TN)
        part = dot(grads, weight_ref[:, cols], NT)
        total = part if total is None else total + part
    grad_in, grad_gain_self = norm_pullback(
        targets_ref[...].astype(f32), gain_self_ref[...], total
    )
    target_grad_ref[...] = (grad_total_ref[...] + grad_in).astype(bf16)
    gains_ref[...] = jnp.concatenate(
        [grad_gain_self, grad_gain_cross_ref[...], grad_gain_feed_ref[...]]
        + [jnp.zeros((5, width), f32)],
        axis=0,
    )
    tail = jnp.concatenate([table, jnp.zeros((8, lane_tile - table.shape[1]), f32)], axis=1)
    tail = jnp.concatenate([tail, jnp.zeros_like(tail)], axis=0)

    def extra(owner):
        shift = lax.rem(width - owner * group_rows, width)
        own = pltpu.roll(gains_ref[...], shift, 1)[:, :lane_tile]
        return jnp.concatenate([own, tail], axis=0)

    put_slots(owners, keep_ref, send_ref, stage_ref, extra)


def self_backward(target_len, bucket_count, owners, operands):
    targets = operands[6]
    bias = operands[8]
    rows, width = targets.shape
    half = (owners.shape[0] // 2, 10 * group_rows, lane_tile)
    whole = pl.BlockSpec(memory_space=pltpu.VMEM)

    def body(*refs):
        self_backward_kernel(target_len, bucket_count, *refs)

    return pl.pallas_call(
        body,
        out_shape=[
            jax.ShapeDtypeStruct((rows, width), bf16),
            jax.ShapeDtypeStruct(half, bf16),
            jax.ShapeDtypeStruct(half, bf16),
        ],
        in_specs=[pl.BlockSpec(memory_space=pltpu.SMEM)] + [whole] * len(operands),
        scratch_shapes=[pltpu.VMEM((rows, width), bf16)] * 3
        + [
            pltpu.VMEM(bias.shape, f32),
            pltpu.VMEM((width, 3 * width), f32),
            pltpu.VMEM((bias.shape[0] * bucket_count, lane_tile), f32),
            pltpu.VMEM((8, width), f32),
        ],
        compiler_params=params(),
        cost_estimate=cost(32 * targets.size * width, 20 * targets.size),
        name="self_backward",
    )(owners, *operands)


def pack(shard):
    rows, columns = shard.shape
    tiles = columns // lane_tile
    return (
        shard.reshape(rows, tiles, lane_tile)
        .transpose(1, 0, 2)
        .reshape(rows * tiles, lane_tile)
    )


def unpack(packed, rows, columns):
    tiles = columns // lane_tile
    return packed.reshape(tiles, rows, lane_tile).transpose(1, 0, 2).reshape(rows, columns)


def regroup(packed, from_groups, to_groups, shapes):
    if from_groups == to_groups:
        return packed
    parts = []
    offset = 0
    for rows, columns in shapes:
        tiles = columns // lane_tile
        size = rows // from_groups * tiles
        part = packed[:, offset : offset + size, :]
        offset += size
        part = part.reshape(from_groups, tiles, rows // from_groups, lane_tile)
        part = part.transpose(0, 2, 1, 3).reshape(to_groups, rows // to_groups, tiles, lane_tile)
        parts.append(
            part.transpose(0, 2, 1, 3).reshape(to_groups, rows // to_groups * tiles, lane_tile)
        )
    return jnp.concatenate(parts, axis=1)


def gather(shards, shapes, groups, devices):
    packed = jnp.concatenate([pack(shard) for shard in shards], axis=0)
    whole = lax.all_gather(packed, axes, axis=0, tiled=False)
    return regroup(whole, devices, groups, shapes)


def scatter(packed, shapes, groups, devices):
    packed = regroup(packed, groups, devices, shapes)
    share = lax.psum_scatter(packed, axes, scatter_dimension=0, tiled=False)
    return split_share(share, shapes, devices)


core_step = 2
plane_steps = (1, 4, 5)
line_steps = (8, 16, 24)


def exchange(values, step):
    return lax.ppermute(values, axes, [(i, i ^ step) for i in range(32)])


def slot_tables(here):
    device = jnp.arange(32, dtype=jnp.int32)
    gap = device ^ here
    slots = ((gap >> 1) & 1) * 16 + ((gap & 1) + ((gap >> 2) & 1) * 2) * 4 + (gap >> 3)
    far = device & 15
    owners = here ^ ((device >> 4) * 2 + (far >> 2 & 1) + (far >> 3) * 4 + (far & 3) * 8)
    return slots.astype(jnp.int32), owners.astype(jnp.int32)


def line_gather(shard):
    return [shard] + [exchange(shard, step) for step in line_steps]


def plane_gather(line):
    line = jnp.stack(line)
    return [line] + [exchange(line, step) for step in plane_steps]


def core_gather(blocks):
    return list(blocks) + [exchange(block, core_step) for block in blocks]


def tree_sum(parts):
    first, second, third, fourth = (part.astype(f32) for part in parts)
    return (first + second) + (third + fourth)


def pair_sums(keep, received):
    return [
        (keep[4 * j : 4 * j + 4].astype(f32) + received[4 * j : 4 * j + 4].astype(f32)).astype(
            bf16
        )
        for j in range(4)
    ]


def plane_exchange(parts):
    return [parts[0]] + [exchange(part, step) for part, step in zip(parts[1:], plane_steps)]


def line_sum(parts):
    moved = [exchange(parts[k + 1], step) for k, step in enumerate(line_steps)]
    return tree_sum([parts[0]] + moved)


def split_share(share, shapes, devices):
    parts = []
    offset = 0
    for rows, columns in shapes:
        size = rows // devices * (columns // lane_tile)
        parts.append(unpack(share[offset : offset + size], rows // devices, columns).astype(f32))
        offset += size
    return parts


def on_device(
    devices,
    direct,
    targets,
    memory,
    mem_lengths,
    buckets,
    cotangent,
    gain_self,
    gain_cross,
    gain_feed,
    self_query,
    self_key,
    self_value,
    self_output,
    cross_query,
    cross_key,
    cross_value,
    cross_output,
    gate_weight,
    up_weight,
    down_weight,
    bias_table,
):
    batch, target_len, width = targets.shape
    bucket_count, head_count = bias_table.shape
    row_count = batch * target_len
    groups = width // group_rows
    square = (width, width)
    feed_width = gate_weight.shape[1]
    feed_shapes = [(width, feed_width), (width, feed_width), (feed_width, width)]

    own_gains = jnp.stack([gain_self, gain_cross, gain_feed])
    output_shards = [self_output, cross_query]
    self_shards = [self_query, self_key, self_value]
    if direct:
        slots, owners = slot_tables(lax.axis_index(axes))
        extra = jnp.pad(own_gains.reshape(1, -1), ((0, 15), (0, lane_tile - own_gains.size)))
        self_line = line_gather(
            jnp.concatenate([pack(shard) for shard in output_shards + self_shards], axis=0)
        )
        memory_line = line_gather(
            jnp.concatenate([pack(cross_key), pack(cross_value), extra], axis=0)
        )
        gate_weight, memory_line = lax.optimization_barrier((gate_weight, memory_line))
        memory_blocks = plane_gather(memory_line)
        memory_blocks, self_line = lax.optimization_barrier((memory_blocks, self_line))
        memory_blocks = core_gather(memory_blocks)
        output_line = [part[: 6 * group_rows] for part in self_line]
        self_blocks = plane_gather([part[6 * group_rows :] for part in self_line])
        hot = (slots[:, None] == jnp.arange(groups)[None, :]).astype(bf16)
        small = [part[:, -16, : own_gains.size] for part in memory_blocks]
        gains = (
            dot(hot, jnp.concatenate(small)).reshape(groups, 3, group_rows).transpose(1, 0, 2)
        ).reshape(3, width)
    else:
        slots, owners = slot_tables(0)

        def halves(shards):
            packed = gather(shards, [square] * len(shards), groups, devices)
            packed = jnp.take(packed, owners, axis=0)
            return [packed[4 * b : 4 * b + 4] for b in range(8)]

        memory_blocks = halves([cross_key, cross_value])
        self_blocks = halves(self_shards)
        output_blocks = halves(output_shards)
        gains = lax.all_gather(own_gains, axes, axis=1, tiled=True).astype(f32)
    packed_feed = gather(
        [gate_weight, up_weight, down_weight, cross_output],
        feed_shapes + [square],
        groups,
        devices,
    )

    pad = pair_width - target_len
    bucket_hot = (
        buckets[:, :, None] == lax.broadcasted_iota(jnp.int32, (1, 1, bucket_count), 2)
    ).reshape(target_len * target_len, bucket_count)
    bias = (
        dot(bucket_hot.astype(bf16), bias_table)
        .reshape(target_len, target_len, head_count)
        .transpose(2, 0, 1)
    )
    causal = lax.broadcasted_iota(jnp.int32, (target_len, target_len), 1) <= lax.broadcasted_iota(
        jnp.int32, (target_len, target_len), 0
    )
    bias = jnp.where(causal, bias, masked_out)
    bias = jnp.pad(bias, ((0, 0), (0, 0), (0, pad)), constant_values=masked_out)
    bias = (
        bias.reshape(head_count // 2, 2, target_len, pair_width)
        .transpose(0, 2, 1, 3)
        .reshape(head_count // 2, target_len, 2 * pair_width)
    )
    wide_buckets = jnp.pad(buckets, ((0, 0), (0, pad)), constant_values=-1)
    target_rows = targets.reshape(row_count, width)
    cot_rows = cotangent.reshape(row_count, width)

    mem_keys, mem_values, memory_weight = project_memory(
        mem_lengths, owners, memory, memory_blocks
    )
    if direct:
        received, output_line, memory_weight = lax.optimization_barrier(
            (self_blocks[1:], output_line, memory_weight)
        )
        self_blocks = core_gather(self_blocks[:1] + received)
        output_blocks = plane_gather(output_line)
    normed_one, queries, key_rows, value_rows, self_context, self_weight = self_attend(
        target_len, owners, target_rows, bias, gains[0:1], self_blocks
    )
    if direct:
        received, self_context = lax.optimization_barrier((output_blocks[1:], self_context))
        output_blocks = core_gather(output_blocks[:1] + received)
    after_self, normed_two, side, output_weight = self_project(
        owners, target_rows, self_context, gains[1:2], output_blocks
    )
    cross_context, weights = cross_forward(mem_lengths, side, mem_keys, mem_values, head_count)
    outputs, grad_after_cross, grad_context, grad_gain_feed, feed_grads = feed_both(
        after_self, cross_context, cot_rows, gains[2:3], packed_feed
    )
    share_gate, share_up, share_down, share_cross_output = scatter(
        feed_grads, feed_shapes + [square], groups, devices
    )
    grad_side, grad_mem_keys, grad_mem_values = cross_backward(
        mem_lengths, grad_context, cross_context, side, mem_keys, mem_values, weights
    )
    grad_total, grad_self_context, grad_gain_cross, output_keep, output_send = (
        self_output_backward(
            owners,
            grad_side,
            after_self,
            grad_after_cross,
            normed_two,
            self_context,
            output_weight,
            gains[1:2],
        )
    )
    target_grad, self_keep, self_send = self_backward(
        target_len,
        bucket_count,
        owners,
        (
            grad_self_context,
            grad_total,
            normed_one,
            queries,
            key_rows,
            value_rows,
            target_rows,
            self_weight,
            bias,
            wide_buckets,
            gains[0:1],
            grad_gain_cross,
            grad_gain_feed,
        ),
    )
    if direct:
        output_parts = pair_sums(output_keep, exchange(output_send, core_step))
        grad_mem_keys, self_keep, output_parts = lax.optimization_barrier(
            (grad_mem_keys, self_keep, output_parts)
        )
    memory_keep, memory_send = memory_weight_grads(
        mem_lengths, owners, memory, grad_mem_keys, grad_mem_values
    )
    if direct:
        output_parts = plane_exchange(output_parts)
        self_parts = pair_sums(self_keep, exchange(self_send, core_step))
        memory_weight, memory_keep, self_parts, output_parts = lax.optimization_barrier(
            (memory_weight, memory_keep, self_parts, output_parts)
        )
    memory_grad = memory_gradient(mem_lengths, grad_mem_keys, grad_mem_values, memory_weight)
    if direct:
        self_parts = plane_exchange(self_parts)
        memory_received = exchange(memory_send, core_step)
        memory_grad, memory_received = lax.optimization_barrier((memory_grad, memory_received))
        memory_grad, self_parts = lax.optimization_barrier((memory_grad, self_parts))
        memory_parts = plane_exchange(pair_sums(memory_keep, memory_received))
        joint = line_sum(
            jnp.concatenate(
                [tree_sum(output_parts).astype(bf16), tree_sum(self_parts).astype(bf16)], axis=1
            )
        )
        output_share = joint[: 6 * group_rows]
        self_share = joint[6 * group_rows :]
        memory_share = line_sum(tree_sum(memory_parts).astype(bf16))
        share_output, share_cross_query = split_share(output_share, [square] * 2, devices)
        share_query, share_key, share_value = split_share(self_share, [square] * 3, devices)
        share_cross_key, share_cross_value = split_share(memory_share, [square] * 2, devices)
        own_grads = self_share[9 * group_rows : 9 * group_rows + 3, : width // devices]
        table = self_share[9 * group_rows + 8 : 9 * group_rows + 10]
    else:

        def reduced(keep, send, count):
            packed = jnp.take(jnp.concatenate([keep, send]), slots, axis=0)
            return scatter(
                packed[:, : 3 * count * group_rows], [square] * count, groups, devices
            )

        share_output, share_cross_query = reduced(output_keep, output_send, 2)
        share_query, share_key, share_value = reduced(self_keep, self_send, 3)
        share_cross_key, share_cross_value = reduced(memory_keep, memory_send, 2)
        small = jnp.take(jnp.concatenate([self_keep, self_send]), slots, axis=0)
        small = small[:, 9 * group_rows :].astype(f32)
        grad_gains = small[:, :3, :group_rows].transpose(1, 0, 2).reshape(-1)
        small = jnp.concatenate([grad_gains, small[0, 8:10].reshape(-1)])
        small = jnp.sum(lax.all_gather(small, axes, axis=0, tiled=False), axis=0)
        own_grads = lax.dynamic_index_in_dim(
            small[: 3 * width].reshape(3, devices, -1), lax.axis_index(axes), 1, False
        )
        table = small[3 * width :].reshape(2, lane_tile)
    table_grad = (
        table[:, : bucket_count * head_count // 2]
        .reshape(2, head_count // 2, bucket_count)
        .transpose(2, 1, 0)
        .reshape(bucket_count, head_count)
    )

    return (
        outputs.reshape(targets.shape),
        target_grad.reshape(targets.shape),
        memory_grad,
        own_grads[0],
        own_grads[1],
        own_grads[2],
        share_query,
        share_key,
        share_value,
        share_output,
        share_cross_query,
        share_cross_key,
        share_cross_value,
        share_cross_output,
        share_gate,
        share_up,
        share_down,
        table_grad,
    )


def solution(mesh):
    devices = mesh.shape["dp"] * mesh.shape["seq"]
    direct = mesh.shape["dp"] == 16 and mesh.shape["seq"] == 2
    rows = P(axes, None, None)
    flat = P(axes)
    weight = P(axes, None)

    def body(*arguments):
        return on_device(devices, direct, *arguments)

    return jax.shard_map(
        body,
        mesh=mesh,
        in_specs=(rows, rows, flat, P(), rows, flat, flat, flat) + (weight,) * 11 + (P(),),
        out_specs=(rows, rows, rows, flat, flat, flat) + (weight,) * 11 + (P(),),
        check_vma=False,
    )
```

```python
import math

import jax
import jax.numpy as jnp
from jax import lax
from jax.experimental import pallas as pl
from jax.experimental.pallas import tpu as pltpu
from jax.sharding import PartitionSpec as P

epsilon = 1e-06
masked_out = -1e30
bf16 = jnp.bfloat16
f32 = jnp.float32
axes = ("dp", "seq")
lane_tile = 256
group_rows = 24
pair_width = 128
pair_group = 3
NN = (((1,), (0,)), ((), ()))
NT = (((1,), (1,)), ((), ()))
TN = (((0,), (0,)), ((), ()))
gelu_scale = math.sqrt(2.0 / math.pi)
gelu_cubic = 0.044715


def dot(left_side, right_side, dims=NN):
    return lax.dot_general(left_side, right_side, dims, preferred_element_type=f32)


def params(mebibytes=40):
    return pltpu.CompilerParams(vmem_limit_bytes=mebibytes * 1024 * 1024)


def cost(flops, size, exps=0):
    return pl.CostEstimate(
        flops=int(flops), bytes_accessed=int(size), transcendentals=int(exps)
    )


def column_tile(packed_ref, index):
    tile = packed_ref[:, index * group_rows : (index + 1) * group_rows, :]
    return tile.reshape(tile.shape[0] * group_rows, lane_tile)


def lane_halves(rows):
    lanes = lax.broadcasted_iota(jnp.int32, (rows, pair_width), 1)
    return lanes < pair_width // 2


def project(rows, packed_ref, base, tiles):
    return [dot(rows, column_tile(packed_ref, base + t)) for t in range(tiles)]


def through(rows, packed_ref, base, tiles):
    total = None
    for t in range(tiles):
        part = dot(
            rows[:, t * lane_tile : (t + 1) * lane_tile], column_tile(packed_ref, base + t), NT
        )
        total = part if total is None else total + part
    return total


def assemble(owners, block_refs, weight_ref):
    slots = block_refs[0].shape[0]
    for first in range(0, len(block_refs), 2):
        even_ref, odd_ref = block_refs[first : first + 2]

        def place(slot, carry):
            owner = owners[first * slots + slot]
            swap = (owner & 1) == 1
            rows = pl.ds(pl.multiple_of((owner >> 1) * (2 * group_rows), 16), 2 * group_rows)
            for t in range(weight_ref.shape[1] // lane_tile):
                part = slice(t * group_rows, (t + 1) * group_rows)
                cols = slice(t * lane_tile, (t + 1) * lane_tile)
                one = even_ref[slot, part, :]
                two = odd_ref[slot, part, :]
                weight_ref[rows, cols] = jnp.concatenate(
                    [jnp.where(swap, two, one), jnp.where(swap, one, two)], axis=0
                )
            return carry

        lax.fori_loop(0, slots, place, 0)


def put_slots(owners, keep_ref, send_ref, stage_ref, extra=None):
    half = keep_ref.shape[0]
    tiles = stage_ref.shape[1] // lane_tile

    def place(slot, carry):
        for offset, out_ref in ((0, keep_ref), (half, send_ref)):
            owner = owners[slot + offset]
            rows = pl.ds(pl.multiple_of(owner * group_rows, 8), group_rows)
            parts = [
                stage_ref[rows, t * lane_tile : (t + 1) * lane_tile] for t in range(tiles)
            ]
            if extra is not None:
                parts.append(extra(owner))
            for t in range(0, len(parts), 2):
                both = jnp.concatenate(parts[t : t + 2], axis=0).astype(bf16)
                start = t * group_rows
                out_ref[slot, start : start + both.shape[0], :] = both
        return carry

    lax.fori_loop(0, half, place, 0)


def norm_scale(values):
    return lax.rsqrt(jnp.mean(values * values, axis=-1, keepdims=True) + epsilon)


def norm_pullback(values, gain_row, grad_in):
    inverse = norm_scale(values)
    weighted = grad_in * gain_row
    inner = jnp.mean(weighted * values, axis=-1, keepdims=True)
    grad_values = inverse * weighted - values * (inverse * inverse * inverse * inner)
    grad_gain = jnp.sum(grad_in * values * inverse, axis=0, keepdims=True)
    return grad_values, grad_gain


def memory_kernel(lengths, owners, memory_ref, *refs):
    block_refs = refs[:-3]
    keys_ref, values_ref, weight_ref = refs[-3:]
    seq = pl.program_id(0)
    memory_len = memory_ref.shape[1]

    @pl.when(seq == 0)
    def _():
        assemble(owners, block_refs, weight_ref)

    def fill(count):
        rows = memory_ref[0, :count, :]
        for base, out_ref in ((0, keys_ref), (3, values_ref)):
            for t in range(3):
                out_ref[0, :count, t * lane_tile : (t + 1) * lane_tile] = dot(
                    rows, weight_ref[:, (base + t) * lane_tile : (base + t + 1) * lane_tile]
                ).astype(bf16)

    @pl.when(lengths[seq] > memory_len // 2)
    def _():
        fill(memory_len)

    @pl.when(lengths[seq] <= memory_len // 2)
    def _():
        fill(memory_len // 2)


def project_memory(mem_lengths, owners, memory, blocks):
    batch, memory_len, width = memory.shape
    block = pl.BlockSpec((1, memory_len, width), lambda b, n, s: (b, 0, 0))
    return pl.pallas_call(
        memory_kernel,
        out_shape=[jax.ShapeDtypeStruct(memory.shape, bf16)] * 2
        + [jax.ShapeDtypeStruct((width, 2 * width), bf16)],
        grid_spec=pltpu.PrefetchScalarGridSpec(
            num_scalar_prefetch=2,
            grid=(batch,),
            in_specs=[block] + [pl.BlockSpec(blocks[0].shape, lambda b, n, s: (0, 0, 0))] * len(blocks),
            out_specs=[block, block, pl.BlockSpec((width, 2 * width), lambda b, n, s: (0, 0))],
        ),
        compiler_params=params(),
        cost_estimate=cost(4 * memory.size * width, 6 * memory.size),
        name="memory_project",
    )(mem_lengths, owners, memory, *blocks)


def stacked_pair(rows, half, pad):
    zero = jnp.zeros_like(rows)
    gap = jnp.zeros((pad, pair_width), rows.dtype)
    return jnp.concatenate(
        [jnp.where(half, rows, zero), gap, jnp.where(half, zero, rows), gap], axis=0
    )


def pair_softmax(scores):
    parts = []
    for h in range(2):
        one = scores[:, h * pair_width : (h + 1) * pair_width]
        terms = jnp.exp(one - jnp.max(one, axis=-1, keepdims=True))
        parts.append(terms * (1.0 / jnp.sum(terms, axis=-1, keepdims=True)))
    return parts


def self_attend_kernel(
    target_len,
    block_refs,
    owners,
    targets_ref,
    bias_ref,
    gain_self_ref,
    normed_one_ref,
    queries_ref,
    keys_ref,
    values_ref,
    context_ref,
    weight_ref,
):
    width = targets_ref.shape[1]
    assemble(owners, block_refs, weight_ref)
    inputs = targets_ref[...].astype(f32)
    normed_one = (inputs * norm_scale(inputs) * gain_self_ref[...]).astype(bf16)
    normed_one_ref[...] = normed_one
    for index, out_ref in ((0, queries_ref), (1, keys_ref), (2, values_ref)):
        out_ref[...] = dot(
            normed_one, weight_ref[:, index * width : (index + 1) * width]
        ).astype(bf16)
    half = lane_halves(target_len)
    pad = pair_width - target_len
    pairs = bias_ref.shape[0]
    columns = [slice(p * pair_width, (p + 1) * pair_width) for p in range(pairs)]

    def attend(seq, carry):
        rows = pl.ds(pl.multiple_of(seq * target_len, 32), target_len)
        scores = [
            dot(queries_ref[rows, cols], stacked_pair(keys_ref[rows, cols], half, pad), NT)
            + bias_ref[p]
            for p, cols in enumerate(columns)
        ]
        probs = [
            jnp.concatenate(pair_softmax(score), axis=1).astype(bf16) for score in scores
        ]
        for p, cols in enumerate(columns):
            value_stack = stacked_pair(values_ref[rows, cols], half, pad)
            context_ref[rows, cols] = dot(probs[p], value_stack).astype(bf16)
        return carry

    lax.fori_loop(0, targets_ref.shape[0] // target_len, attend, 0)


def self_attend(target_len, owners, targets, bias, gain_self, blocks):
    width = targets.shape[1]
    whole = pl.BlockSpec(memory_space=pltpu.VMEM)
    low = jax.ShapeDtypeStruct(targets.shape, bf16)

    def body(*refs):
        stop = 4 + len(blocks)
        self_attend_kernel(target_len, refs[4:stop], *refs[:4], *refs[stop:])

    return pl.pallas_call(
        body,
        out_shape=[low] * 5 + [jax.ShapeDtypeStruct((width, 3 * width), bf16)],
        in_specs=[pl.BlockSpec(memory_space=pltpu.SMEM)] + [whole] * (3 + len(blocks)),
        compiler_params=params(),
        cost_estimate=cost(16 * targets.size * width, 12 * targets.size),
        name="self_attend",
    )(owners, targets, bias, gain_self, *blocks)


def self_project_kernel(
    block_refs,
    owners,
    targets_ref,
    context_ref,
    gain_cross_ref,
    after_ref,
    normed_two_ref,
    side_ref,
    weight_ref,
):
    width = targets_ref.shape[1]
    assemble(owners, block_refs, weight_ref)
    after = targets_ref[...].astype(f32) + dot(context_ref[...], weight_ref[:, :width])
    after_ref[...] = after
    normed_two = (after * norm_scale(after) * gain_cross_ref[...]).astype(bf16)
    normed_two_ref[...] = normed_two
    side_ref[...] = dot(normed_two, weight_ref[:, width:]).astype(bf16)


def self_project(owners, targets, context, gain_cross, blocks):
    width = targets.shape[1]
    whole = pl.BlockSpec(memory_space=pltpu.VMEM)
    low = jax.ShapeDtypeStruct(targets.shape, bf16)

    def body(*refs):
        stop = 4 + len(blocks)
        self_project_kernel(refs[4:stop], *refs[:4], *refs[stop:])

    return pl.pallas_call(
        body,
        out_shape=[
            jax.ShapeDtypeStruct(targets.shape, f32),
            low,
            low,
            jax.ShapeDtypeStruct((width, 2 * width), bf16),
        ],
        in_specs=[pl.BlockSpec(memory_space=pltpu.SMEM)] + [whole] * (3 + len(blocks)),
        compiler_params=params(),
        cost_estimate=cost(4 * targets.size * width, 12 * targets.size),
        name="self_project",
    )(owners, targets, context, gain_cross, *blocks)


def masked_stack(rows, half):
    zero = jnp.zeros_like(rows)
    return jnp.concatenate([jnp.where(half, rows, zero), jnp.where(half, zero, rows)], axis=0)


def cross_forward_kernel(lengths, side_ref, keys_ref, values_ref, context_ref, weights_ref):
    seq = pl.program_id(0)
    target_len, width = side_ref.shape
    memory_len = keys_ref.shape[1]
    half = lane_halves(target_len)

    pairs = width // pair_width
    columns = [slice(p * pair_width, (p + 1) * pair_width) for p in range(pairs)]

    def attend(count):
        def pair_scores(p):
            stack = masked_stack(side_ref[:, columns[p]], half)
            return dot(stack, keys_ref[0, :count, columns[p]], NT)

        coming = pair_scores(0)
        for p, cols in enumerate(columns):
            scores = coming
            if p + 1 < pairs:
                coming = pair_scores(p + 1)
            terms = jnp.exp(scores - jnp.max(scores, axis=-1, keepdims=True))
            scale = 1.0 / jnp.sum(terms, axis=-1, keepdims=True)
            weights = (terms * scale).astype(bf16)
            weights_ref[0, 2 * target_len * p : 2 * target_len * (p + 1), :count] = weights
            both = dot(weights, values_ref[0, :count, cols])
            context_ref[:, cols] = jnp.where(half, both[:target_len], both[target_len:]).astype(
                bf16
            )

    @pl.when(lengths[seq] > memory_len // 2)
    def _():
        attend(memory_len)

    @pl.when(lengths[seq] <= memory_len // 2)
    def _():
        attend(memory_len // 2)


def cross_forward(mem_lengths, side, mem_keys, mem_values, head_count):
    batch, memory_len, width = mem_keys.shape
    target_len = side.shape[0] // batch
    rows = pl.BlockSpec((target_len, width), lambda b, n: (b, 0))
    memory = pl.BlockSpec((1, memory_len, width), lambda b, n: (b, 0, 0))
    weights = pl.BlockSpec((1, head_count * target_len, memory_len), lambda b, n: (b, 0, 0))
    return pl.pallas_call(
        cross_forward_kernel,
        out_shape=[
            jax.ShapeDtypeStruct(side.shape, bf16),
            jax.ShapeDtypeStruct((batch, head_count * target_len, memory_len), bf16),
        ],
        grid_spec=pltpu.PrefetchScalarGridSpec(
            num_scalar_prefetch=1,
            grid=(batch,),
            in_specs=[rows, memory, memory],
            out_specs=[rows, weights],
        ),
        compiler_params=params(),
        cost_estimate=cost(16 * side.size * memory_len, 6 * mem_keys.size, batch * head_count * target_len * memory_len),
        name="cross_forward",
    )(mem_lengths, side, mem_keys, mem_values)


def feed_kernel(
    after_ref,
    context_ref,
    cot_ref,
    gain_ref,
    side_output_ref,
    gate_ref,
    up_ref,
    down_ref,
    outputs_ref,
    grad_after_ref,
    grad_context_ref,
    grad_gain_ref,
    packed_ref,
    after_cross_ref,
    normed_ref,
    out_total_ref,
    grad_normed_ref,
):
    step = pl.program_id(0)
    steps = pl.num_programs(0)

    @pl.when(step == 0)
    def _():
        after_cross = after_ref[...] + jnp.concatenate(
            project(context_ref[...], side_output_ref, 0, 3), axis=1
        )
        after_cross_ref[...] = after_cross
        normed_ref[...] = (after_cross * norm_scale(after_cross) * gain_ref[...]).astype(bf16)
        out_total_ref[...] = after_cross
        grad_normed_ref[...] = jnp.zeros_like(grad_normed_ref)

    normed = normed_ref[...]
    cot = cot_ref[...]
    gate_weight = column_tile(gate_ref, 0)
    up_weight = column_tile(up_ref, 0)
    share = down_ref.shape[1] // 3
    owners = down_ref.shape[0]
    down_weight = jnp.concatenate(
        [
            down_ref[:, c * share : (c + 1) * share, :].reshape(owners * share, lane_tile)
            for c in range(3)
        ],
        axis=1,
    )
    gate = dot(normed, gate_weight)
    up = dot(normed, up_weight)
    grad_hidden = dot(cot, down_weight, NT)
    square = gate * gate
    tanh = jnp.tanh(gelu_scale * (gate + gelu_cubic * (square * gate)))
    half_sum = 0.5 * (1.0 + tanh)
    active = gate * half_sum
    slope = half_sum + 0.5 * gate * (1.0 - tanh * tanh) * (
        gelu_scale * (1.0 + 3.0 * gelu_cubic * square)
    )
    hidden = (active * up).astype(bf16)
    grad_gate = (grad_hidden * up * slope).astype(bf16)
    grad_up = (grad_hidden * active).astype(bf16)
    out_total_ref[...] += dot(hidden, down_weight)
    grad_normed_ref[...] += dot(grad_gate, gate_weight, NT) + dot(grad_up, up_weight, NT)
    groups = packed_ref.shape[0]

    def put(base, value):
        packed_ref[:, pl.ds(base + step * group_rows, group_rows), :] = value.reshape(
            groups, group_rows, lane_tile
        ).astype(bf16)

    put(0, dot(normed, grad_gate, TN))
    put(steps * group_rows, dot(normed, grad_up, TN))
    down_base = 2 * steps * group_rows
    for c in range(3):
        part = dot(hidden, cot[:, c * lane_tile : (c + 1) * lane_tile], TN)
        packed_ref[
            pl.ds(step * owners, owners), down_base + c * share : down_base + (c + 1) * share, :
        ] = part.reshape(owners, share, lane_tile).astype(bf16)

    @pl.when(step == steps - 1)
    def _():
        outputs_ref[...] = out_total_ref[...].astype(bf16)
        grad_in, grad_gain = norm_pullback(
            after_cross_ref[...], gain_ref[...], grad_normed_ref[...]
        )
        grad_gain_ref[...] = grad_gain
        grad_after = cot_ref[...].astype(f32) + grad_in
        grad_after_ref[...] = grad_after
        low = grad_after.astype(bf16)
        for c in range(3):
            cols = slice(c * lane_tile, (c + 1) * lane_tile)
            start = 3 * down_base // 2 + c * group_rows
            packed_ref[:, start : start + group_rows, :] = (
                dot(context_ref[...], low[:, cols], TN)
                .reshape(groups, group_rows, lane_tile)
                .astype(bf16)
            )
        grad_context_ref[...] = through(low, side_output_ref, 0, 3).astype(bf16)


def feed_both(after_self, context, cotangent, gain, packed_feed):
    rows, width = context.shape
    groups, feed_rows, _ = packed_feed.shape
    steps = feed_rows // (3 * group_rows) - 1
    owners = groups // steps
    whole = lambda f: (0, 0)
    full = pl.BlockSpec((rows, width), whole)
    tile = (groups, group_rows, lane_tile)
    return pl.pallas_call(
        feed_kernel,
        out_shape=[
            jax.ShapeDtypeStruct((rows, width), bf16),
            jax.ShapeDtypeStruct((rows, width), f32),
            jax.ShapeDtypeStruct((rows, width), bf16),
            jax.ShapeDtypeStruct((1, width), f32),
            jax.ShapeDtypeStruct((groups, feed_rows, lane_tile), bf16),
        ],
        grid=(steps,),
        in_specs=[
            full,
            full,
            full,
            pl.BlockSpec((1, width), whole),
            pl.BlockSpec((groups, 3 * group_rows, lane_tile), lambda f: (0, steps, 0)),
            pl.BlockSpec(tile, lambda f: (0, f, 0)),
            pl.BlockSpec(tile, lambda f: (0, steps + f, 0)),
            pl.BlockSpec((owners, steps * group_rows, lane_tile), lambda f: (f, 2, 0)),
        ],
        out_specs=[
            full,
            full,
            full,
            pl.BlockSpec((1, width), whole),
            pl.BlockSpec((groups, feed_rows, lane_tile), lambda f: (0, 0, 0)),
        ],
        scratch_shapes=[
            pltpu.VMEM((rows, width), f32),
            pltpu.VMEM((rows, width), bf16),
            pltpu.VMEM((rows, width), f32),
            pltpu.VMEM((rows, width), f32),
        ],
        compiler_params=params(60),
        cost_estimate=cost(18 * rows * width * steps * lane_tile, 30 * rows * width),
        name="feed_both",
    )(after_self, context, cotangent, gain, packed_feed, packed_feed, packed_feed, packed_feed)


def cross_backward_kernel(
    lengths,
    grad_ref,
    context_ref,
    side_ref,
    keys_ref,
    values_ref,
    weights_ref,
    grad_side_ref,
    grad_keys_ref,
    grad_values_ref,
):
    seq = pl.program_id(0)
    target_len, width = side_ref.shape
    memory_len = keys_ref.shape[1]
    half = lane_halves(target_len)

    pairs = width // pair_width
    columns = [slice(p * pair_width, (p + 1) * pair_width) for p in range(pairs)]

    def attend(count):
        def pair_start(p):
            cols = columns[p]
            grad_stack = masked_stack(grad_ref[:, cols], half)
            return grad_stack, dot(grad_stack, values_ref[0, :count, cols], NT)

        coming = pair_start(0)
        for p, cols in enumerate(columns):
            grad_stack, grad_probs = coming
            weights = weights_ref[0, 2 * target_len * p : 2 * target_len * (p + 1), :count]
            if p + 1 < pairs:
                coming = pair_start(p + 1)
            query_stack = masked_stack(side_ref[:, cols], half)
            product = grad_ref[:, cols].astype(f32) * context_ref[:, cols].astype(f32)
            inner = jnp.sum(masked_stack(product, half), axis=-1, keepdims=True)
            grad_scores = (weights.astype(f32) * (grad_probs - inner)).astype(bf16)
            grad_values_ref[0, cols, :count] = dot(grad_stack, weights, TN).astype(bf16)
            both = dot(grad_scores, keys_ref[0, :count, cols])
            grad_side_ref[:, cols] = jnp.where(half, both[:target_len], both[target_len:]).astype(
                bf16
            )
            grad_keys_ref[0, cols, :count] = dot(query_stack, grad_scores, TN).astype(bf16)

    @pl.when(lengths[seq] > memory_len // 2)
    def _():
        attend(memory_len)

    @pl.when(lengths[seq] <= memory_len // 2)
    def _():
        attend(memory_len // 2)


def cross_backward(mem_lengths, grad_context, context, side, mem_keys, mem_values, weights):
    batch, memory_len, width = mem_keys.shape
    target_len = side.shape[0] // batch
    rows = pl.BlockSpec((target_len, width), lambda b, n: (b, 0))
    memory = pl.BlockSpec((1, memory_len, width), lambda b, n: (b, 0, 0))
    turned = pl.BlockSpec((1, width, memory_len), lambda b, n: (b, 0, 0))
    return pl.pallas_call(
        cross_backward_kernel,
        out_shape=[jax.ShapeDtypeStruct(side.shape, bf16)]
        + [jax.ShapeDtypeStruct((batch, width, memory_len), bf16)] * 2,
        grid_spec=pltpu.PrefetchScalarGridSpec(
            num_scalar_prefetch=1,
            grid=(batch,),
            in_specs=[
                rows,
                rows,
                rows,
                memory,
                memory,
                pl.BlockSpec((1,) + weights.shape[1:], lambda b, n: (b, 0, 0)),
            ],
            out_specs=[rows, turned, turned],
        ),
        compiler_params=params(),
        cost_estimate=cost(32 * side.size * memory_len, 10 * mem_keys.size),
        name="cross_backward",
    )(mem_lengths, grad_context, context, side, mem_keys, mem_values, weights)


def memory_weight_kernel(
    lengths,
    owners,
    memory_ref,
    grad_keys_ref,
    grad_values_ref,
    keep_ref,
    send_ref,
    key_total_ref,
    value_total_ref,
    stage_ref,
):
    seq = pl.program_id(0)
    memory_len = memory_ref.shape[1]

    @pl.when(seq == 0)
    def _():
        key_total_ref[...] = jnp.zeros_like(key_total_ref)
        value_total_ref[...] = jnp.zeros_like(value_total_ref)

    def add(count):
        rows = memory_ref[0, :count, :]
        key_total_ref[...] += dot(grad_keys_ref[0, :, :count], rows)
        value_total_ref[...] += dot(grad_values_ref[0, :, :count], rows)

    @pl.when(lengths[seq] > memory_len // 2)
    def _():
        add(memory_len)

    @pl.when(lengths[seq] <= memory_len // 2)
    def _():
        add(memory_len // 2)

    @pl.when(seq == pl.num_programs(0) - 1)
    def _():
        width = key_total_ref.shape[0]
        for base, total_ref in ((0, key_total_ref), (width, value_total_ref)):
            for start in range(0, width, lane_tile):
                stage_ref[:, base + start : base + start + lane_tile] = jnp.transpose(
                    total_ref[start : start + lane_tile, :]
                )
        put_slots(owners, keep_ref, send_ref, stage_ref)


def memory_weight_grads(mem_lengths, owners, memory, grad_keys, grad_values):
    batch, memory_len, width = memory.shape
    block = pl.BlockSpec((1, memory_len, width), lambda b, n, o: (b, 0, 0))
    turned = pl.BlockSpec((1, width, memory_len), lambda b, n, o: (b, 0, 0))
    half = (owners.shape[0] // 2, 2 * width // lane_tile * group_rows, lane_tile)
    return pl.pallas_call(
        memory_weight_kernel,
        out_shape=[jax.ShapeDtypeStruct(half, bf16)] * 2,
        grid_spec=pltpu.PrefetchScalarGridSpec(
            num_scalar_prefetch=2,
            grid=(batch,),
            in_specs=[block, turned, turned],
            out_specs=[pl.BlockSpec(half, lambda b, n, o: (0, 0, 0))] * 2,
            scratch_shapes=[pltpu.VMEM((width, width), f32)] * 2
            + [pltpu.VMEM((width, 2 * width), f32)],
        ),
        compiler_params=params(),
        cost_estimate=cost(4 * memory.size * width, 6 * memory.size),
        name="memory_weight_grads",
    )(mem_lengths, owners, memory, grad_keys, grad_values)


def memory_grad_kernel(
    lengths, grad_keys_ref, grad_values_ref, weight_ref, out_ref, key_turned_ref, value_turned_ref
):
    seq = pl.program_id(0)
    memory_len = out_ref.shape[1]

    @pl.when(seq == 0)
    def _():
        for base, turned_ref in ((0, key_turned_ref), (3, value_turned_ref)):
            for t in range(3):
                turned_ref[t * lane_tile : (t + 1) * lane_tile, :] = jnp.transpose(
                    weight_ref[:, (base + t) * lane_tile : (base + t + 1) * lane_tile]
                )

    def fill(count):
        out_ref[0, :count, :] = (
            dot(grad_keys_ref[0, :, :count], key_turned_ref[...], TN)
            + dot(grad_values_ref[0, :, :count], value_turned_ref[...], TN)
        ).astype(bf16)

    @pl.when(lengths[seq] > memory_len // 2)
    def _():
        fill(memory_len)

    @pl.when(lengths[seq] <= memory_len // 2)
    def _():
        fill(memory_len // 2)
        out_ref[0, memory_len // 2 :, :] = jnp.zeros_like(out_ref[0, memory_len // 2 :, :])


def memory_gradient(mem_lengths, grad_keys, grad_values, weight):
    batch, width, memory_len = grad_keys.shape
    turned = pl.BlockSpec((1, width, memory_len), lambda b, n: (b, 0, 0))
    return pl.pallas_call(
        memory_grad_kernel,
        out_shape=jax.ShapeDtypeStruct((batch, memory_len, width), bf16),
        grid_spec=pltpu.PrefetchScalarGridSpec(
            num_scalar_prefetch=1,
            grid=(batch,),
            in_specs=[turned, turned, pl.BlockSpec(weight.shape, lambda b, n: (0, 0))],
            out_specs=pl.BlockSpec((1, memory_len, width), lambda b, n: (b, 0, 0)),
            scratch_shapes=[pltpu.VMEM((width, width), bf16)] * 2,
        ),
        compiler_params=params(),
        cost_estimate=cost(4 * grad_keys.size * width, 6 * grad_keys.size),
        name="memory_grad",
    )(mem_lengths, grad_keys, grad_values, weight)


def self_output_kernel(
    owners,
    grad_side_ref,
    after_ref,
    grad_after_ref,
    normed_two_ref,
    context_ref,
    weight_ref,
    gain_cross_ref,
    grad_total_ref,
    grad_context_ref,
    grad_gain_ref,
    keep_ref,
    send_ref,
    stage_ref,
):
    width = after_ref.shape[1]
    grad_side = grad_side_ref[...]
    grad_normed = dot(grad_side, weight_ref[:, width:], NT)
    grad_in, grad_gain = norm_pullback(after_ref[...], gain_cross_ref[...], grad_normed)
    grad_gain_ref[...] = grad_gain
    grad_total = grad_after_ref[...] + grad_in
    grad_total_ref[...] = grad_total
    low = grad_total.astype(bf16)
    stage_ref[:, :width] = dot(context_ref[...], low, TN)
    stage_ref[:, width:] = dot(normed_two_ref[...], grad_side, TN)
    grad_context_ref[...] = dot(low, weight_ref[:, :width], NT).astype(bf16)
    put_slots(owners, keep_ref, send_ref, stage_ref)


def self_output_backward(
    owners, grad_side, after, grad_after, normed_two, context, weight, gain_cross
):
    rows, width = after.shape
    half = (owners.shape[0] // 2, 2 * width // lane_tile * group_rows, lane_tile)
    whole = pl.BlockSpec(memory_space=pltpu.VMEM)
    return pl.pallas_call(
        self_output_kernel,
        out_shape=[
            jax.ShapeDtypeStruct((rows, width), f32),
            jax.ShapeDtypeStruct((rows, width), bf16),
            jax.ShapeDtypeStruct((1, width), f32),
            jax.ShapeDtypeStruct(half, bf16),
            jax.ShapeDtypeStruct(half, bf16),
        ],
        in_specs=[pl.BlockSpec(memory_space=pltpu.SMEM)] + [whole] * 7,
        scratch_shapes=[pltpu.VMEM((width, 2 * width), f32)],
        compiler_params=params(),
        cost_estimate=cost(8 * after.size * width, 20 * after.size),
        name="self_output_backward",
    )(owners, grad_side, after, grad_after, normed_two, context, weight, gain_cross)


def self_backward_kernel(
    target_len,
    bucket_count,
    owners,
    grad_context_ref,
    grad_total_ref,
    normed_one_ref,
    queries_ref,
    keys_ref,
    values_ref,
    targets_ref,
    weight_ref,
    bias_ref,
    buckets_ref,
    gain_self_ref,
    grad_gain_cross_ref,
    grad_gain_feed_ref,
    target_grad_ref,
    keep_ref,
    send_ref,
    grad_queries_ref,
    grad_keys_ref,
    grad_values_ref,
    score_total_ref,
    stage_ref,
    table_ref,
    gains_ref,
):
    width = targets_ref.shape[1]
    half = lane_halves(target_len)
    pad = pair_width - target_len
    pairs = bias_ref.shape[0]
    columns = [slice(p * pair_width, (p + 1) * pair_width) for p in range(pairs)]
    score_total_ref[...] = jnp.zeros_like(score_total_ref)

    def pick(values):
        return jnp.where(
            half, values[:target_len], values[pair_width : pair_width + target_len]
        ).astype(bf16)

    def attend(seq, carry):
        rows = pl.ds(pl.multiple_of(seq * target_len, 32), target_len)
        for first in range(0, pairs, pair_group):
            chosen = range(first, first + pair_group)
            key_stacks = [stacked_pair(keys_ref[rows, columns[p]], half, pad) for p in chosen]
            scores = [
                dot(queries_ref[rows, columns[p]], stack, NT) + bias_ref[p]
                for p, stack in zip(chosen, key_stacks)
            ]
            grad_probs = [
                dot(
                    grad_context_ref[rows, columns[p]],
                    stacked_pair(values_ref[rows, columns[p]], half, pad),
                    NT,
                )
                for p in chosen
            ]
            probs = [pair_softmax(score) for score in scores]
            grad_scores = []
            for prob, grad_prob in zip(probs, grad_probs):
                parts = []
                for h in range(2):
                    one = grad_prob[:, h * pair_width : (h + 1) * pair_width]
                    inner = jnp.sum(one * prob[h], axis=-1, keepdims=True)
                    parts.append(prob[h] * (one - inner))
                grad_scores.append(jnp.concatenate(parts, axis=1).astype(bf16))
            for p, stack, prob, grad_score in zip(chosen, key_stacks, probs, grad_scores):
                cols = columns[p]
                weights = jnp.concatenate(prob, axis=1).astype(bf16)
                score_total_ref[p] += grad_score.astype(f32)
                grad_queries_ref[rows, cols] = dot(grad_score, stack).astype(bf16)
                grad_keys_ref[rows, cols] = pick(dot(grad_score, queries_ref[rows, cols], TN))
                grad_values_ref[rows, cols] = pick(
                    dot(weights, grad_context_ref[rows, cols], TN)
                )
        return carry

    lax.fori_loop(0, targets_ref.shape[0] // target_len, attend, 0)
    buckets = buckets_ref[...]
    both = jnp.concatenate([buckets, buckets], axis=1)

    def count(bucket, carry):
        chosen = both == bucket
        for p in range(pairs):
            table_ref[pl.ds(p * bucket_count + bucket, 1), :] = jnp.sum(
                jnp.where(chosen, score_total_ref[p], 0.0), axis=0, keepdims=True
            )
        return carry

    lax.fori_loop(0, bucket_count, count, 0)
    lanes = lax.broadcasted_iota(jnp.int32, (8, lane_tile), 1) >> 7
    head = (lanes == lax.broadcasted_iota(jnp.int32, (8, lane_tile), 0)).astype(f32)
    table = lax.dot_general(
        head, table_ref[...], NT, precision=lax.Precision.HIGHEST, preferred_element_type=f32
    )

    normed_one = normed_one_ref[...]
    total = None
    for index, grad_ref in enumerate((grad_queries_ref, grad_keys_ref, grad_values_ref)):
        cols = slice(index * width, (index + 1) * width)
        grads = grad_ref[...]
        stage_ref[:, cols] = dot(normed_one, grads, TN)
        part = dot(grads, weight_ref[:, cols], NT)
        total = part if total is None else total + part
    grad_in, grad_gain_self = norm_pullback(
        targets_ref[...].astype(f32), gain_self_ref[...], total
    )
    target_grad_ref[...] = (grad_total_ref[...] + grad_in).astype(bf16)
    gains_ref[...] = jnp.concatenate(
        [grad_gain_self, grad_gain_cross_ref[...], grad_gain_feed_ref[...]]
        + [jnp.zeros((5, width), f32)],
        axis=0,
    )
    tail = jnp.concatenate([table, jnp.zeros((8, lane_tile - table.shape[1]), f32)], axis=1)
    tail = jnp.concatenate([tail, jnp.zeros_like(tail)], axis=0)

    def extra(owner):
        shift = lax.rem(width - owner * group_rows, width)
        own = pltpu.roll(gains_ref[...], shift, 1)[:, :lane_tile]
        return jnp.concatenate([own, tail], axis=0)

    put_slots(owners, keep_ref, send_ref, stage_ref, extra)


def self_backward(target_len, bucket_count, owners, operands):
    targets = operands[6]
    bias = operands[8]
    rows, width = targets.shape
    half = (owners.shape[0] // 2, 10 * group_rows, lane_tile)
    whole = pl.BlockSpec(memory_space=pltpu.VMEM)

    def body(*refs):
        self_backward_kernel(target_len, bucket_count, *refs)

    return pl.pallas_call(
        body,
        out_shape=[
            jax.ShapeDtypeStruct((rows, width), bf16),
            jax.ShapeDtypeStruct(half, bf16),
            jax.ShapeDtypeStruct(half, bf16),
        ],
        in_specs=[pl.BlockSpec(memory_space=pltpu.SMEM)] + [whole] * len(operands),
        scratch_shapes=[pltpu.VMEM((rows, width), bf16)] * 3
        + [
            pltpu.VMEM(bias.shape, f32),
            pltpu.VMEM((width, 3 * width), f32),
            pltpu.VMEM((bias.shape[0] * bucket_count, lane_tile), f32),
            pltpu.VMEM((8, width), f32),
        ],
        compiler_params=params(),
        cost_estimate=cost(32 * targets.size * width, 20 * targets.size),
        name="self_backward",
    )(owners, *operands)


def pack(shard):
    rows, columns = shard.shape
    tiles = columns // lane_tile
    return (
        shard.reshape(rows, tiles, lane_tile)
        .transpose(1, 0, 2)
        .reshape(rows * tiles, lane_tile)
    )


def unpack(packed, rows, columns):
    tiles = columns // lane_tile
    return packed.reshape(tiles, rows, lane_tile).transpose(1, 0, 2).reshape(rows, columns)


def regroup(packed, from_groups, to_groups, shapes):
    if from_groups == to_groups:
        return packed
    parts = []
    offset = 0
    for rows, columns in shapes:
        tiles = columns // lane_tile
        size = rows // from_groups * tiles
        part = packed[:, offset : offset + size, :]
        offset += size
        part = part.reshape(from_groups, tiles, rows // from_groups, lane_tile)
        part = part.transpose(0, 2, 1, 3).reshape(to_groups, rows // to_groups, tiles, lane_tile)
        parts.append(
            part.transpose(0, 2, 1, 3).reshape(to_groups, rows // to_groups * tiles, lane_tile)
        )
    return jnp.concatenate(parts, axis=1)


def gather(shards, shapes, groups, devices):
    packed = jnp.concatenate([pack(shard) for shard in shards], axis=0)
    whole = lax.all_gather(packed, axes, axis=0, tiled=False)
    return regroup(whole, devices, groups, shapes)


def scatter(packed, shapes, groups, devices):
    packed = regroup(packed, groups, devices, shapes)
    share = lax.psum_scatter(packed, axes, scatter_dimension=0, tiled=False)
    return split_share(share, shapes, devices)


core_step = 2
plane_steps = (1, 4, 5)
line_steps = (8, 16, 24)


def exchange(values, step):
    return lax.ppermute(values, axes, [(i, i ^ step) for i in range(32)])


def slot_tables(here):
    device = jnp.arange(32, dtype=jnp.int32)
    gap = device ^ here
    slots = ((gap >> 1) & 1) * 16 + ((gap & 1) + ((gap >> 2) & 1) * 2) * 4 + (gap >> 3)
    far = device & 15
    owners = here ^ ((device >> 4) * 2 + (far >> 2 & 1) + (far >> 3) * 4 + (far & 3) * 8)
    return slots.astype(jnp.int32), owners.astype(jnp.int32)


def line_gather(shard):
    return [shard] + [exchange(shard, step) for step in line_steps]


def plane_gather(line):
    line = jnp.stack(line)
    return [line] + [exchange(line, step) for step in plane_steps]


def core_gather(blocks):
    return list(blocks) + [exchange(block, core_step) for block in blocks]


def tree_sum(parts):
    first, second, third, fourth = (part.astype(f32) for part in parts)
    return (first + second) + (third + fourth)


def pair_sums(keep, received):
    return [
        (keep[4 * j : 4 * j + 4].astype(f32) + received[4 * j : 4 * j + 4].astype(f32)).astype(
            bf16
        )
        for j in range(4)
    ]


def plane_exchange(parts):
    return [parts[0]] + [exchange(part, step) for part, step in zip(parts[1:], plane_steps)]


def line_sum(parts):
    moved = [exchange(parts[k + 1], step) for k, step in enumerate(line_steps)]
    return tree_sum([parts[0]] + moved)


def split_share(share, shapes, devices):
    parts = []
    offset = 0
    for rows, columns in shapes:
        size = rows // devices * (columns // lane_tile)
        parts.append(unpack(share[offset : offset + size], rows // devices, columns).astype(f32))
        offset += size
    return parts


def on_device(
    devices,
    direct,
    targets,
    memory,
    mem_lengths,
    buckets,
    cotangent,
    gain_self,
    gain_cross,
    gain_feed,
    self_query,
    self_key,
    self_value,
    self_output,
    cross_query,
    cross_key,
    cross_value,
    cross_output,
    gate_weight,
    up_weight,
    down_weight,
    bias_table,
):
    batch, target_len, width = targets.shape
    bucket_count, head_count = bias_table.shape
    row_count = batch * target_len
    groups = width // group_rows
    square = (width, width)
    feed_width = gate_weight.shape[1]
    feed_shapes = [(width, feed_width), (width, feed_width), (feed_width, width)]

    own_gains = jnp.stack([gain_self, gain_cross, gain_feed])
    output_shards = [self_output, cross_query]
    self_shards = [self_query, self_key, self_value]
    if direct:
        slots, owners = slot_tables(lax.axis_index(axes))
        extra = jnp.pad(own_gains.reshape(1, -1), ((0, 15), (0, lane_tile - own_gains.size)))
        self_line = line_gather(
            jnp.concatenate([pack(shard) for shard in output_shards + self_shards], axis=0)
        )
        memory_line = line_gather(
            jnp.concatenate([pack(cross_key), pack(cross_value), extra], axis=0)
        )
        gate_weight, memory_line = lax.optimization_barrier((gate_weight, memory_line))
        memory_blocks = plane_gather(memory_line)
        memory_blocks, self_line = lax.optimization_barrier((memory_blocks, self_line))
        memory_blocks = core_gather(memory_blocks)
        output_line = [part[: 6 * group_rows] for part in self_line]
        self_blocks = plane_gather([part[6 * group_rows :] for part in self_line])
        hot = (slots[:, None] == jnp.arange(groups)[None, :]).astype(bf16)
        small = [part[:, -16, : own_gains.size] for part in memory_blocks]
        gains = (
            dot(hot, jnp.concatenate(small)).reshape(groups, 3, group_rows).transpose(1, 0, 2)
        ).reshape(3, width)
    else:
        slots, owners = slot_tables(0)

        def halves(shards):
            packed = gather(shards, [square] * len(shards), groups, devices)
            packed = jnp.take(packed, owners, axis=0)
            return [packed[4 * b : 4 * b + 4] for b in range(8)]

        memory_blocks = halves([cross_key, cross_value])
        self_blocks = halves(self_shards)
        output_blocks = halves(output_shards)
        gains = lax.all_gather(own_gains, axes, axis=1, tiled=True).astype(f32)
    packed_feed = gather(
        [gate_weight, up_weight, down_weight, cross_output],
        feed_shapes + [square],
        groups,
        devices,
    )

    pad = pair_width - target_len
    bucket_hot = (
        buckets[:, :, None] == lax.broadcasted_iota(jnp.int32, (1, 1, bucket_count), 2)
    ).reshape(target_len * target_len, bucket_count)
    bias = (
        dot(bucket_hot.astype(bf16), bias_table)
        .reshape(target_len, target_len, head_count)
        .transpose(2, 0, 1)
    )
    causal = lax.broadcasted_iota(jnp.int32, (target_len, target_len), 1) <= lax.broadcasted_iota(
        jnp.int32, (target_len, target_len), 0
    )
    bias = jnp.where(causal, bias, masked_out)
    bias = jnp.pad(bias, ((0, 0), (0, 0), (0, pad)), constant_values=masked_out)
    bias = (
        bias.reshape(head_count // 2, 2, target_len, pair_width)
        .transpose(0, 2, 1, 3)
        .reshape(head_count // 2, target_len, 2 * pair_width)
    )
    wide_buckets = jnp.pad(buckets, ((0, 0), (0, pad)), constant_values=-1)
    target_rows = targets.reshape(row_count, width)
    cot_rows = cotangent.reshape(row_count, width)

    mem_keys, mem_values, memory_weight = project_memory(
        mem_lengths, owners, memory, memory_blocks
    )
    if direct:
        received, output_line, memory_weight = lax.optimization_barrier(
            (self_blocks[1:], output_line, memory_weight)
        )
        self_blocks = core_gather(self_blocks[:1] + received)
        output_blocks = plane_gather(output_line)
    normed_one, queries, key_rows, value_rows, self_context, self_weight = self_attend(
        target_len, owners, target_rows, bias, gains[0:1], self_blocks
    )
    if direct:
        received, self_context = lax.optimization_barrier((output_blocks[1:], self_context))
        output_blocks = core_gather(output_blocks[:1] + received)
    after_self, normed_two, side, output_weight = self_project(
        owners, target_rows, self_context, gains[1:2], output_blocks
    )
    cross_context, weights = cross_forward(mem_lengths, side, mem_keys, mem_values, head_count)
    outputs, grad_after_cross, grad_context, grad_gain_feed, feed_grads = feed_both(
        after_self, cross_context, cot_rows, gains[2:3], packed_feed
    )
    share_gate, share_up, share_down, share_cross_output = scatter(
        feed_grads, feed_shapes + [square], groups, devices
    )
    grad_side, grad_mem_keys, grad_mem_values = cross_backward(
        mem_lengths, grad_context, cross_context, side, mem_keys, mem_values, weights
    )
    grad_total, grad_self_context, grad_gain_cross, output_keep, output_send = (
        self_output_backward(
            owners,
            grad_side,
            after_self,
            grad_after_cross,
            normed_two,
            self_context,
            output_weight,
            gains[1:2],
        )
    )
    target_grad, self_keep, self_send = self_backward(
        target_len,
        bucket_count,
        owners,
        (
            grad_self_context,
            grad_total,
            normed_one,
            queries,
            key_rows,
            value_rows,
            target_rows,
            self_weight,
            bias,
            wide_buckets,
            gains[0:1],
            grad_gain_cross,
            grad_gain_feed,
        ),
    )
    if direct:
        output_parts = pair_sums(output_keep, exchange(output_send, core_step))
        grad_mem_keys, self_keep, output_parts = lax.optimization_barrier(
            (grad_mem_keys, self_keep, output_parts)
        )
    memory_keep, memory_send = memory_weight_grads(
        mem_lengths, owners, memory, grad_mem_keys, grad_mem_values
    )
    if direct:
        output_parts = plane_exchange(output_parts)
        self_parts = pair_sums(self_keep, exchange(self_send, core_step))
        memory_weight, memory_keep, self_parts, output_parts = lax.optimization_barrier(
            (memory_weight, memory_keep, self_parts, output_parts)
        )
    memory_grad = memory_gradient(mem_lengths, grad_mem_keys, grad_mem_values, memory_weight)
    if direct:
        self_parts = plane_exchange(self_parts)
        memory_received = exchange(memory_send, core_step)
        memory_grad, memory_received = lax.optimization_barrier((memory_grad, memory_received))
        memory_grad, self_parts = lax.optimization_barrier((memory_grad, self_parts))
        memory_parts = plane_exchange(pair_sums(memory_keep, memory_received))
        joint = line_sum(
            jnp.concatenate(
                [tree_sum(output_parts).astype(bf16), tree_sum(self_parts).astype(bf16)], axis=1
            )
        )
        output_share = joint[: 6 * group_rows]
        self_share = joint[6 * group_rows :]
        memory_share = line_sum(tree_sum(memory_parts).astype(bf16))
        share_output, share_cross_query = split_share(output_share, [square] * 2, devices)
        share_query, share_key, share_value = split_share(self_share, [square] * 3, devices)
        share_cross_key, share_cross_value = split_share(memory_share, [square] * 2, devices)
        own_grads = self_share[9 * group_rows : 9 * group_rows + 3, : width // devices]
        table = self_share[9 * group_rows + 8 : 9 * group_rows + 10]
    else:

        def reduced(keep, send, count):
            packed = jnp.take(jnp.concatenate([keep, send]), slots, axis=0)
            return scatter(
                packed[:, : 3 * count * group_rows], [square] * count, groups, devices
            )

        share_output, share_cross_query = reduced(output_keep, output_send, 2)
        share_query, share_key, share_value = reduced(self_keep, self_send, 3)
        share_cross_key, share_cross_value = reduced(memory_keep, memory_send, 2)
        small = jnp.take(jnp.concatenate([self_keep, self_send]), slots, axis=0)
        small = small[:, 9 * group_rows :].astype(f32)
        grad_gains = small[:, :3, :group_rows].transpose(1, 0, 2).reshape(-1)
        small = jnp.concatenate([grad_gains, small[0, 8:10].reshape(-1)])
        small = jnp.sum(lax.all_gather(small, axes, axis=0, tiled=False), axis=0)
        own_grads = lax.dynamic_index_in_dim(
            small[: 3 * width].reshape(3, devices, -1), lax.axis_index(axes), 1, False
        )
        table = small[3 * width :].reshape(2, lane_tile)
    table_grad = (
        table[:, : bucket_count * head_count // 2]
        .reshape(2, head_count // 2, bucket_count)
        .transpose(2, 1, 0)
        .reshape(bucket_count, head_count)
    )

    return (
        outputs.reshape(targets.shape),
        target_grad.reshape(targets.shape),
        memory_grad,
        own_grads[0],
        own_grads[1],
        own_grads[2],
        share_query,
        share_key,
        share_value,
        share_output,
        share_cross_query,
        share_cross_key,
        share_cross_value,
        share_cross_output,
        share_gate,
        share_up,
        share_down,
        table_grad,
    )


def solution(mesh):
    devices = mesh.shape["dp"] * mesh.shape["seq"]
    direct = mesh.shape["dp"] == 16 and mesh.shape["seq"] == 2
    rows = P(axes, None, None)
    flat = P(axes)
    weight = P(axes, None)

    def body(*arguments):
        return on_device(devices, direct, *arguments)

    return jax.shard_map(
        body,
        mesh=mesh,
        in_specs=(rows, rows, flat, P(), rows, flat, flat, flat) + (weight,) * 11 + (P(),),
        out_specs=(rows, rows, rows, flat, flat, flat) + (weight,) * 11 + (P(),),
        check_vma=False,
    )
```
